128 devices in a mesh: row: 16 (over y_hi, x, core), col: 8 (over y_lo, z).
Axes of the slice: x: 4, y: 4 (y_hi: 2, y_lo: 2; y = y_hi * 2 + y_lo), z: 4, core: 2. Of those that a mesh axis runs over, the one named last changes fastest.
Arguments:
- ket: float32 [16, 8, 2, 81], P('row', 'col'), may hold values from -6 to 6
- corner_tl: bfloat16 [16, 8, 128, 128], P('row', 'col'), may hold values from -6 to 6
- corner_tr: bfloat16 [16, 8, 128, 128], P('row', 'col'), may hold values from -6 to 6
- corner_bl: bfloat16 [16, 8, 128, 128], P('row', 'col'), may hold values from -6 to 6
- edge_left: bfloat16 [16, 8, 128, 9, 128], P('row', 'col'), may hold values from -6 to 6
- edge_top: bfloat16 [16, 8, 128, 9, 128], P('row', 'col'), may hold values from -6 to 6
- edge_right: bfloat16 [16, 8, 128, 9, 128], P('row', 'col'), may hold values from -6 to 6
- edge_bottom: bfloat16 [16, 8, 128, 9, 128], P('row', 'col'), may hold values from -6 to 6
- row_sketch: bfloat16 [16, 8, 2, 1152, 128], P('row', 'col'), may hold values from -0.1875 to 0.1875
- col_sketch: bfloat16 [16, 8, 2, 1152, 128], P('row', 'col'), may hold values from -0.1875 to 0.1875
Outputs:
- edge_left_new: bfloat16 [16, 8, 128, 9, 128], P('row', 'col')
- corner_bl_new: bfloat16 [16, 8, 128, 128], P('row', 'col')
- edge_top_new: bfloat16 [16, 8, 128, 9, 128], P('row', 'col')
- corner_tl_new: bfloat16 [16, 8, 128, 128], P('row', 'col')
- corner_tr_new: bfloat16 [16, 8, 128, 128], P('row', 'col')
The draws below stay inside these ranges and needn't reach their ends.
All inputs are finite; a program needn't handle non-finite values.
Results may differ from the reference program's by a relative error of at most 0.03.
Values may be sent and summed in bfloat16 or wider, within the bound.
A program may use at most 64 MiB of HBM per device.

```python
import jax
import jax.numpy as jnp
from jax import lax

D = 3
PHYS = 2
CHI = 128
NS_STEPS = 8
D2 = 9
WIN_ROWS = 16
WIN_COLS = 8


def shard_levels(key, extent, pieces, smallest, largest):
    def one(axis_at, shards_of):
        draws = jax.random.uniform(jax.random.fold_in(jax.random.fold_in(key, 6), axis_at), (shards_of,), jnp.float32, smallest / len(pieces), largest / len(pieces))
        return jnp.repeat(jnp.exp(draws), extent[axis_at] // shards_of).reshape((-1,) + (1,) * (len(extent) - axis_at - 1))

    level = one(*pieces[0])
    for cut in pieces[1:]:
        level = level * one(*cut)
    return level


def bell_draw(own_key, dims, scale, most, shards=(), kind=jnp.bfloat16):
    entries = scale * jax.random.normal(own_key, dims, jnp.float32)
    if shards:
        entries = entries * shard_levels(own_key, dims, shards, -0.22, 0.18)
    return jnp.clip(entries, -most, most).astype(kind)


def setup_inputs(seed: int = 0) -> dict:
    key_list = jax.random.split(jax.random.key(seed), 11)
    ket = bell_draw(key_list[0], (WIN_ROWS, WIN_COLS, PHYS, D * D * D * D), 1.0, 6.0, ((0, 16), (1, 8)), jnp.float32)
    corner_tl = bell_draw(key_list[1], (WIN_ROWS, WIN_COLS, CHI, CHI), 1.0, 6.0, ((0, 16), (1, 8)))
    corner_tr = bell_draw(key_list[2], (WIN_ROWS, WIN_COLS, CHI, CHI), 1.0, 6.0, ((0, 16), (1, 8)))
    corner_bl = bell_draw(key_list[3], (WIN_ROWS, WIN_COLS, CHI, CHI), 1.0, 6.0, ((0, 16), (1, 8)))
    edge_left = bell_draw(key_list[4], (WIN_ROWS, WIN_COLS, CHI, D2, CHI), 1.0, 6.0, ((0, 16), (1, 8)))
    edge_top = bell_draw(key_list[5], (WIN_ROWS, WIN_COLS, CHI, D2, CHI), 1.0, 6.0, ((0, 16), (1, 8)))
    edge_right = bell_draw(key_list[6], (WIN_ROWS, WIN_COLS, CHI, D2, CHI), 1.0, 6.0, ((0, 16), (1, 8)))
    edge_bottom = bell_draw(key_list[7], (WIN_ROWS, WIN_COLS, CHI, D2, CHI), 1.0, 6.0, ((0, 16), (1, 8)))
    row_sketch = bell_draw(key_list[8], (WIN_ROWS, WIN_COLS, 2, CHI * D2, CHI), (CHI * D2) ** -0.5, 0.1875, ((0, 16), (1, 8)))
    col_sketch = bell_draw(key_list[9], (WIN_ROWS, WIN_COLS, 2, CHI * D2, CHI), (CHI * D2) ** -0.5, 0.1875, ((0, 16), (1, 8)))
    return dict(ket=ket, corner_tl=corner_tl, corner_tr=corner_tr, corner_bl=corner_bl, edge_left=edge_left, edge_top=edge_top, edge_right=edge_right, edge_bottom=edge_bottom, row_sketch=row_sketch, col_sketch=col_sketch)


def contract(pattern, former, latter):
    return jnp.einsum(pattern, former.astype(jnp.float32), latter.astype(jnp.float32))

def double_layer(ket_site):
    phys_size = ket_site.shape[0]
    tensor = ket_site.reshape(phys_size, D, D, D, D)
    doubled = jnp.einsum('sulda,svmeb->uvlmdeab', tensor, tensor, precision=lax.Precision.HIGHEST)
    return doubled.reshape(D * D, D * D, D * D, D * D).astype(jnp.bfloat16)

def upper_corner(corner, top_edge, left_edge, double_site):
    top_pair = contract('ab,auc->buc', corner, top_edge).astype(jnp.bfloat16)
    upper_half = contract('buc,blg->culg', top_pair, left_edge).astype(jnp.bfloat16)
    enlarged = contract('culg,uldr->crgd', upper_half, double_site).astype(jnp.bfloat16)
    cut_size = enlarged.shape[0] * enlarged.shape[1]
    return (top_pair, enlarged.reshape(cut_size, cut_size))

def lower_corner(corner, bottom_edge, left_edge, double_site):
    bottom_pair = contract('ge,edz->gdz', corner, bottom_edge).astype(jnp.bfloat16)
    lower_half = contract('gdz,blg->zdbl', bottom_pair, left_edge).astype(jnp.bfloat16)
    enlarged = contract('zdbl,uldr->zrbu', lower_half, double_site).astype(jnp.bfloat16)
    cut_size = enlarged.shape[0] * enlarged.shape[1]
    return (bottom_pair, enlarged.reshape(cut_size, cut_size))

def right_corner(corner, top_edge, right_edge, double_site):
    right_pair = contract('ch,hrt->crt', corner, right_edge).astype(jnp.bfloat16)
    right_half = contract('auc,crt->taur', top_edge, right_pair).astype(jnp.bfloat16)
    enlarged = contract('taur,uldr->tdal', right_half, double_site).astype(jnp.bfloat16)
    cut_size = enlarged.shape[0] * enlarged.shape[1]
    return (right_pair, enlarged.reshape(cut_size, cut_size))

def isometry(cut_terms):
    chi_size = cut_terms.shape[1]
    gram = jnp.dot(cut_terms.T, cut_terms, precision=lax.Precision.HIGHEST)
    scaling = jnp.sum(cut_terms * cut_terms) + 1e-06
    identity = jnp.eye(chi_size, dtype=jnp.float32)
    current = gram / scaling
    inverse = identity
    for iteration in range(NS_STEPS):
        factor = 1.5 * identity - 0.5 * jnp.dot(inverse, current, precision=lax.Precision.HIGHEST)
        current = jnp.dot(current, factor, precision=lax.Precision.HIGHEST)
        inverse = jnp.dot(factor, inverse, precision=lax.Precision.HIGHEST)
    result = jnp.dot(cut_terms, inverse, precision=lax.Precision.HIGHEST) / jnp.sqrt(scaling)
    return result.astype(jnp.bfloat16)

def rescale(tensor):
    return (tensor / jnp.sqrt(jnp.mean(tensor * tensor) + 1e-06)).astype(jnp.bfloat16)

def absorb_left(left_edge, double_site, top_pair, bottom_pair, above_iso, below_iso):
    chi_size = left_edge.shape[0]
    bond_size = left_edge.shape[1]
    upper_map = above_iso.reshape(chi_size, bond_size, chi_size)
    lower_map = below_iso.reshape(chi_size, bond_size, chi_size)
    left_first = contract('buk,blg->kulg', upper_map, left_edge).astype(jnp.bfloat16)
    left_second = contract('kulg,uldr->kgdr', left_first, double_site).astype(jnp.bfloat16)
    new_edge = rescale(contract('kgdr,gdm->krm', left_second, lower_map))
    new_top = rescale(contract('buc,buk->ck', top_pair, upper_map))
    new_bottom = rescale(contract('gdz,gdm->mz', bottom_pair, lower_map))
    return (new_edge, new_top, new_bottom)

def absorb_up(top_edge, double_site, corner, left_edge, right_pair, west_map, east_map):
    chi_size = top_edge.shape[0]
    bond_size = top_edge.shape[1]
    west_iso = west_map.reshape(chi_size, bond_size, chi_size)
    east_iso = east_map.reshape(chi_size, bond_size, chi_size)
    top_first = contract('alk,auc->kluc', west_iso, top_edge).astype(jnp.bfloat16)
    top_second = contract('kluc,uldr->kcdr', top_first, double_site).astype(jnp.bfloat16)
    new_edge = rescale(contract('kcdr,crm->kdm', top_second, east_iso))
    left_pair = contract('ab,blg->alg', corner, left_edge).astype(jnp.bfloat16)
    new_left = rescale(contract('alg,alk->kg', left_pair, west_iso))
    new_right = rescale(contract('crt,crm->mt', right_pair, east_iso))
    return (new_edge, new_left, new_right)

def reference(ket, corner_tl, corner_tr, corner_bl, edge_left, edge_top, edge_right, edge_bottom, row_sketch, col_sketch):
    grid_shape = (ket.shape[0], ket.shape[1])

    def flatten_sites(values_in):
        return values_in.reshape((grid_shape[0] * grid_shape[1],) + values_in.shape[2:])

    def unflatten_sites(values_in):
        return values_in.reshape(grid_shape + values_in.shape[1:])

    def site_map(function, operands):
        flat_operands = tuple((flatten_sites(operand) for operand in operands))
        outputs = lax.map(lambda packed: function(*packed), flat_operands)
        return jax.tree.map(unflatten_sites, outputs)
    doubles = site_map(double_layer, (ket,))

    def left_parts(corner, top_edge, left_edge, bottom_corner, bottom_edge, double_site, sketch):
        top_pair, upper_matrix = upper_corner(corner, top_edge, left_edge, double_site)
        bottom_pair, lower_matrix = lower_corner(bottom_corner, bottom_edge, left_edge, double_site)
        upper_term = contract('pq,pk->qk', upper_matrix, sketch[0])
        lower_term = contract('pq,pk->qk', lower_matrix, sketch[1])
        return (top_pair, bottom_pair, upper_term, lower_term)
    top_pairs, bottom_pairs, upper_terms, lower_terms = site_map(left_parts, (corner_tl, edge_top, edge_left, corner_bl, edge_bottom, doubles, row_sketch))
    row_cut = upper_terms + jnp.roll(lower_terms, -1, axis=0)
    row_iso = site_map(isometry, (row_cut,))
    edges_mid, corners_top, corners_bottom = site_map(absorb_left, (edge_left, doubles, top_pairs, bottom_pairs, jnp.roll(row_iso, 1, axis=0), row_iso))
    edge_left_new = jnp.roll(edges_mid, 1, axis=1)
    corner_tl_mid = jnp.roll(corners_top, 1, axis=1)
    corner_bl_new = jnp.roll(corners_bottom, 1, axis=1)

    def col_parts(corner, top_edge, left_edge, other_corner, right_edge, double_site, sketch):
        unused_pair, left_matrix = upper_corner(corner, top_edge, left_edge, double_site)
        right_pair, right_matrix = right_corner(other_corner, top_edge, right_edge, double_site)
        left_term = contract('pq,qk->pk', left_matrix, sketch[0])
        right_term = contract('pq,pk->qk', right_matrix, sketch[1])
        return (right_pair, left_term, right_term)
    right_pairs, left_terms, right_terms = site_map(col_parts, (corner_tl_mid, edge_top, edge_left_new, corner_tr, edge_right, doubles, col_sketch))
    col_cut = left_terms + jnp.roll(right_terms, -1, axis=1)
    col_iso = site_map(isometry, (col_cut,))
    edges_up, corners_left, corners_right = site_map(absorb_up, (edge_top, doubles, corner_tl_mid, edge_left_new, right_pairs, jnp.roll(col_iso, 1, axis=1), col_iso))
    return (edge_left_new, corner_bl_new, jnp.roll(edges_up, 1, axis=0), jnp.roll(corners_left, 1, axis=0), jnp.roll(corners_right, 1, axis=0))
```

```python
import numpy as np
import jax
import jax.numpy as jnp
from jax import lax
from jax.experimental import pallas as pl
from jax.experimental.pallas import tpu as pltpu
from jax.sharding import PartitionSpec as P

D = 3
D2 = 9
CHI = 128
NS_STEPS = 8
EPS = 1e-6
WIDE = D2 * CHI
BF = jnp.bfloat16
F32 = jnp.float32

FORMS = ((0, 1, 3, 2), (2, 1, 3, 0), (1, 0, 2, 3), (3, 0, 2, 1))
LOWER, UPPER, RIGHT, AHEAD = range(4)


def padded_legs():
    legs = [(-1, -1)] * 96
    for major in range(D2):
        for minor in range(8):
            legs[major * 8 + minor] = (major, minor)
        legs[72 + major] = (major, 8)
    return legs


def site_masks():
    legs = padded_legs()
    entry = np.stack(np.unravel_index(np.arange(81), (D,) * 4))
    masks = np.zeros((4, 2, 2, 96, 128), np.float32)
    for form, (out, v_leg, y_leg, x_leg) in enumerate(FORMS):
        for side, (major_leg, minor_leg) in enumerate(((out, v_leg), (y_leg, x_leg))):
            for row, (major, minor) in enumerate(legs):
                if major < 0:
                    continue
                for layer in range(2):
                    part = (lambda n: n // D) if layer == 0 else (lambda n: n % D)
                    fits = (entry[major_leg] == part(major)) & (entry[minor_leg] == part(minor))
                    masks[form, layer, side, row, :81] = fits
    return masks


def dot(a, b):
    return jnp.dot(a, b, preferred_element_type=F32)


def dot_nt(a, b):
    return lax.dot_general(a, b, (((1,), (1,)), ((), ())), preferred_element_type=F32)


def dot_tn(a, b):
    return lax.dot_general(a, b, (((0,), (0,)), ((), ())), preferred_element_type=F32)


def lanes(value, index):
    return value[:, index * CHI : (index + 1) * CHI]


def site_form(ket_ref, masks_ref, form, ket_scr):
    ket_scr[...] = jnp.zeros_like(ket_scr)
    ket_scr[0:2, 0:81] = ket_ref[...]
    ket = ket_scr[...]
    high = ket.astype(BF)
    rest = ket - high.astype(F32)
    mid = rest.astype(BF)
    low = (rest - mid.astype(F32)).astype(BF)
    layers = []
    for layer in range(2):
        rows = masks_ref[form, layer, 0]
        cols = masks_ref[form, layer, 1]
        left = []
        for s in range(2):
            left.append(
                jnp.concatenate(
                    [(rows.astype(F32) * part[s : s + 1].astype(F32)).astype(BF) for part in (high, mid, low)],
                    axis=1,
                )
            )
        layers.append(dot_nt(jnp.concatenate(left, 0), jnp.concatenate([cols] * 3, 1)))
    first, second = layers
    return (first[:96] * second[:96] + first[96:] * second[96:]).astype(BF)


def chain(x8, x1, y, v8t, v1t, site, zs, ws):
    z_last = dot(x1, y)
    for q in range(D2):
        zs[pl.ds(q, CHI, stride=24), :] = lanes(z_last, q)
    z = dot(x8, y)
    outs = []
    for pair in range(CHI // 2):
        cols = []
        for h in range(2):
            p = 2 * pair + h
            cols.append(
                jnp.concatenate(
                    [lanes(z, q)[p * 8 : p * 8 + 8] for q in range(D2)] + [zs[p * 24 : (p + 1) * 24, :]], 0
                )
            )
        w = dot(site, jnp.concatenate(cols, 1).astype(BF))
        for h in range(2):
            p = 2 * pair + h
            half = lanes(w, h)
            outs.append(jnp.concatenate([half[e * 8 : e * 8 + 8] for e in range(D2)], 1))
            ws[p * 16 : (p + 1) * 16, :] = half[72:88]
    wide = jnp.concatenate(outs, 0).astype(BF)
    w_last = jnp.concatenate([ws[pl.ds(e, CHI, stride=16), :] for e in range(D2)], 1).astype(BF)
    return dot(v8t, wide) + dot(v1t, w_last)


def spread(edge_ref, scr):
    scr[:, 0:D2, :] = edge_ref[...].astype(F32)


def leg_of(scr, leg):
    return scr.reshape(CHI * 16, CHI)[pl.ds(leg, CHI, stride=16), :].astype(BF)


def leading(scr):
    return scr[:, 0:8, :].reshape(CHI * 8, CHI).astype(BF)


def flat_sketch(sketch, scr):
    scr[...] = sketch.astype(F32)
    return jnp.concatenate([scr[pl.ds(r, CHI, stride=D2), :] for r in range(D2)], 1).astype(BF)


def to_rows(wide, scr):
    for leg in range(8):
        scr[pl.ds(leg, CHI, stride=8), :] = lanes(wide, leg)
    return scr[...].astype(BF), lanes(wide, 8).astype(BF)


def split(value):
    high = value.astype(BF)
    return high, (value - high.astype(F32)).astype(BF)


def product(a, b):
    a_high, a_low = split(a)
    b_high, b_low = split(b)
    return dot(jnp.concatenate([a_high, a_low], 1), jnp.concatenate([b_high, b_high], 0)) + dot(a_high, b_low)


def scaled_inverses(grams):
    rows = lax.broadcasted_iota(jnp.int32, (CHI, CHI), 0)
    cols = lax.broadcasted_iota(jnp.int32, (CHI, CHI), 1)
    identity = jnp.where(rows == cols, 1.0, 0.0).astype(F32)
    states = []
    for gram in grams:
        scaling = jnp.sum(gram * identity) + EPS
        states.append((gram * (1.0 / scaling), None, scaling))
    for step in range(NS_STEPS):
        after = []
        for current, inverse, scaling in states:
            mixed = current if inverse is None else product(inverse, current)
            factor = 1.5 * identity - 0.5 * mixed
            if inverse is None:
                after.append((product(factor, current), factor, scaling))
            elif step + 1 < NS_STEPS:
                both = product(factor, jnp.concatenate([current, inverse], 1))
                after.append((lanes(both, 0), lanes(both, 1), scaling))
            else:
                after.append((None, product(factor, inverse), scaling))
        states = after
    return [inverse * lax.rsqrt(jnp.full((1, 1), scaling, F32)) for _, inverse, scaling in states]


def rescale(value):
    mean = jnp.sum(value * value) * (1.0 / value.size)
    return value * lax.rsqrt(jnp.full((1, 1), mean + EPS, F32))


def both_sides(raw, left, right):
    left_high = left.astype(BF)
    turned = dot(left_high, raw.astype(BF)).astype(BF)
    stacked = dot(jnp.concatenate([lanes(turned, r) for r in range(D2)], 0), right.astype(BF))
    return jnp.concatenate([stacked[r * CHI : (r + 1) * CHI] for r in range(D2)], 1)


def lower_kernel(ket_ref, masks_ref, edge_left, edge_bottom, corner_bl, sketch, term, sites, ket_scr, a_scr, b_scr, s_scr, rows_scr, zs, ws):
    zs[...] = jnp.zeros_like(zs)
    for form in range(4):
        sites[form] = site_form(ket_ref, masks_ref, form, ket_scr)
    spread(edge_left, a_scr)
    spread(edge_bottom, b_scr)
    y = flat_sketch(sketch[1], s_scr)
    corner_t = corner_bl[...].T
    for leg in range(D2):
        turned = dot_nt(corner_t, leg_of(a_scr, leg))
        if leg < 8:
            rows_scr[pl.ds(leg, CHI, stride=8), :] = turned
    v8t = rows_scr[...].astype(BF).T
    term[...] = chain(
        leading(b_scr), leg_of(b_scr, 8), y, v8t, turned.astype(BF).T, sites[LOWER, 0:88, :], zs, ws
    ).astype(BF)


def upper_kernel(sites, edge_left, edge_top, corner_tl, sketch, term, pair8, pair1, a_scr, b_scr, s_scr, rows_scr, zs, ws):
    zs[...] = jnp.zeros_like(zs)
    spread(edge_left, a_scr)
    spread(edge_top, b_scr)
    y = flat_sketch(sketch[0], s_scr)
    corner_t = corner_tl[...].T
    for leg in range(D2):
        turned = dot(corner_t, leg_of(b_scr, leg))
        if leg < 8:
            rows_scr[pl.ds(leg, CHI, stride=8), :] = turned
    x8 = rows_scr[...].astype(BF)
    x1 = turned.astype(BF)
    pair8[...] = x8
    pair1[...] = x1
    term[...] = chain(x8, x1, y, leading(a_scr).T, leg_of(a_scr, 8).T, sites[UPPER, 0:88, :], zs, ws).astype(BF)


def right_kernel(sites, edge_right, edge_top, corner_tr, sketch, term, pair, a_scr, b_scr, s_scr, rows_scr, zs, ws):
    zs[...] = jnp.zeros_like(zs)
    spread(edge_right, a_scr)
    spread(edge_top, b_scr)
    y = flat_sketch(sketch[1], s_scr)
    corner_t = corner_tr[...].T
    for leg in range(D2):
        turned = dot_nt(corner_t, leg_of(b_scr, leg))
        if leg < 8:
            rows_scr[pl.ds(leg, CHI, stride=8), :] = turned
        pair[leg * CHI : (leg + 1) * CHI, :] = dot(corner_tr[...], leg_of(a_scr, leg)).astype(BF)
    v8t = rows_scr[...].astype(BF).T
    term[...] = chain(
        leading(a_scr), leg_of(a_scr, 8), y, v8t, turned.astype(BF).T, sites[RIGHT, 0:88, :], zs, ws
    ).astype(BF)


def summed(one, other):
    return (one[...].astype(F32) + other[...].astype(F32)).astype(BF)


def absorb(cut_one, cut_other, x8, x1, side8, side1, pair, site, rows_scr, zs, ws):
    v8, v1 = to_rows(cut_one.astype(F32), rows_scr)
    v8t = v8.T
    v1t = v1.T
    first = dot(v8t, jnp.concatenate([v8, side8], 1)) + dot(v1t, jnp.concatenate([v1, side1], 1))
    stacked = jnp.concatenate([lanes(cut_other, r) for r in range(D2)], 0)
    second = dot_tn(stacked, jnp.concatenate([stacked, pair], 1))
    left, right = scaled_inverses([lanes(first, 0), lanes(second, 0)])
    raw = chain(x8, x1, cut_other, v8t, v1t, site, zs, ws)
    edge = rescale(both_sides(raw, left, right))
    near = rescale(dot(left.astype(BF), lanes(first, 1).astype(BF)))
    far = rescale(dot(right.astype(BF), lanes(second, 1).astype(BF)))
    return edge, near, far


def left_kernel(sites, edge_left, edge_bottom, corner_bl, upper_here, lower_below, upper_above, lower_here, pair8, pair1, edge, near, far, a_scr, b_scr, rows_scr, pair_scr, zs, ws):
    zs[...] = jnp.zeros_like(zs)
    spread(edge_left, a_scr)
    spread(edge_bottom, b_scr)
    for leg in range(D2):
        pair_scr[leg * CHI : (leg + 1) * CHI, :] = dot(corner_bl[...], leg_of(b_scr, leg)).astype(BF)
    edge_value, near_value, far_value = absorb(
        summed(upper_above, lower_here),
        summed(upper_here, lower_below),
        leading(a_scr),
        leg_of(a_scr, 8),
        pair8[...],
        pair1[...],
        pair_scr[...],
        sites[AHEAD, 0:88, :],
        rows_scr,
        zs,
        ws,
    )
    edge[...] = edge_value.astype(BF)
    near[...] = near_value.T.astype(BF)
    far[...] = far_value.astype(BF)


def ahead_kernel(sites, edge_new, corner_mid, edge_top, sketch, right_term, cut, side8, side1, a_scr, s_scr, rows_scr, zs, ws):
    zs[...] = jnp.zeros_like(zs)
    spread(edge_top, a_scr)
    y = flat_sketch(sketch[0], s_scr)
    x8, x1 = to_rows(dot(corner_mid[...], edge_new[...]), rows_scr)
    side8[...] = x8
    side1[...] = x1
    term = chain(x8, x1, y, leading(a_scr).T, leg_of(a_scr, 8).T, sites[AHEAD, 0:88, :], zs, ws)
    cut[...] = (term + right_term[...].astype(F32)).astype(BF)


def up_kernel(sites, edge_top, cut_west, cut_east, side8, side1, pair, edge, near, far, a_scr, rows_scr, zs, ws):
    zs[...] = jnp.zeros_like(zs)
    spread(edge_top, a_scr)
    edge_value, near_value, far_value = absorb(
        cut_west[...],
        cut_east[...],
        leading(a_scr),
        leg_of(a_scr, 8),
        side8[...],
        side1[...],
        pair[...],
        sites[UPPER, 0:88, :],
        rows_scr,
        zs,
        ws,
    )
    edge[...] = edge_value.astype(BF)
    near[...] = near_value.astype(BF)
    far[...] = far_value.astype(BF)


def natural_kernel(edge_left, edge_top, out_left, out_top, a_scr):
    for source, target in ((edge_left, out_left), (edge_top, out_top)):
        for leg in range(D2):
            a_scr.reshape(CHI * 16, CHI)[pl.ds(leg, CHI, stride=16), :] = lanes(source[...], leg).astype(F32)
        target[...] = a_scr[:, 0:D2, :].astype(BF)


NATURAL = pltpu.VMEM((CHI, 16, CHI), F32)
SKETCH = pltpu.VMEM((WIDE, CHI), F32)
ROWS = pltpu.VMEM((CHI * 8, CHI), F32)
PAIR = pltpu.VMEM((WIDE, CHI), BF)
WORK = [pltpu.VMEM((CHI * 24, CHI), F32), pltpu.VMEM((CHI * 16, CHI), F32)]
FLAT = jax.ShapeDtypeStruct((CHI, WIDE), BF)
SQUARE = jax.ShapeDtypeStruct((CHI, CHI), BF)
STACK8 = jax.ShapeDtypeStruct((CHI * 8, CHI), BF)
STACK9 = jax.ShapeDtypeStruct((WIDE, CHI), BF)
SITES = jax.ShapeDtypeStruct((4, 96, 96), BF)
EDGE = jax.ShapeDtypeStruct((CHI, D2, CHI), BF)


def call(kernel, outs, scratch, *operands):
    spec = pl.BlockSpec(memory_space=pltpu.VMEM)
    return pl.pallas_call(
        kernel,
        out_shape=outs,
        in_specs=[spec] * len(operands),
        out_specs=[spec] * len(outs),
        scratch_shapes=scratch,
        compiler_params=pltpu.CompilerParams(vmem_limit_bytes=48 << 20),
        cost_estimate=pl.CostEstimate(flops=900_000_000, bytes_accessed=2_000_000, transcendentals=0),
        name=kernel.__name__,
    )(*operands)


def shifted(value, axis, steps):
    count = lax.axis_size(axis)
    return lax.ppermute(value, axis, [(source, (source + steps) % count) for source in range(count)])


def local(*arrays):
    (ket, corner_tl, corner_tr, corner_bl, edge_left, edge_top, edge_right, edge_bottom, row_sketch, col_sketch) = [
        array.reshape(array.shape[2:]) for array in arrays
    ]
    masks = jnp.asarray(site_masks(), BF)
    ket_scr = pltpu.VMEM((8, 128), F32)
    lower, sites = call(
        lower_kernel, [FLAT, SITES], [ket_scr, NATURAL, NATURAL, SKETCH, ROWS] + WORK,
        ket, masks, edge_left, edge_bottom, corner_bl, row_sketch,
    )
    lower_below = shifted(lower, "row", -1)
    upper, pair8, pair1 = call(
        upper_kernel, [FLAT, STACK8, SQUARE], [NATURAL, NATURAL, SKETCH, ROWS] + WORK,
        sites, edge_left, edge_top, corner_tl, row_sketch,
    )
    upper_above = shifted(upper, "row", 1)
    right, right_pair = call(
        right_kernel, [FLAT, STACK9], [NATURAL, NATURAL, SKETCH, ROWS] + WORK,
        sites, edge_right, edge_top, corner_tr, col_sketch,
    )
    right_next = shifted(right, "col", -1)
    edge_mid, corner_mid, corner_bottom = call(
        left_kernel, [FLAT, SQUARE, SQUARE], [NATURAL, NATURAL, ROWS, PAIR] + WORK,
        sites, edge_left, edge_bottom, corner_bl, upper, lower_below, upper_above, lower, pair8, pair1,
    )
    edge_left_new, corner_tl_mid, corner_bl_new = [shifted(v, "col", 1) for v in (edge_mid, corner_mid, corner_bottom)]
    cut, side8, side1 = call(
        ahead_kernel, [FLAT, STACK8, SQUARE], [NATURAL, SKETCH, ROWS] + WORK,
        sites, edge_left_new, corner_tl_mid, edge_top, col_sketch, right_next,
    )
    cut_west = shifted(cut, "col", 1)
    edge_up, corner_left, corner_right = call(
        up_kernel, [FLAT, SQUARE, SQUARE], [NATURAL, ROWS] + WORK,
        sites, edge_top, cut_west, cut, side8, side1, right_pair,
    )
    edge_top_new, corner_tl_new, corner_tr_new = [shifted(v, "row", 1) for v in (edge_up, corner_left, corner_right)]
    left_out, top_out = call(natural_kernel, [EDGE, EDGE], [NATURAL], edge_left_new, edge_top_new)
    results = (left_out, corner_bl_new, top_out, corner_tl_new, corner_tr_new)
    return tuple(value[None, None] for value in results)


def solution(mesh):
    four = P("row", "col", None, None)
    five = P("row", "col", None, None, None)
    return jax.shard_map(
        local,
        mesh=mesh,
        in_specs=(four, four, four, four, five, five, five, five, five, five),
        out_specs=(five, four, five, four, four),
        check_vma=False,
    )
```

```python
import numpy as np
import jax
import jax.numpy as jnp
from jax import lax
from jax.experimental import pallas as pl
from jax.experimental.pallas import tpu as pltpu
from jax.sharding import PartitionSpec as P

D = 3
D2 = 9
CHI = 128
NS_STEPS = 8
EPS = 1e-6
WIDE = D2 * CHI
BF = jnp.bfloat16
F32 = jnp.float32

FORMS = ((0, 1, 3, 2), (2, 1, 3, 0), (1, 0, 2, 3), (3, 0, 2, 1))
LOWER, UPPER, RIGHT, AHEAD = range(4)


def padded_legs():
    legs = [(-1, -1)] * 96
    for major in range(D2):
        for minor in range(8):
            legs[major * 8 + minor] = (major, minor)
        legs[72 + major] = (major, 8)
    return legs


def site_masks():
    legs = padded_legs()
    entry = np.stack(np.unravel_index(np.arange(81), (D,) * 4))
    masks = np.zeros((4, 2, 2, 96, 128), np.float32)
    for form, (out, v_leg, y_leg, x_leg) in enumerate(FORMS):
        for side, (major_leg, minor_leg) in enumerate(((out, v_leg), (y_leg, x_leg))):
            for row, (major, minor) in enumerate(legs):
                if major < 0:
                    continue
                for layer in range(2):
                    part = (lambda n: n // D) if layer == 0 else (lambda n: n % D)
                    fits = (entry[major_leg] == part(major)) & (entry[minor_leg] == part(minor))
                    masks[form, layer, side, row, :81] = fits
    return masks


def dot(a, b):
    return jnp.dot(a, b, preferred_element_type=F32)


def dot_nt(a, b):
    return lax.dot_general(a, b, (((1,), (1,)), ((), ())), preferred_element_type=F32)


def dot_tn(a, b):
    return lax.dot_general(a, b, (((0,), (0,)), ((), ())), preferred_element_type=F32)


def lanes(value, index):
    return value[:, index * CHI : (index + 1) * CHI]


def site_form(ket_ref, masks_ref, form, ket_scr):
    ket_scr[...] = jnp.zeros_like(ket_scr)
    ket_scr[0:2, 0:81] = ket_ref[...]
    ket = ket_scr[...]
    high = ket.astype(BF)
    rest = ket - high.astype(F32)
    mid = rest.astype(BF)
    low = (rest - mid.astype(F32)).astype(BF)
    layers = []
    for layer in range(2):
        rows = masks_ref[form, layer, 0]
        cols = masks_ref[form, layer, 1]
        left = []
        for s in range(2):
            left.append(
                jnp.concatenate(
                    [(rows.astype(F32) * part[s : s + 1].astype(F32)).astype(BF) for part in (high, mid, low)],
                    axis=1,
                )
            )
        layers.append(dot_nt(jnp.concatenate(left, 0), jnp.concatenate([cols] * 3, 1)))
    first, second = layers
    return (first[:96] * second[:96] + first[96:] * second[96:]).astype(BF)


def flat_sketch(sketch, scr):
    scr[...] = sketch.astype(F32)
    return jnp.concatenate([scr[pl.ds(r, CHI, stride=D2), :] for r in range(D2)], 1).astype(BF)


def to_rows(wide, scr):
    for leg in range(8):
        scr[pl.ds(leg, CHI, stride=8), :] = lanes(wide, leg)
    return scr[...].astype(BF), lanes(wide, 8).astype(BF)


def split(value):
    high = value.astype(BF)
    return high, (value - high.astype(F32)).astype(BF)


def product(a, b):
    a_high, a_low = split(a)
    b_high, b_low = split(b)
    return dot(jnp.concatenate([a_high, a_low], 1), jnp.concatenate([b_high, b_high], 0)) + dot(a_high, b_low)


def start_inverse(gram):
    rows = lax.broadcasted_iota(jnp.int32, (CHI, CHI), 0)
    cols = lax.broadcasted_iota(jnp.int32, (CHI, CHI), 1)
    identity = jnp.where(rows == cols, 1.0, 0.0).astype(F32)
    scaling = jnp.sum(gram * identity) + EPS
    return identity, gram * (1.0 / scaling), scaling


def inverse_steps(gram):
    identity, current, scaling = start_inverse(gram)
    factor = 1.5 * identity - 0.5 * current
    inverse = factor
    current = product(factor, current)
    yield None
    for step in range(1, NS_STEPS):
        factor = 1.5 * identity - 0.5 * product(inverse, current)
        yield None
        if step + 1 < NS_STEPS:
            both = product(factor, jnp.concatenate([current, inverse], 1))
            current, inverse = lanes(both, 0), lanes(both, 1)
            yield None
        else:
            inverse = product(factor, inverse)
    yield inverse * lax.rsqrt(jnp.full((1, 1), scaling, F32))


def rescale(value):
    mean = jnp.sum(value * value) * (1.0 / value.size)
    return value * lax.rsqrt(jnp.full((1, 1), mean + EPS, F32))


GROUPS = 8
GROUP = CHI // GROUPS


def site_group(index, x8, y, site, work):
    zs, ws, zb, wb = work
    rows = index * GROUP * 8
    zb[rows : rows + GROUP * 8, :] = dot(x8[rows : rows + GROUP * 8, :], y)

    def pair(step, carry):
        at = index * (GROUP // 2) + step
        z = zb[pl.ds(pl.multiple_of(at * 16, 16), 16), :]
        tail = zs[pl.ds(pl.multiple_of(at * 48, 48), 48), :]
        cols = []
        for h in range(2):
            cols.append(
                jnp.concatenate(
                    [lanes(z, q)[h * 8 : h * 8 + 8] for q in range(D2)] + [tail[h * 24 : h * 24 + 24]], 0
                )
            )
        w = dot(site, jnp.concatenate(cols, 1).astype(BF))
        halves = [lanes(w, h) for h in range(2)]
        wide = [jnp.concatenate([half[e * 8 : e * 8 + 8] for e in range(D2)], 1) for half in halves]
        wb[pl.ds(pl.multiple_of(at * 16, 16), 16), :] = jnp.concatenate(wide, 0).astype(BF)
        ws[pl.ds(pl.multiple_of(at * 32, 32), 32), :] = jnp.concatenate([half[72:88] for half in halves], 0)
        return carry

    lax.fori_loop(0, GROUP // 2, pair, 0, unroll=True)


def site_products(x8, x1, y, site, work, beside=None):
    zs = work[0]
    z_last = dot(x1, y)
    for q in range(D2):
        zs[pl.ds(q, CHI, stride=24), :] = lanes(z_last, q)
    found = None
    for index in range(GROUPS):
        if beside is not None:
            for _ in range(2):
                found = next(beside, found)
        site_group(index, x8, y, site, work)
    return found


def last_product(v8t, v1t, work):
    ws, wb = work[1], work[3]
    w_last = jnp.concatenate([ws[pl.ds(e, CHI, stride=16), :] for e in range(D2)], 1).astype(BF)
    return dot(v8t, wb[...]) + dot(v1t, w_last)


def leading(edge, scr):
    for leg in range(8):
        scr[pl.ds(leg, CHI, stride=8), :] = edge[leg].astype(F32)
    return scr[...].astype(BF)


def joined(one, other):
    return (one[...].astype(F32) + other[...].astype(F32)).astype(BF)


def stack_legs(wide):
    return jnp.concatenate([lanes(wide, leg) for leg in range(D2)], 0)


def right_turn(raw, right):
    turned = dot(stack_legs(raw).astype(BF), right)
    return jnp.concatenate([turned[r * CHI : (r + 1) * CHI] for r in range(D2)], 1).astype(BF)


SQ = (CHI, CHI)
FL = (CHI, WIDE)
PACK = (CHI, WIDE + 2 * CHI)
V = pltpu.VMEM
COPIES = 13
SENDS = 8
SCRATCH = dict(
    ket=V((8, 128), F32),
    masks=V((4, 2, 2, 96, 128), BF),
    corner_tl=V(SQ, BF),
    corner_tr=V(SQ, BF),
    corner_bl=V(SQ, BF),
    edge_left=V((D2, CHI, CHI), BF),
    edge_top=V((D2, CHI, CHI), BF),
    edge_right=V((D2, CHI, CHI), BF),
    edge_bottom=V((D2, CHI, CHI), BF),
    row_upper=V((WIDE, CHI), BF),
    row_lower=V((WIDE, CHI), BF),
    col_left=V((WIDE, CHI), BF),
    col_right=V((WIDE, CHI), BF),
    ket_in=V((2, 81), F32),
    sites=V((4, 96, 96), BF),
    s_scr=V((WIDE, CHI), F32),
    rows=V((CHI * 8, CHI), F32),
    zs=V((CHI * 24, CHI), F32),
    ws=V((CHI * 16, CHI), F32),
    zb=V((CHI * 8, WIDE), F32),
    wb=V((CHI * 8, WIDE), BF),
    left8=V((CHI * 8, CHI), BF),
    pair8=V((CHI * 8, CHI), BF),
    pair1=V(SQ, BF),
    stacked=V((WIDE, CHI), BF),
    top8=V((CHI * 8, CHI), BF),
    lower=V(FL, BF),
    lower_below=V(FL, BF),
    upper=V(FL, BF),
    upper_above=V(FL, BF),
    root=V(SQ, BF),
    root_above=V(SQ, BF),
    moved=V(PACK, BF),
    moved_in=V(PACK, BF),
    right=V(FL, BF),
    right_next=V(FL, BF),
    cut=V(FL, BF),
    cut_west=V(FL, BF),
    root_col=V(SQ, BF),
    root_west=V(SQ, BF),
    raised=V(PACK, BF),
    raised_in=V(PACK, BF),
    in_sems=pltpu.SemaphoreType.DMA((COPIES,)),
    send_sems=pltpu.SemaphoreType.DMA((SENDS,)),
    recv_sems=pltpu.SemaphoreType.DMA((SENDS,)),
)


def move_kernel(ket, masks, corner_tl, corner_tr, corner_bl, edge_left, edge_top, edge_right, edge_bottom, row_sketch, col_sketch, left_out, top_out, *scratch):
    s = dict(zip(SCRATCH, scratch))
    work = (s["zs"], s["ws"], s["zb"], s["wb"])
    sources = (
        ("ket_in", ket),
        ("masks", masks),
        ("edge_left", edge_left),
        ("corner_bl", corner_bl),
        ("row_lower", row_sketch.at[1]),
        ("edge_bottom", edge_bottom),
        ("corner_tl", corner_tl),
        ("edge_top", edge_top),
        ("row_upper", row_sketch.at[0]),
        ("corner_tr", corner_tr),
        ("edge_right", edge_right),
        ("col_right", col_sketch.at[1]),
        ("col_left", col_sketch.at[0]),
    )
    loads = {}
    for index, (name, source) in enumerate(sources):
        loads[name] = pltpu.make_async_copy(source, s[name], s["in_sems"].at[index])
        loads[name].start()

    row, col = lax.axis_index("row"), lax.axis_index("col")
    row_count, col_count = lax.axis_size("row"), lax.axis_size("col")
    above = {"row": lax.rem(row + row_count - 1, row_count), "col": col}
    below = {"row": lax.rem(row + 1, row_count), "col": col}
    west = {"row": row, "col": lax.rem(col + col_count - 1, col_count)}
    east = {"row": row, "col": lax.rem(col + 1, col_count)}
    barrier = pltpu.get_barrier_semaphore()
    for neighbour in (above, below, west, east):
        pl.semaphore_signal(barrier, inc=1, device_id=neighbour, device_id_type=pl.DeviceIdType.MESH)

    sent = []

    def send(source, target, device):
        copy = pltpu.make_async_remote_copy(
            src_ref=s[source],
            dst_ref=s[target],
            send_sem=s["send_sems"].at[len(sent)],
            recv_sem=s["recv_sems"].at[len(sent)],
            device_id=device,
            device_id_type=pl.DeviceIdType.MESH,
        )
        copy.start()
        sent.append(copy)
        return copy

    s["zs"][...] = jnp.zeros_like(s["zs"])
    loads["ket_in"].wait()
    loads["masks"].wait()
    for form in range(4):
        s["sites"][form] = site_form(s["ket_in"], s["masks"], form, s["ket"])

    def site(form):
        return s["sites"][form, 0:88, :]

    for name in ("edge_left", "corner_bl", "row_lower", "edge_bottom"):
        loads[name].wait()
    corner_t = s["corner_bl"][...].T
    for leg in range(D2):
        turned = dot_nt(corner_t, s["edge_left"][leg])
        if leg < 8:
            s["rows"][pl.ds(leg, CHI, stride=8), :] = turned
    v8t = s["rows"][...].astype(BF).T
    v1t = turned.astype(BF).T
    site_products(
        leading(s["edge_bottom"], s["rows"]),
        s["edge_bottom"][8],
        flat_sketch(s["row_lower"][...], s["s_scr"]),
        site(LOWER),
        work,
    )
    s["lower"][...] = last_product(v8t, v1t, work).astype(BF)
    pl.semaphore_wait(barrier, 4)
    lower_copy = send("lower", "lower_below", above)

    for name in ("corner_tl", "edge_top", "row_upper"):
        loads[name].wait()
    corner_t = s["corner_tl"][...].T
    for leg in range(D2):
        turned = dot(corner_t, s["edge_top"][leg])
        if leg < 8:
            s["rows"][pl.ds(leg, CHI, stride=8), :] = turned
    s["pair8"][...] = s["rows"][...].astype(BF)
    s["pair1"][...] = turned.astype(BF)
    s["left8"][...] = leading(s["edge_left"], s["rows"])
    site_products(
        s["pair8"], s["pair1"][...], flat_sketch(s["row_upper"][...], s["s_scr"]), site(UPPER), work
    )
    s["upper"][...] = last_product(s["left8"][...].T, s["edge_left"][8].T, work).astype(BF)
    upper_copy = send("upper", "upper_above", below)
    for leg in range(D2):
        s["stacked"][leg * CHI : (leg + 1) * CHI, :] = dot(s["corner_bl"][...], s["edge_bottom"][leg]).astype(BF)

    lower_copy.wait_recv()
    cut = joined(s["upper"], s["lower_below"])
    stacked = stack_legs(cut)
    second = dot_tn(stacked, jnp.concatenate([stacked, s["stacked"][...]], 1))
    root = site_products(
        s["left8"], s["edge_left"][8], cut, site(AHEAD), work, inverse_steps(lanes(second, 0))
    )
    s["root"][...] = root.astype(BF)
    root_copy = send("root", "root_above", below)
    s["moved"][:, WIDE + CHI :] = rescale(dot(s["root"][...], lanes(second, 1).astype(BF))).astype(BF)
    upper_copy.wait_recv()
    v8, v1 = to_rows(joined(s["upper_above"], s["lower"]).astype(F32), s["rows"])
    v8t, v1t = v8.T, v1.T
    first = dot(v8t, s["pair8"][...]) + dot(v1t, s["pair1"][...])
    raw = right_turn(last_product(v8t, v1t, work), s["root"][...])
    root_copy.wait_recv()
    above_root = s["root_above"][...]
    s["moved"][:, :WIDE] = rescale(dot(above_root, raw)).astype(BF)
    s["moved"][:, WIDE : WIDE + CHI] = rescale(dot(above_root, first.astype(BF))).T.astype(BF)
    moved_copy = send("moved", "moved_in", east)

    for name in ("corner_tr", "edge_right", "col_right"):
        loads[name].wait()
    corner_t = s["corner_tr"][...].T
    for leg in range(D2):
        turned = dot_nt(corner_t, s["edge_top"][leg])
        if leg < 8:
            s["rows"][pl.ds(leg, CHI, stride=8), :] = turned
    v8t = s["rows"][...].astype(BF).T
    v1t = turned.astype(BF).T
    site_products(
        leading(s["edge_right"], s["rows"]),
        s["edge_right"][8],
        flat_sketch(s["col_right"][...], s["s_scr"]),
        site(RIGHT),
        work,
    )
    s["right"][...] = last_product(v8t, v1t, work).astype(BF)
    right_copy = send("right", "right_next", west)
    for leg in range(D2):
        s["stacked"][leg * CHI : (leg + 1) * CHI, :] = dot(s["corner_tr"][...], s["edge_right"][leg]).astype(BF)
    s["top8"][...] = leading(s["edge_top"], s["rows"])
    loads["col_left"].wait()
    y = flat_sketch(s["col_left"][...], s["s_scr"])

    moved_copy.wait_recv()
    left_out[...] = s["moved_in"][...]
    side = dot(s["moved_in"][:, WIDE : WIDE + CHI], s["moved_in"][:, :WIDE])
    side8, side1 = to_rows(side, s["rows"])
    s["pair8"][...] = side8
    s["pair1"][...] = side1
    site_products(s["pair8"], side1, y, site(AHEAD), work)
    term = last_product(s["top8"][...].T, s["edge_top"][8].T, work)
    right_copy.wait_recv()
    s["cut"][...] = (term + s["right_next"][...].astype(F32)).astype(BF)
    cut_copy = send("cut", "cut_west", east)

    cut = s["cut"][...]
    stacked = stack_legs(cut)
    second = dot_tn(stacked, jnp.concatenate([stacked, s["stacked"][...]], 1))
    root = site_products(s["top8"], s["edge_top"][8], cut, site(UPPER), work, inverse_steps(lanes(second, 0)))
    s["root_col"][...] = root.astype(BF)
    col_copy = send("root_col", "root_west", east)
    s["raised"][:, WIDE + CHI :] = rescale(dot(s["root_col"][...], lanes(second, 1).astype(BF))).astype(BF)
    cut_copy.wait_recv()
    v8, v1 = to_rows(s["cut_west"][...].astype(F32), s["rows"])
    v8t, v1t = v8.T, v1.T
    first = dot(v8t, s["pair8"][...]) + dot(v1t, s["pair1"][...])
    raw = right_turn(last_product(v8t, v1t, work), s["root_col"][...])
    col_copy.wait_recv()
    west_root = s["root_west"][...]
    s["raised"][:, :WIDE] = rescale(dot(west_root, raw)).astype(BF)
    s["raised"][:, WIDE : WIDE + CHI] = rescale(dot(west_root, first.astype(BF))).astype(BF)
    raised_copy = send("raised", "raised_in", below)
    raised_copy.wait_recv()
    top_out[...] = s["raised_in"][...]
    for copy in sent:
        copy.wait_send()


def result_kernel(left, top, edge_left, corner_bl, edge_top, corner_tl, corner_tr):
    for leg in range(D2):
        edge_left[leg] = left[:, leg * CHI : (leg + 1) * CHI]
        edge_top[leg] = top[:, leg * CHI : (leg + 1) * CHI]
    corner_bl[...] = left[:, WIDE + CHI :]
    corner_tl[...] = top[:, WIDE : WIDE + CHI]
    corner_tr[...] = top[:, WIDE + CHI :]


def local(*arrays):
    ket, corner_tl, corner_tr, corner_bl, *edges, row_sketch, col_sketch = [a.reshape(a.shape[2:]) for a in arrays]
    edges = [edge.transpose(1, 0, 2) for edge in edges]
    vmem = pl.BlockSpec(memory_space=pltpu.VMEM)
    operands = (ket, jnp.asarray(site_masks(), BF), corner_tl, corner_tr, corner_bl, *edges, row_sketch, col_sketch)
    packs = pl.pallas_call(
        move_kernel,
        out_shape=[jax.ShapeDtypeStruct(PACK, BF)] * 2,
        in_specs=[pl.BlockSpec(memory_space=pl.ANY)] * len(operands),
        out_specs=[vmem] * 2,
        scratch_shapes=list(SCRATCH.values()),
        compiler_params=pltpu.CompilerParams(
            vmem_limit_bytes=56 << 20, collective_id=0, has_side_effects=True
        ),
        name="moves",
    )(*operands)
    edge = jax.ShapeDtypeStruct((D2, CHI, CHI), BF)
    square = jax.ShapeDtypeStruct((CHI, CHI), BF)
    left, corner_bl, top, corner_tl, corner_tr = pl.pallas_call(
        result_kernel,
        out_shape=[edge, square, edge, square, square],
        in_specs=[vmem] * 2,
        out_specs=[vmem] * 5,
        name="results",
    )(*packs)
    results = (left.transpose(1, 0, 2), corner_bl, top.transpose(1, 0, 2), corner_tl, corner_tr)
    return tuple(value[None, None] for value in results)


def solution(mesh):
    four = P("row", "col", None, None)
    five = P("row", "col", None, None, None)
    return jax.shard_map(
        local,
        mesh=mesh,
        in_specs=(four, four, four, four, five, five, five, five, five, five),
        out_specs=(five, four, five, four, four),
        check_vma=False,
    )
```

```python
import numpy as np
import jax
import jax.numpy as jnp
from jax import lax
from jax.experimental import pallas as pl
from jax.experimental.pallas import tpu as pltpu
from jax.sharding import PartitionSpec as P

D = 3
D2 = 9
CHI = 128
NS_STEPS = 8
EPS = 1e-6
WIDE = D2 * CHI
BF = jnp.bfloat16
F32 = jnp.float32

FORMS = ((0, 1, 3, 2), (2, 1, 3, 0), (1, 0, 2, 3), (3, 0, 2, 1))
LOWER, UPPER, RIGHT, AHEAD = range(4)


def padded_legs():
    legs = [(-1, -1)] * 96
    for major in range(D2):
        for minor in range(8):
            legs[major * 8 + minor] = (major, minor)
        legs[72 + major] = (major, 8)
    return legs


def site_masks():
    legs = padded_legs()
    entry = np.stack(np.unravel_index(np.arange(81), (D,) * 4))
    masks = np.zeros((4, 2, 2, 96, 128), np.float32)
    for form, (out, v_leg, y_leg, x_leg) in enumerate(FORMS):
        for side, (major_leg, minor_leg) in enumerate(((out, v_leg), (y_leg, x_leg))):
            for row, (major, minor) in enumerate(legs):
                if major < 0:
                    continue
                for layer in range(2):
                    part = (lambda n: n // D) if layer == 0 else (lambda n: n % D)
                    fits = (entry[major_leg] == part(major)) & (entry[minor_leg] == part(minor))
                    masks[form, layer, side, row, :81] = fits
    return masks


def dot(a, b):
    return jnp.dot(a, b, preferred_element_type=F32)


def dot_nt(a, b):
    return lax.dot_general(a, b, (((1,), (1,)), ((), ())), preferred_element_type=F32)


def dot_tn(a, b):
    return lax.dot_general(a, b, (((0,), (0,)), ((), ())), preferred_element_type=F32)


def lanes(value, index):
    return value[:, index * CHI : (index + 1) * CHI]


def site_form(ket_ref, masks_ref, form, ket_scr):
    ket_scr[...] = jnp.zeros_like(ket_scr)
    ket_scr[0:2, 0:81] = ket_ref[...]
    ket = ket_scr[...]
    high = ket.astype(BF)
    rest = ket - high.astype(F32)
    mid = rest.astype(BF)
    low = (rest - mid.astype(F32)).astype(BF)
    layers = []
    for layer in range(2):
        rows = masks_ref[form, layer, 0]
        cols = masks_ref[form, layer, 1]
        left = []
        for s in range(2):
            left.append(
                jnp.concatenate(
                    [(rows.astype(F32) * part[s : s + 1].astype(F32)).astype(BF) for part in (high, mid, low)],
                    axis=1,
                )
            )
        layers.append(dot_nt(jnp.concatenate(left, 0), jnp.concatenate([cols] * 3, 1)))
    first, second = layers
    return (first[:96] * second[:96] + first[96:] * second[96:]).astype(BF)


def flat_sketch(sketch, scr):
    scr[...] = sketch.astype(F32)
    return jnp.concatenate([scr[pl.ds(r, CHI, stride=D2), :] for r in range(D2)], 1).astype(BF)


def to_rows(wide, scr):
    for leg in range(8):
        scr[pl.ds(leg, CHI, stride=8), :] = lanes(wide, leg)
    return scr[...].astype(BF), lanes(wide, 8).astype(BF)


def split(value):
    high = value.astype(BF)
    return high, (value - high.astype(F32)).astype(BF)


def product(a, b):
    a_high, a_low = split(a)
    b_high, b_low = split(b)
    return dot(jnp.concatenate([a_high, a_low], 1), jnp.concatenate([b_high, b_high], 0)) + dot(a_high, b_low)


def start_inverse(gram):
    rows = lax.broadcasted_iota(jnp.int32, (CHI, CHI), 0)
    cols = lax.broadcasted_iota(jnp.int32, (CHI, CHI), 1)
    identity = jnp.where(rows == cols, 1.0, 0.0).astype(F32)
    scaling = jnp.sum(gram * identity) + EPS
    return identity, gram * (1.0 / scaling), scaling


def inverse_steps(gram):
    identity, current, scaling = start_inverse(gram)
    factor = 1.5 * identity - 0.5 * current
    inverse = factor
    current = product(factor, current)
    yield None
    for step in range(1, NS_STEPS):
        factor = 1.5 * identity - 0.5 * product(inverse, current)
        yield None
        if step + 1 < NS_STEPS:
            both = product(factor, jnp.concatenate([current, inverse], 1))
            current, inverse = lanes(both, 0), lanes(both, 1)
            yield None
        else:
            inverse = product(factor, inverse)
    yield inverse * lax.rsqrt(jnp.full((1, 1), scaling, F32))


def rescale(value):
    mean = jnp.sum(value * value) * (1.0 / value.size)
    return value * lax.rsqrt(jnp.full((1, 1), mean + EPS, F32))


GROUPS = 8
GROUP = CHI // GROUPS


def site_group(index, x8, y, site, work):
    zs, ws, zb, wb = work
    rows = index * GROUP * 8
    zb[rows : rows + GROUP * 8, :] = dot(x8[rows : rows + GROUP * 8, :], y)

    def pair(step, carry):
        at = index * (GROUP // 2) + step
        z = zb[pl.ds(pl.multiple_of(at * 16, 16), 16), :]
        tail = zs[pl.ds(pl.multiple_of(at * 48, 48), 48), :]
        cols = []
        for h in range(2):
            cols.append(
                jnp.concatenate(
                    [lanes(z, q)[h * 8 : h * 8 + 8] for q in range(D2)] + [tail[h * 24 : h * 24 + 24]], 0
                )
            )
        w = dot(site, jnp.concatenate(cols, 1).astype(BF))
        halves = [lanes(w, h) for h in range(2)]
        wide = [jnp.concatenate([half[e * 8 : e * 8 + 8] for e in range(D2)], 1) for half in halves]
        wb[pl.ds(pl.multiple_of(at * 16, 16), 16), :] = jnp.concatenate(wide, 0).astype(BF)
        ws[pl.ds(pl.multiple_of(at * 32, 32), 32), :] = jnp.concatenate([half[72:88] for half in halves], 0)
        return carry

    lax.fori_loop(0, GROUP // 2, pair, 0, unroll=True)


def site_products(x8, x1, y, site, work, beside=None):
    zs = work[0]
    z_last = dot(x1, y)
    for q in range(D2):
        zs[pl.ds(q, CHI, stride=24), :] = lanes(z_last, q)
    found = None
    for index in range(GROUPS):
        if beside is not None:
            for _ in range(2):
                found = next(beside, found)
        site_group(index, x8, y, site, work)
    return found


def last_product(v8t, v1t, work):
    ws, wb = work[1], work[3]
    w_last = jnp.concatenate([ws[pl.ds(e, CHI, stride=16), :] for e in range(D2)], 1).astype(BF)
    return dot(v8t, wb[...]) + dot(v1t, w_last)


def leading(edge, scr):
    for leg in range(8):
        scr[pl.ds(leg, CHI, stride=8), :] = edge[leg].astype(F32)
    return scr[...].astype(BF)


def joined(one, other):
    return (one[...].astype(F32) + other[...].astype(F32)).astype(BF)


def stack_legs(wide):
    return jnp.concatenate([lanes(wide, leg) for leg in range(D2)], 0)


def right_turn(raw, right):
    turned = dot(stack_legs(raw), right)
    return jnp.concatenate([turned[r * CHI : (r + 1) * CHI] for r in range(D2)], 1).astype(BF)


SQ = (CHI, CHI)
FL = (CHI, WIDE)
PACK = (CHI, WIDE + 2 * CHI)
V = pltpu.VMEM
COPIES = 12
SENDS = 12
SCRATCH = dict(
    ket=V((8, 128), F32),
    ket_in=V((2, 81), F32),
    masks=V((4, 2, 2, 96, 128), BF),
    corners=V((2, CHI, CHI), BF),
    corner_tr=V(SQ, BF),
    edge_left=V((D2, CHI, CHI), BF),
    edges=V((2, D2, CHI, CHI), BF),
    edge_right=V((D2, CHI, CHI), BF),
    row_sketch=V((2, WIDE, CHI), BF),
    col_sketch=V((2, WIDE, CHI), BF),
    sites=V((4, 96, 96), BF),
    s_scr=V((WIDE, CHI), F32),
    rows=V((CHI * 8, CHI), F32),
    last=V(SQ, F32),
    zs=V((CHI * 24, CHI), F32),
    ws=V((CHI * 16, CHI), F32),
    zb=V((CHI * 8, WIDE), F32),
    wb=V((CHI * 8, WIDE), BF),
    pair8=V((CHI * 8, CHI), BF),
    pair1=V(SQ, BF),
    stacked=V((WIDE, CHI), BF),
    top8=V((CHI * 8, CHI), BF),
    terms=V((2, CHI, WIDE), BF),
    terms_in=V((2, CHI, WIDE), BF),
    root=V(SQ, BF),
    root_near=V(SQ, BF),
    root_far=V(SQ, BF),
    moved=V(FL, BF),
    moved_in=V(FL, BF),
    moved_ends=V((CHI, 2 * CHI), BF),
    moved_ends_in=V((CHI, 2 * CHI), BF),
    right=V(FL, BF),
    right_next=V(FL, BF),
    cut=V(FL, BF),
    cut_west=V(FL, BF),
    root_col=V(SQ, BF),
    root_col_near=V(SQ, BF),
    root_col_far=V(SQ, BF),
    raised=V(FL, BF),
    raised_in=V(FL, BF),
    raised_ends=V((CHI, 2 * CHI), BF),
    raised_ends_in=V((CHI, 2 * CHI), BF),
    in_sems=pltpu.SemaphoreType.DMA((COPIES,)),
    send_sems=pltpu.SemaphoreType.DMA((SENDS,)),
    recv_sems=pltpu.SemaphoreType.DMA((SENDS,)),
)


def move_kernel(ket, masks, corner_tl, corner_tr, corner_bl, edge_left, edge_top, edge_right, edge_bottom, row_sketch, col_sketch, left_out, top_out, *scratch):
    s = dict(zip(SCRATCH, scratch))
    work = (s["zs"], s["ws"], s["zb"], s["wb"])
    sources = (
        (ket, s["ket_in"]),
        (masks, s["masks"]),
        (edge_left, s["edge_left"]),
        (corner_bl, s["corners"].at[LOWER]),
        (corner_tl, s["corners"].at[UPPER]),
        (row_sketch, s["row_sketch"]),
        (edge_bottom, s["edges"].at[LOWER]),
        (edge_top, s["edges"].at[UPPER]),
        (corner_tr, s["corner_tr"]),
        (edge_right, s["edge_right"]),
        (col_sketch.at[1], s["col_sketch"].at[1]),
        (col_sketch.at[0], s["col_sketch"].at[0]),
    )
    loads = [pltpu.make_async_copy(a, b, s["in_sems"].at[n]) for n, (a, b) in enumerate(sources)]
    for load in loads:
        load.start()

    row, col = lax.axis_index("row"), lax.axis_index("col")
    row_count, col_count = lax.axis_size("row"), lax.axis_size("col")

    def device(down, across):
        return {
            "row": lax.rem(row + (row_count + down), row_count),
            "col": lax.rem(col + (col_count + across), col_count),
        }

    barrier = pltpu.get_barrier_semaphore()
    for offset in ((-1, 0), (1, 0), (0, -1), (0, 1), (1, 1), (-1, -1)):
        pl.semaphore_signal(barrier, inc=1, device_id=device(*offset), device_id_type=pl.DeviceIdType.MESH)

    def remote(number, source, target, down, across):
        return pltpu.make_async_remote_copy(
            src_ref=source,
            dst_ref=target,
            send_sem=s["send_sems"].at[number],
            recv_sem=s["recv_sems"].at[number],
            device_id=device(down, across),
            device_id_type=pl.DeviceIdType.MESH,
        )

    sent = []

    def send(source, target, down, across):
        copy = remote(len(sent) + 2, s[source], s[target], down, across)
        copy.start()
        sent.append(copy)
        return copy

    def site(form):
        return s["sites"][form, 0:88, :]

    s["zs"][...] = jnp.zeros_like(s["zs"])
    for load in loads[:2]:
        load.wait()
    for form in (LOWER, UPPER):
        s["sites"][form] = site_form(s["ket_in"], s["masks"], form, s["ket"])
    for load in loads[2:8]:
        load.wait()

    half = row_count // 2
    far = (lax.rem(row, half) + 1) // half

    def term(step, carry):
        which = lax.rem(step + far, 2)

        @pl.when(which == LOWER)
        def _():
            corner_t = s["corners"][LOWER].T
            for leg in range(D2):
                turned = dot_nt(corner_t, s["edge_left"][leg])
                if leg < 8:
                    s["rows"][pl.ds(leg, CHI, stride=8), :] = turned
            s["last"][...] = turned

        @pl.when(which == UPPER)
        def _():
            corner = s["corners"][UPPER]
            for leg in range(D2):
                turned = dot(corner, s["edge_left"][leg])
                if leg < 8:
                    s["rows"][pl.ds(leg, CHI, stride=8), :] = turned
            s["last"][...] = turned

        v8t = s["rows"][...].astype(BF).T
        v1t = s["last"][...].astype(BF).T
        edge = s["edges"].at[which]
        site_products(
            leading(edge, s["rows"]),
            edge[8],
            flat_sketch(s["row_sketch"][1 - which], s["s_scr"]),
            s["sites"][which][0:88],
            work,
        )
        s["terms"][which] = last_product(v8t, v1t, work).astype(BF)

        @pl.when(step == 0)
        def _():
            pl.semaphore_wait(barrier, 6)

        remote(which, s["terms"].at[which], s["terms_in"].at[which], 2 * which - 1, 0).start()
        return carry

    lax.fori_loop(0, 2, term, 0)
    lower_copy = remote(LOWER, s["terms"].at[LOWER], s["terms_in"].at[LOWER], -1, 0)
    upper_copy = remote(UPPER, s["terms"].at[UPPER], s["terms_in"].at[UPPER], 1, 0)
    for form in (AHEAD, RIGHT):
        s["sites"][form] = site_form(s["ket_in"], s["masks"], form, s["ket"])
    left8 = leading(s["edge_left"], s["rows"])
    for leg in range(D2):
        s["stacked"][leg * CHI : (leg + 1) * CHI, :] = dot(
            s["corners"][LOWER], s["edges"][LOWER, leg]
        ).astype(BF)
    corner_t = s["corners"][UPPER].T
    for leg in range(D2):
        turned = dot(corner_t, s["edges"][UPPER, leg])
        if leg < 8:
            s["rows"][pl.ds(leg, CHI, stride=8), :] = turned
    s["pair8"][...] = s["rows"][...].astype(BF)
    s["pair1"][...] = turned.astype(BF)

    lower_copy.wait_recv()
    cut = joined(s["terms"].at[UPPER], s["terms_in"].at[LOWER])
    s["cut"][...] = cut
    site_products(left8, s["edge_left"][8], cut, site(AHEAD), work)
    upper_copy.wait_recv()
    v8, v1 = to_rows(joined(s["terms_in"].at[UPPER], s["terms"].at[LOWER]).astype(F32), s["rows"])
    v8t, v1t = v8.T, v1.T
    s["moved"][...] = last_product(v8t, v1t, work).astype(BF)
    moved_copy = send("moved", "moved_in", 0, 1)
    first = dot(v8t, s["pair8"][...]) + dot(v1t, s["pair1"][...])
    stacked = stack_legs(s["cut"][...])
    second = dot_tn(stacked, jnp.concatenate([stacked, s["stacked"][...]], 1))
    s["moved_ends"][...] = jnp.concatenate([first, lanes(second, 1)], 1).astype(BF)
    moved_ends_copy = send("moved_ends", "moved_ends_in", 0, 1)

    for load in loads[8:11]:
        load.wait()
    corner_t = s["corner_tr"][...].T
    for leg in range(D2):
        turned = dot_nt(corner_t, s["edges"][UPPER, leg])
        if leg < 8:
            s["rows"][pl.ds(leg, CHI, stride=8), :] = turned
    v8t = s["rows"][...].astype(BF).T
    v1t = turned.astype(BF).T
    root = site_products(
        leading(s["edge_right"], s["rows"]),
        s["edge_right"][8],
        flat_sketch(s["col_sketch"][1], s["s_scr"]),
        site(RIGHT),
        work,
        inverse_steps(lanes(second, 0)),
    )
    s["root"][...] = root.astype(BF)
    near_copy = send("root", "root_near", 0, 1)
    far_copy = send("root", "root_far", 1, 1)
    s["right"][...] = last_product(v8t, v1t, work).astype(BF)
    right_copy = send("right", "right_next", 0, -1)
    for leg in range(D2):
        s["stacked"][leg * CHI : (leg + 1) * CHI, :] = dot(s["corner_tr"][...], s["edge_right"][leg]).astype(BF)
    s["top8"][...] = leading(s["edges"].at[UPPER], s["rows"])
    loads[11].wait()
    y = flat_sketch(s["col_sketch"][0], s["s_scr"])

    for copy in (moved_ends_copy, near_copy, far_copy):
        copy.wait_recv()
    above_root = s["root_far"][...]
    own_root = s["root_near"][...]
    corner_mid = rescale(dot(above_root, s["moved_ends_in"][:, :CHI])).T.astype(BF)
    left_out[:, WIDE : WIDE + CHI] = corner_mid
    left_out[:, WIDE + CHI :] = rescale(dot(own_root, s["moved_ends_in"][:, CHI:])).astype(BF)
    moved_copy.wait_recv()
    edge_new = rescale(dot(above_root, right_turn(s["moved_in"][...], own_root))).astype(BF)
    left_out[:, :WIDE] = edge_new
    side8, side1 = to_rows(dot(corner_mid, edge_new), s["rows"])
    s["pair8"][...] = side8
    s["pair1"][...] = side1
    site_products(s["pair8"], side1, y, site(AHEAD), work)
    left_term = last_product(s["top8"][...].T, s["edges"][UPPER, 8].T, work)
    right_copy.wait_recv()
    s["cut"][...] = (left_term + s["right_next"][...].astype(F32)).astype(BF)
    cut_copy = send("cut", "cut_west", 0, 1)

    cut = s["cut"][...]
    stacked = stack_legs(cut)
    second = dot_tn(stacked, jnp.concatenate([stacked, s["stacked"][...]], 1))
    root = site_products(
        s["top8"], s["edges"][UPPER, 8], cut, site(UPPER), work, inverse_steps(lanes(second, 0))
    )
    s["root_col"][...] = root.astype(BF)
    near_copy = send("root_col", "root_col_near", 1, 0)
    far_copy = send("root_col", "root_col_far", 1, 1)
    cut_copy.wait_recv()
    v8, v1 = to_rows(s["cut_west"][...].astype(F32), s["rows"])
    v8t, v1t = v8.T, v1.T
    s["raised"][...] = last_product(v8t, v1t, work).astype(BF)
    raised_copy = send("raised", "raised_in", 1, 0)
    first = dot(v8t, s["pair8"][...]) + dot(v1t, s["pair1"][...])
    s["raised_ends"][...] = jnp.concatenate([first, lanes(second, 1)], 1).astype(BF)
    raised_ends_copy = send("raised_ends", "raised_ends_in", 1, 0)
    near_copy.wait_recv()
    far_copy.wait_recv()
    raised_copy.wait_recv()
    west_root = s["root_col_far"][...]
    own_root = s["root_col_near"][...]
    top_out[:, :WIDE] = rescale(dot(west_root, right_turn(s["raised_in"][...], own_root))).astype(BF)
    raised_ends_copy.wait_recv()
    top_out[:, WIDE : WIDE + CHI] = rescale(dot(west_root, s["raised_ends_in"][:, :CHI])).astype(BF)
    top_out[:, WIDE + CHI :] = rescale(dot(own_root, s["raised_ends_in"][:, CHI:])).astype(BF)
    for copy in [lower_copy, upper_copy] + sent:
        copy.wait_send()


def result_kernel(left, top, edge_left, corner_bl, edge_top, corner_tl, corner_tr):
    for leg in range(D2):
        edge_left[leg] = left[:, leg * CHI : (leg + 1) * CHI]
        edge_top[leg] = top[:, leg * CHI : (leg + 1) * CHI]
    corner_bl[...] = left[:, WIDE + CHI :]
    corner_tl[...] = top[:, WIDE : WIDE + CHI]
    corner_tr[...] = top[:, WIDE + CHI :]


def local(*arrays):
    ket, corner_tl, corner_tr, corner_bl, *edges, row_sketch, col_sketch = [a.reshape(a.shape[2:]) for a in arrays]
    edges = [edge.transpose(1, 0, 2) for edge in edges]
    vmem = pl.BlockSpec(memory_space=pltpu.VMEM)
    operands = (ket, jnp.asarray(site_masks(), BF), corner_tl, corner_tr, corner_bl, *edges, row_sketch, col_sketch)
    packs = pl.pallas_call(
        move_kernel,
        out_shape=[jax.ShapeDtypeStruct(PACK, BF)] * 2,
        in_specs=[pl.BlockSpec(memory_space=pl.ANY)] * len(operands),
        out_specs=[vmem] * 2,
        scratch_shapes=list(SCRATCH.values()),
        compiler_params=pltpu.CompilerParams(
            vmem_limit_bytes=56 << 20, collective_id=0, has_side_effects=True
        ),
        name="moves",
    )(*operands)
    edge = jax.ShapeDtypeStruct((D2, CHI, CHI), BF)
    square = jax.ShapeDtypeStruct((CHI, CHI), BF)
    left, corner_bl, top, corner_tl, corner_tr = pl.pallas_call(
        result_kernel,
        out_shape=[edge, square, edge, square, square],
        in_specs=[vmem] * 2,
        out_specs=[vmem] * 5,
        name="results",
    )(*packs)
    results = (left.transpose(1, 0, 2), corner_bl, top.transpose(1, 0, 2), corner_tl, corner_tr)
    return tuple(value[None, None] for value in results)


def solution(mesh):
    four = P("row", "col", None, None)
    five = P("row", "col", None, None, None)
    return jax.shard_map(
        local,
        mesh=mesh,
        in_specs=(four, four, four, four, five, five, five, five, five, five),
        out_specs=(five, four, five, four, four),
        check_vma=False,
    )
```

```python
import numpy as np
import jax
import jax.numpy as jnp
from jax import lax
from jax.experimental import pallas as pl
from jax.experimental.pallas import tpu as pltpu
from jax.sharding import PartitionSpec as P

D = 3
D2 = 9
CHI = 128
NS_STEPS = 8
EPS = 1e-6
WIDE = D2 * CHI
BF = jnp.bfloat16
F32 = jnp.float32

FORMS = ((0, 1, 3, 2), (2, 1, 3, 0), (1, 0, 2, 3), (3, 0, 2, 1))
LOWER, UPPER, RIGHT, AHEAD = range(4)


def padded_legs():
    legs = [(-1, -1)] * 96
    for major in range(D2):
        for minor in range(8):
            legs[major * 8 + minor] = (major, minor)
        legs[72 + major] = (major, 8)
    return legs


def site_masks():
    legs = padded_legs()
    entry = np.stack(np.unravel_index(np.arange(81), (D,) * 4))
    masks = np.zeros((4, 2, 2, 96, 128), np.float32)
    for form, (out, v_leg, y_leg, x_leg) in enumerate(FORMS):
        for side, (major_leg, minor_leg) in enumerate(((out, v_leg), (y_leg, x_leg))):
            for row, (major, minor) in enumerate(legs):
                if major < 0:
                    continue
                for layer in range(2):
                    part = (lambda n: n // D) if layer == 0 else (lambda n: n % D)
                    fits = (entry[major_leg] == part(major)) & (entry[minor_leg] == part(minor))
                    masks[form, layer, side, row, :81] = fits
    return masks


def dot(a, b):
    return jnp.dot(a, b, preferred_element_type=F32)


def dot_nt(a, b):
    return lax.dot_general(a, b, (((1,), (1,)), ((), ())), preferred_element_type=F32)


def dot_tn(a, b):
    return lax.dot_general(a, b, (((0,), (0,)), ((), ())), preferred_element_type=F32)


def lanes(value, index):
    return value[:, index * CHI : (index + 1) * CHI]


def site_form(ket_ref, masks_ref, form, ket_scr):
    ket_scr[...] = jnp.zeros_like(ket_scr)
    ket_scr[0:2, 0:81] = ket_ref[...]
    ket = ket_scr[...]
    high = ket.astype(BF)
    rest = ket - high.astype(F32)
    mid = rest.astype(BF)
    low = (rest - mid.astype(F32)).astype(BF)
    layers = []
    for layer in range(2):
        rows = masks_ref[form, layer, 0]
        cols = masks_ref[form, layer, 1]
        left = []
        for s in range(2):
            left.append(
                jnp.concatenate(
                    [(rows.astype(F32) * part[s : s + 1].astype(F32)).astype(BF) for part in (high, mid, low)],
                    axis=1,
                )
            )
        layers.append(dot_nt(jnp.concatenate(left, 0), jnp.concatenate([cols] * 3, 1)))
    first, second = layers
    return (first[:96] * second[:96] + first[96:] * second[96:]).astype(BF)


def flat_sketch(sketch, scr):
    scr[...] = sketch.astype(F32)
    return jnp.concatenate([scr[pl.ds(r, CHI, stride=D2), :] for r in range(D2)], 1).astype(BF)


def to_rows(wide, scr):
    for leg in range(8):
        scr[pl.ds(leg, CHI, stride=8), :] = lanes(wide, leg)
    return scr[...].astype(BF), lanes(wide, 8).astype(BF)


def split(value):
    high = value.astype(BF)
    return high, (value - high.astype(F32)).astype(BF)


def product(a, b):
    a_high, a_low = split(a)
    b_high, b_low = split(b)
    return dot(jnp.concatenate([a_high, a_low], 1), jnp.concatenate([b_high, b_high], 0)) + dot(a_high, b_low)


def start_inverse(gram):
    rows = lax.broadcasted_iota(jnp.int32, (CHI, CHI), 0)
    cols = lax.broadcasted_iota(jnp.int32, (CHI, CHI), 1)
    identity = jnp.where(rows == cols, 1.0, 0.0).astype(F32)
    scaling = jnp.sum(gram * identity) + EPS
    return identity, gram * (1.0 / scaling), scaling


def inverse_steps(gram):
    identity, current, scaling = start_inverse(gram)
    factor = 1.5 * identity - 0.5 * current
    inverse = factor
    current = product(factor, current)
    yield None
    for step in range(1, NS_STEPS):
        factor = 1.5 * identity - 0.5 * product(inverse, current)
        yield None
        if step + 1 < NS_STEPS:
            both = product(factor, jnp.concatenate([current, inverse], 1))
            current, inverse = lanes(both, 0), lanes(both, 1)
            yield None
        else:
            inverse = product(factor, inverse)
    yield inverse * lax.rsqrt(jnp.full((1, 1), scaling, F32))


def rescale(value):
    mean = jnp.sum(value * value) * (1.0 / value.size)
    return value * lax.rsqrt(jnp.full((1, 1), mean + EPS, F32))


PAIRS = CHI // 2
PIECES = ((0, 5), (5, 9))


def site_pairs(start, count, site, work):
    zs, ws, zb, wb = work

    def pair(step, carry):
        at = start + step
        z = zb[pl.ds(pl.multiple_of(at * 16, 16), 16), :]
        tail = zs[pl.ds(pl.multiple_of(at * 48, 48), 48), :]
        cols = []
        for h in range(2):
            cols.append(
                jnp.concatenate(
                    [lanes(z, q)[h * 8 : h * 8 + 8] for q in range(D2)] + [tail[h * 24 : h * 24 + 24]], 0
                )
            )
        w = dot(site, jnp.concatenate(cols, 1).astype(BF))
        halves = [lanes(w, h) for h in range(2)]
        wide = [jnp.concatenate([half[e * 8 : e * 8 + 8] for e in range(D2)], 1) for half in halves]
        wb[pl.ds(pl.multiple_of(at * 16, 16), 16), :] = jnp.concatenate(wide, 0).astype(BF)
        ws[pl.ds(pl.multiple_of(at * 32, 32), 32), :] = jnp.concatenate([half[72:88] for half in halves], 0)
        return carry

    lax.fori_loop(0, count, pair, 0, unroll=True)


def site_products(x8, x1, y, site, work, beside=None):
    zs, _, zb, _ = work
    z_last = dot(x1, y)
    for q in range(D2):
        zs[pl.ds(q, CHI, stride=24), :] = lanes(z_last, q)
    if beside is None:
        zb[...] = dot(x8[...], y)
        site_pairs(0, PAIRS, site, work)
        return None
    found = None
    for part in range(4):
        found = next(beside, found)
        zb[part * 256 : part * 256 + 256, :] = dot(x8[part * 256 : part * 256 + 256, :], y)
    for start in range(0, PAIRS, 6):
        found = next(beside, found)
        site_pairs(start, min(6, PAIRS - start), site, work)
    return found


def last_product(v8t, v1t, work, piece):
    ws, wb = work[1], work[3]
    low, high = piece
    w_last = jnp.concatenate([ws[pl.ds(e, CHI, stride=16), :] for e in range(low, high)], 1).astype(BF)
    return dot(v8t, wb[:, low * CHI : high * CHI]) + dot(v1t, w_last)


def columns(piece):
    return slice(piece[0] * CHI, piece[1] * CHI)


def leading(edge, scr):
    for leg in range(8):
        scr[pl.ds(leg, CHI, stride=8), :] = edge[leg].astype(F32)
    return scr[...].astype(BF)


def joined(one, other):
    return (one[...].astype(F32) + other[...].astype(F32)).astype(BF)


def stack_legs(wide):
    return jnp.concatenate([lanes(wide, leg) for leg in range(D2)], 0)


def right_turn(raw, right):
    turned = dot(stack_legs(raw), right)
    return jnp.concatenate([turned[r * CHI : (r + 1) * CHI] for r in range(D2)], 1).astype(BF)


SQ = (CHI, CHI)
FL = (CHI, WIDE)
PACK = (CHI, WIDE + 2 * CHI)
V = pltpu.VMEM
COPIES = 12
SENDS = 17
SCRATCH = dict(
    ket=V((8, 128), F32),
    ket_in=V((2, 81), F32),
    masks=V((4, 2, 2, 96, 128), BF),
    corners=V((2, CHI, CHI), BF),
    corner_tr=V(SQ, BF),
    edge_left=V((D2, CHI, CHI), BF),
    edges=V((2, D2, CHI, CHI), BF),
    edge_right=V((D2, CHI, CHI), BF),
    row_sketch=V((2, WIDE, CHI), BF),
    col_sketch=V((2, WIDE, CHI), BF),
    sites=V((4, 96, 96), BF),
    s_scr=V((WIDE, CHI), F32),
    rows=V((CHI * 8, CHI), F32),
    last=V(SQ, F32),
    zs=V((CHI * 24, CHI), F32),
    ws=V((CHI * 16, CHI), F32),
    zb=V((CHI * 8, WIDE), F32),
    wb=V((CHI * 8, WIDE), BF),
    pair8=V((CHI * 8, CHI), BF),
    pair1=V(SQ, BF),
    stacked=V((WIDE, CHI), BF),
    top8=V((CHI * 8, CHI), BF),
    terms=V((2, CHI, WIDE), BF),
    terms_in=V((2, CHI, WIDE), BF),
    root=V(SQ, BF),
    root_near=V(SQ, BF),
    root_far=V(SQ, BF),
    moved=V(FL, BF),
    moved_in=V(FL, BF),
    moved_ends=V((CHI, 2 * CHI), BF),
    moved_ends_in=V((CHI, 2 * CHI), BF),
    right=V(FL, BF),
    right_next=V(FL, BF),
    cut=V(FL, BF),
    cut_west=V(FL, BF),
    root_col=V(SQ, BF),
    root_col_near=V(SQ, BF),
    root_col_far=V(SQ, BF),
    raised=V(FL, BF),
    raised_in=V(FL, BF),
    raised_ends=V((CHI, 2 * CHI), BF),
    raised_ends_in=V((CHI, 2 * CHI), BF),
    left_pack=V(PACK, BF),
    top_pack=V(PACK, BF),
    out_sems=pltpu.SemaphoreType.DMA((2,)),
    in_sems=pltpu.SemaphoreType.DMA((COPIES,)),
    send_sems=pltpu.SemaphoreType.DMA((SENDS,)),
    recv_sems=pltpu.SemaphoreType.DMA((SENDS,)),
)


def move_kernel(ket, masks, corner_tl, corner_tr, corner_bl, edge_left, edge_top, edge_right, edge_bottom, row_sketch, col_sketch, left_out, top_out, *scratch):
    s = dict(zip(SCRATCH, scratch))
    work = (s["zs"], s["ws"], s["zb"], s["wb"])
    sources = (
        (ket, s["ket_in"]),
        (masks, s["masks"]),
        (edge_left, s["edge_left"]),
        (corner_bl, s["corners"].at[LOWER]),
        (corner_tl, s["corners"].at[UPPER]),
        (row_sketch, s["row_sketch"]),
        (edge_bottom, s["edges"].at[LOWER]),
        (edge_top, s["edges"].at[UPPER]),
        (corner_tr, s["corner_tr"]),
        (edge_right, s["edge_right"]),
        (col_sketch.at[1], s["col_sketch"].at[1]),
        (col_sketch.at[0], s["col_sketch"].at[0]),
    )
    loads = [pltpu.make_async_copy(a, b, s["in_sems"].at[n]) for n, (a, b) in enumerate(sources)]
    for load in loads:
        load.start()

    row, col = lax.axis_index("row"), lax.axis_index("col")
    row_count, col_count = lax.axis_size("row"), lax.axis_size("col")

    def device(down, across):
        return {
            "row": lax.rem(row + (row_count + down), row_count),
            "col": lax.rem(col + (col_count + across), col_count),
        }

    barrier = pltpu.get_barrier_semaphore()
    for offset in ((-1, 0), (1, 0), (0, -1), (0, 1), (1, 1), (-1, -1)):
        pl.semaphore_signal(barrier, inc=1, device_id=device(*offset), device_id_type=pl.DeviceIdType.MESH)

    def remote(number, source, target, down, across):
        return pltpu.make_async_remote_copy(
            src_ref=source,
            dst_ref=target,
            send_sem=s["send_sems"].at[number],
            recv_sem=s["recv_sems"].at[number],
            device_id=device(down, across),
            device_id_type=pl.DeviceIdType.MESH,
        )

    sent = []

    def send(source, target, down, across, piece=None):
        source, target = s[source], s[target]
        if piece is not None:
            source, target = source.at[:, columns(piece)], target.at[:, columns(piece)]
        copy = remote(len(sent) + 4, source, target, down, across)
        copy.start()
        sent.append(copy)
        return copy

    def send_term(which, number):
        places = (which, slice(None), columns(PIECES[number]))
        return remote(
            2 * which + number, s["terms"].at[places], s["terms_in"].at[places], 2 * which - 1, 0
        )

    def site(form):
        return s["sites"][form, 0:88, :]

    s["zs"][...] = jnp.zeros_like(s["zs"])
    for load in loads[:2]:
        load.wait()
    for form in (LOWER, UPPER):
        s["sites"][form] = site_form(s["ket_in"], s["masks"], form, s["ket"])
    for load in loads[2:8]:
        load.wait()

    half = row_count // 2
    far = (lax.rem(row, half) + 1) // half

    def term(step, carry):
        which = lax.rem(step + far, 2)

        @pl.when(which == LOWER)
        def _():
            corner_t = s["corners"][LOWER].T
            for leg in range(D2):
                turned = dot_nt(corner_t, s["edge_left"][leg])
                if leg < 8:
                    s["rows"][pl.ds(leg, CHI, stride=8), :] = turned
            s["last"][...] = turned

        @pl.when(which == UPPER)
        def _():
            corner = s["corners"][UPPER]
            for leg in range(D2):
                turned = dot(corner, s["edge_left"][leg])
                if leg < 8:
                    s["rows"][pl.ds(leg, CHI, stride=8), :] = turned
            s["last"][...] = turned

        v8t = s["rows"][...].astype(BF).T
        v1t = s["last"][...].astype(BF).T
        edge = s["edges"].at[which]
        site_products(
            leading(edge, s["rows"]),
            edge[8],
            flat_sketch(s["row_sketch"][1 - which], s["s_scr"]),
            s["sites"][which][0:88],
            work,
        )
        for number, piece in enumerate(PIECES):
            s["terms"][which, :, columns(piece)] = last_product(v8t, v1t, work, piece).astype(BF)
            if number == 0:

                @pl.when(step == 0)
                def _():
                    pl.semaphore_wait(barrier, 6)

            send_term(which, number).start()
        return carry

    lax.fori_loop(0, 2, term, 0)
    lower_copies = [send_term(LOWER, number) for number in range(2)]
    upper_copies = [send_term(UPPER, number) for number in range(2)]
    for form in (AHEAD, RIGHT):
        s["sites"][form] = site_form(s["ket_in"], s["masks"], form, s["ket"])
    left8 = leading(s["edge_left"], s["rows"])
    for leg in range(D2):
        s["stacked"][leg * CHI : (leg + 1) * CHI, :] = dot(
            s["corners"][LOWER], s["edges"][LOWER, leg]
        ).astype(BF)
    corner_t = s["corners"][UPPER].T
    for leg in range(D2):
        turned = dot(corner_t, s["edges"][UPPER, leg])
        if leg < 8:
            s["rows"][pl.ds(leg, CHI, stride=8), :] = turned
    s["pair8"][...] = s["rows"][...].astype(BF)
    s["pair1"][...] = turned.astype(BF)

    for copy in lower_copies:
        copy.wait_recv()
    cut = joined(s["terms"].at[UPPER], s["terms_in"].at[LOWER])
    s["cut"][...] = cut
    site_products(left8, s["edge_left"][8], cut, site(AHEAD), work)
    for copy in upper_copies:
        copy.wait_recv()
    v8, v1 = to_rows(joined(s["terms_in"].at[UPPER], s["terms"].at[LOWER]).astype(F32), s["rows"])
    v8t, v1t = v8.T, v1.T
    moved_copies = []
    for piece in PIECES:
        s["moved"][:, columns(piece)] = last_product(v8t, v1t, work, piece).astype(BF)
        moved_copies.append(send("moved", "moved_in", 0, 1, piece))
    first = dot(v8t, s["pair8"][...]) + dot(v1t, s["pair1"][...])
    stacked = stack_legs(s["cut"][...])
    second = dot_tn(stacked, jnp.concatenate([stacked, s["stacked"][...]], 1))
    s["moved_ends"][...] = jnp.concatenate([first, lanes(second, 1)], 1).astype(BF)
    moved_ends_copy = send("moved_ends", "moved_ends_in", 0, 1)

    for load in loads[8:11]:
        load.wait()
    corner_t = s["corner_tr"][...].T
    for leg in range(D2):
        turned = dot_nt(corner_t, s["edges"][UPPER, leg])
        if leg < 8:
            s["rows"][pl.ds(leg, CHI, stride=8), :] = turned
    v8t = s["rows"][...].astype(BF).T
    v1t = turned.astype(BF).T
    root = site_products(
        leading(s["edge_right"], s["rows"]),
        s["edge_right"][8],
        flat_sketch(s["col_sketch"][1], s["s_scr"]),
        site(RIGHT),
        work,
        inverse_steps(lanes(second, 0)),
    )
    s["root"][...] = root.astype(BF)
    near_copy = send("root", "root_near", 0, 1)
    far_copy = send("root", "root_far", 1, 1)
    s["right"][...] = last_product(v8t, v1t, work, (0, D2)).astype(BF)
    right_copy = send("right", "right_next", 0, -1)
    for leg in range(D2):
        s["stacked"][leg * CHI : (leg + 1) * CHI, :] = dot(s["corner_tr"][...], s["edge_right"][leg]).astype(BF)
    s["top8"][...] = leading(s["edges"].at[UPPER], s["rows"])
    loads[11].wait()
    y = flat_sketch(s["col_sketch"][0], s["s_scr"])

    for copy in (moved_ends_copy, near_copy, far_copy):
        copy.wait_recv()
    above_root = s["root_far"][...]
    own_root = s["root_near"][...]
    corner_mid = rescale(dot(above_root, s["moved_ends_in"][:, :CHI])).T.astype(BF)
    s["left_pack"][:, WIDE : WIDE + CHI] = corner_mid
    s["left_pack"][:, WIDE + CHI :] = rescale(dot(own_root, s["moved_ends_in"][:, CHI:])).astype(BF)
    for copy in moved_copies:
        copy.wait_recv()
    edge_new = rescale(dot(above_root, right_turn(s["moved_in"][...], own_root))).astype(BF)
    s["left_pack"][:, :WIDE] = edge_new
    left_copy = pltpu.make_async_copy(s["left_pack"], left_out, s["out_sems"].at[0])
    left_copy.start()
    side8, side1 = to_rows(dot(corner_mid, edge_new), s["rows"])
    s["pair8"][...] = side8
    s["pair1"][...] = side1
    site_products(s["pair8"], side1, y, site(AHEAD), work)
    v8t, v1t = s["top8"][...].T, s["edges"][UPPER, 8].T
    cut_copies = []
    for piece in PIECES:
        left_term = last_product(v8t, v1t, work, piece)
        if not cut_copies:
            right_copy.wait_recv()
        s["cut"][:, columns(piece)] = (left_term + s["right_next"][:, columns(piece)].astype(F32)).astype(BF)
        cut_copies.append(send("cut", "cut_west", 0, 1, piece))

    cut = s["cut"][...]
    stacked = stack_legs(cut)
    second = dot_tn(stacked, jnp.concatenate([stacked, s["stacked"][...]], 1))
    root = site_products(
        s["top8"], s["edges"][UPPER, 8], cut, site(UPPER), work, inverse_steps(lanes(second, 0))
    )
    s["root_col"][...] = root.astype(BF)
    near_copy = send("root_col", "root_col_near", 1, 0)
    far_copy = send("root_col", "root_col_far", 1, 1)
    for copy in cut_copies:
        copy.wait_recv()
    v8, v1 = to_rows(s["cut_west"][...].astype(F32), s["rows"])
    v8t, v1t = v8.T, v1.T
    raised_copies = []
    for piece in PIECES:
        s["raised"][:, columns(piece)] = last_product(v8t, v1t, work, piece).astype(BF)
        raised_copies.append(send("raised", "raised_in", 1, 0, piece))
    first = dot(v8t, s["pair8"][...]) + dot(v1t, s["pair1"][...])
    s["raised_ends"][...] = jnp.concatenate([first, lanes(second, 1)], 1).astype(BF)
    raised_ends_copy = send("raised_ends", "raised_ends_in", 1, 0)
    near_copy.wait_recv()
    far_copy.wait_recv()
    for copy in raised_copies:
        copy.wait_recv()
    west_root = s["root_col_far"][...]
    own_root = s["root_col_near"][...]
    s["top_pack"][:, :WIDE] = rescale(dot(west_root, right_turn(s["raised_in"][...], own_root))).astype(BF)
    raised_ends_copy.wait_recv()
    s["top_pack"][:, WIDE : WIDE + CHI] = rescale(dot(west_root, s["raised_ends_in"][:, :CHI])).astype(BF)
    s["top_pack"][:, WIDE + CHI :] = rescale(dot(own_root, s["raised_ends_in"][:, CHI:])).astype(BF)
    top_copy = pltpu.make_async_copy(s["top_pack"], top_out, s["out_sems"].at[1])
    top_copy.start()
    for copy in lower_copies + upper_copies + sent:
        copy.wait_send()
    left_copy.wait()
    top_copy.wait()


def result_kernel(left, top, edge_left, corner_bl, edge_top, corner_tl, corner_tr, left_scr, top_scr, in_sems, sems):
    blocks = [(left, left_scr, n, target) for n, target in enumerate([edge_left.at[leg] for leg in range(D2)])]
    blocks += [(left, left_scr, 10, corner_bl)]
    blocks += [(top, top_scr, n, target) for n, target in enumerate([edge_top.at[leg] for leg in range(D2)])]
    blocks += [(top, top_scr, 9, corner_tl), (top, top_scr, 10, corner_tr)]
    loads, stores = [], []
    for index, (pack, scr, n, target) in enumerate(blocks):
        block = scr.at[:, n * CHI : (n + 1) * CHI]
        loads.append(pltpu.make_async_copy(pack.at[:, n * CHI : (n + 1) * CHI], block, in_sems.at[index]))
        stores.append(pltpu.make_async_copy(block, target, sems.at[index]))
        loads[-1].start()
    for load, store in zip(loads, stores):
        load.wait()
        store.start()
    for store in stores:
        store.wait()


def local(*arrays):
    ket, corner_tl, corner_tr, corner_bl, *edges, row_sketch, col_sketch = [a.reshape(a.shape[2:]) for a in arrays]
    edges = [edge.transpose(1, 0, 2) for edge in edges]
    hbm = pl.BlockSpec(memory_space=pltpu.HBM)
    operands = (ket, jnp.asarray(site_masks(), BF), corner_tl, corner_tr, corner_bl, *edges, row_sketch, col_sketch)
    packs = pl.pallas_call(
        move_kernel,
        out_shape=[jax.ShapeDtypeStruct(PACK, BF)] * 2,
        in_specs=[hbm] * len(operands),
        out_specs=[hbm] * 2,
        scratch_shapes=list(SCRATCH.values()),
        compiler_params=pltpu.CompilerParams(
            vmem_limit_bytes=56 << 20, collective_id=0, has_side_effects=True
        ),
        name="moves",
    )(*operands)
    edge = jax.ShapeDtypeStruct((D2, CHI, CHI), BF)
    square = jax.ShapeDtypeStruct((CHI, CHI), BF)
    left, corner_bl, top, corner_tl, corner_tr = pl.pallas_call(
        result_kernel,
        out_shape=[edge, square, edge, square, square],
        in_specs=[hbm] * 2,
        out_specs=[hbm] * 5,
        scratch_shapes=[V(PACK, BF)] * 2 + [pltpu.SemaphoreType.DMA((2 * D2 + 3,))] * 2,
        name="results",
    )(*packs)
    results = (left.transpose(1, 0, 2), corner_bl, top.transpose(1, 0, 2), corner_tl, corner_tr)
    return tuple(value[None, None] for value in results)


def solution(mesh):
    four = P("row", "col", None, None)
    five = P("row", "col", None, None, None)
    return jax.shard_map(
        local,
        mesh=mesh,
        in_specs=(four, four, four, four, five, five, five, five, five, five),
        out_specs=(five, four, five, four, four),
        check_vma=False,
    )
```

```python
import numpy as np
import jax
import jax.numpy as jnp
from jax import lax
from jax.experimental import pallas as pl
from jax.experimental.pallas import tpu as pltpu
from jax.sharding import PartitionSpec as P

D = 3
D2 = 9
CHI = 128
NS_STEPS = 8
EPS = 1e-6
WIDE = D2 * CHI
BF = jnp.bfloat16
F32 = jnp.float32

FORMS = ((0, 1, 3, 2), (2, 1, 3, 0), (1, 0, 2, 3), (3, 0, 2, 1))
LOWER, UPPER, RIGHT, AHEAD = range(4)


def padded_legs():
    legs = [(-1, -1)] * 96
    for major in range(D2):
        for minor in range(8):
            legs[major * 8 + minor] = (major, minor)
        legs[72 + major] = (major, 8)
    return legs


def site_masks():
    legs = padded_legs()
    entry = np.stack(np.unravel_index(np.arange(81), (D,) * 4))
    masks = np.zeros((4, 2, 2, 96, 128), np.float32)
    for form, (out, v_leg, y_leg, x_leg) in enumerate(FORMS):
        for side, (major_leg, minor_leg) in enumerate(((out, v_leg), (y_leg, x_leg))):
            for row, (major, minor) in enumerate(legs):
                if major < 0:
                    continue
                for layer in range(2):
                    part = (lambda n: n // D) if layer == 0 else (lambda n: n % D)
                    fits = (entry[major_leg] == part(major)) & (entry[minor_leg] == part(minor))
                    masks[form, layer, side, row, :81] = fits
    return masks


def dot(a, b):
    return jnp.dot(a, b, preferred_element_type=F32)


def dot_nt(a, b):
    return lax.dot_general(a, b, (((1,), (1,)), ((), ())), preferred_element_type=F32)


def dot_tn(a, b):
    return lax.dot_general(a, b, (((0,), (0,)), ((), ())), preferred_element_type=F32)


def lanes(value, index):
    return value[:, index * CHI : (index + 1) * CHI]


def site_form(ket_ref, masks_ref, form, ket_scr):
    ket_scr[...] = jnp.zeros_like(ket_scr)
    ket_scr[0:2, 0:81] = ket_ref[...]
    ket = ket_scr[...]
    high = ket.astype(BF)
    rest = ket - high.astype(F32)
    mid = rest.astype(BF)
    low = (rest - mid.astype(F32)).astype(BF)
    layers = []
    for layer in range(2):
        rows = masks_ref[form, layer, 0]
        cols = masks_ref[form, layer, 1]
        left = []
        for s in range(2):
            left.append(
                jnp.concatenate(
                    [(rows.astype(F32) * part[s : s + 1].astype(F32)).astype(BF) for part in (high, mid, low)],
                    axis=1,
                )
            )
        layers.append(dot_nt(jnp.concatenate(left, 0), jnp.concatenate([cols] * 3, 1)))
    first, second = layers
    return (first[:96] * second[:96] + first[96:] * second[96:]).astype(BF)


def flat_sketch(sketch, scr):
    scr[...] = sketch.astype(F32)
    return jnp.concatenate([scr[pl.ds(r, CHI, stride=D2), :] for r in range(D2)], 1).astype(BF)


def to_rows(wide, scr):
    for leg in range(8):
        scr[pl.ds(leg, CHI, stride=8), :] = lanes(wide, leg)
    return scr[...].astype(BF), lanes(wide, 8).astype(BF)


def split(value):
    high = value.astype(BF)
    return high, (value - high.astype(F32)).astype(BF)


def product(a, b):
    a_high, a_low = split(a)
    b_high, b_low = split(b)
    return dot(jnp.concatenate([a_high, a_low], 1), jnp.concatenate([b_high, b_high], 0)) + dot(a_high, b_low)


def start_inverse(gram):
    rows = lax.broadcasted_iota(jnp.int32, (CHI, CHI), 0)
    cols = lax.broadcasted_iota(jnp.int32, (CHI, CHI), 1)
    identity = jnp.where(rows == cols, 1.0, 0.0).astype(F32)
    scaling = jnp.sum(gram * identity) + EPS
    return identity, gram * (1.0 / scaling), scaling


def inverse_steps(gram):
    identity, current, scaling = start_inverse(gram)
    factor = 1.5 * identity - 0.5 * current
    inverse = factor
    current = product(factor, current)
    yield None
    for step in range(1, NS_STEPS):
        factor = 1.5 * identity - 0.5 * product(inverse, current)
        yield None
        if step + 1 < NS_STEPS:
            both = product(factor, jnp.concatenate([current, inverse], 1))
            current, inverse = lanes(both, 0), lanes(both, 1)
            yield None
        else:
            inverse = product(factor, inverse)
    yield inverse * lax.rsqrt(jnp.full((1, 1), scaling, F32))


def rescale(value):
    mean = jnp.sum(value * value) * (1.0 / value.size)
    return value * lax.rsqrt(jnp.full((1, 1), mean + EPS, F32))


PAIRS = CHI // 2
PIECES = ((0, 5), (5, 9))


def site_pairs(start, count, site, work):
    zs, ws, zb, wb = work

    def pair(step, carry):
        at = start + step
        z = zb[pl.ds(pl.multiple_of(at * 16, 16), 16), :]
        tail = zs[pl.ds(pl.multiple_of(at * 48, 48), 48), :]
        cols = []
        for h in range(2):
            cols.append(
                jnp.concatenate(
                    [lanes(z, q)[h * 8 : h * 8 + 8] for q in range(D2)] + [tail[h * 24 : h * 24 + 24]], 0
                )
            )
        w = dot(site, jnp.concatenate(cols, 1).astype(BF))
        halves = [lanes(w, h) for h in range(2)]
        wide = [jnp.concatenate([half[e * 8 : e * 8 + 8] for e in range(D2)], 1) for half in halves]
        wb[pl.ds(pl.multiple_of(at * 16, 16), 16), :] = jnp.concatenate(wide, 0).astype(BF)
        ws[pl.ds(pl.multiple_of(at * 32, 32), 32), :] = jnp.concatenate([half[72:88] for half in halves], 0)
        return carry

    lax.fori_loop(0, count, pair, 0, unroll=True)


def site_products(x8, x1, y, site, work, beside=None):
    zs, _, zb, _ = work
    z_last = dot(x1, y)
    for q in range(D2):
        zs[pl.ds(q, CHI, stride=24), :] = lanes(z_last, q)
    if beside is None:
        zb[...] = dot(x8[...], y)
        site_pairs(0, PAIRS, site, work)
        return None
    found = None
    for part in range(4):
        found = next(beside, found)
        zb[part * 256 : part * 256 + 256, :] = dot(x8[part * 256 : part * 256 + 256, :], y)
    for start in range(0, PAIRS, 6):
        found = next(beside, found)
        site_pairs(start, min(6, PAIRS - start), site, work)
    return found


def last_product(v8t, v1t, work, piece):
    ws, wb = work[1], work[3]
    low, high = piece
    w_last = jnp.concatenate([ws[pl.ds(e, CHI, stride=16), :] for e in range(low, high)], 1).astype(BF)
    return dot(v8t, wb[:, low * CHI : high * CHI]) + dot(v1t, w_last)


def columns(piece):
    return slice(piece[0] * CHI, piece[1] * CHI)


def leading(edge, scr):
    for leg in range(8):
        scr[pl.ds(leg, CHI, stride=8), :] = edge[leg].astype(F32)
    return scr[...].astype(BF)


def joined(one, other):
    return (one[...].astype(F32) + other[...].astype(F32)).astype(BF)


def stack_legs(wide):
    return jnp.concatenate([lanes(wide, leg) for leg in range(D2)], 0)


def turned(raw, piece, left, right):
    legs = piece[1] - piece[0]
    stacked = jnp.concatenate([raw[:, leg * CHI : (leg + 1) * CHI] for leg in range(*piece)], 0)
    after = dot(stacked, right).astype(BF)
    return dot(left, jnp.concatenate([after[n * CHI : (n + 1) * CHI] for n in range(legs)], 1))


def factor_of(squares, size):
    return lax.rsqrt(jnp.full((1, 1), squares * (1.0 / size) + EPS, F32))


SQ = (CHI, CHI)
FL = (CHI, WIDE)
PACK = (CHI, WIDE + 2 * CHI)
TALL = (CHI * 8, CHI)
V = pltpu.VMEM
SENDS = 20
SCRATCH = dict(
    ket_scr=V((8, 128), F32),
    sites=V((4, 96, 96), BF),
    s_scr=V((WIDE, CHI), F32),
    rows=V(TALL, F32),
    rows_x=V(TALL, F32),
    last=V(SQ, F32),
    last_x=V(SQ, BF),
    zs=V((CHI * 24, CHI), F32),
    ws=V((CHI * 16, CHI), F32),
    zb=V((CHI * 8, WIDE), F32),
    wb=V((CHI * 8, WIDE), BF),
    left8=V(TALL, BF),
    left_y=V(FL, BF),
    pair8=V(TALL, BF),
    pair1=V(SQ, BF),
    below=V((WIDE, CHI), BF),
    beside=V((WIDE, CHI), BF),
    top8=V(TALL, BF),
    top8t=V((CHI, CHI * 8), BF),
    top1t=V(SQ, BF),
    terms=V((2, CHI, WIDE), BF),
    terms_in=V((2, CHI, WIDE), BF),
    root=V(SQ, BF),
    root_near=V(SQ, BF),
    root_far=V(SQ, BF),
    moved=V(FL, BF),
    moved_in=V(FL, BF),
    near=V(SQ, BF),
    near_in=V(SQ, BF),
    far=V(SQ, BF),
    far_in=V(SQ, BF),
    edge_raw=V(FL, F32),
    right=V(FL, BF),
    right_next=V(FL, BF),
    cut=V(FL, BF),
    cut_west=V(FL, BF),
    root_col=V(SQ, BF),
    root_col_near=V(SQ, BF),
    root_col_far=V(SQ, BF),
    raised=V(FL, BF),
    raised_in=V(FL, BF),
    near_up=V(SQ, BF),
    near_up_in=V(SQ, BF),
    far_up=V(SQ, BF),
    far_up_in=V(SQ, BF),
    send_sems=pltpu.SemaphoreType.DMA((SENDS,)),
    recv_sems=pltpu.SemaphoreType.DMA((SENDS,)),
)


def move_kernel(ket, masks, corner_tl, corner_tr, corner_bl, edge_left, edge_top, edge_right, edge_bottom, row_sketch, col_sketch, left_out, top_out, *scratch):
    s = dict(zip(SCRATCH, scratch))
    work = (s["zs"], s["ws"], s["zb"], s["wb"])
    row, col = lax.axis_index("row"), lax.axis_index("col")
    row_count, col_count = lax.axis_size("row"), lax.axis_size("col")

    def device(down, across):
        return {
            "row": lax.rem(row + (row_count + down), row_count),
            "col": lax.rem(col + (col_count + across), col_count),
        }

    barrier = pltpu.get_barrier_semaphore()
    for offset in ((-1, 0), (1, 0), (0, -1), (0, 1), (1, 1), (-1, -1)):
        pl.semaphore_signal(barrier, inc=1, device_id=device(*offset), device_id_type=pl.DeviceIdType.MESH)

    def remote(number, source, target, down, across):
        return pltpu.make_async_remote_copy(
            src_ref=source,
            dst_ref=target,
            send_sem=s["send_sems"].at[number],
            recv_sem=s["recv_sems"].at[number],
            device_id=device(down, across),
            device_id_type=pl.DeviceIdType.MESH,
        )

    sent = []

    def send(source, target, down, across, piece=None):
        source, target = s[source], s[target]
        if piece is not None:
            source, target = source.at[:, columns(piece)], target.at[:, columns(piece)]
        copy = remote(len(sent) + 4, source, target, down, across)
        copy.start()
        sent.append(copy)
        return copy

    def send_term(which, number):
        places = (which, slice(None), columns(PIECES[number]))
        return remote(
            2 * which + number, s["terms"].at[places], s["terms_in"].at[places], 2 * which - 1, 0
        )

    def site(form):
        return s["sites"][form, 0:88, :]

    def transposed_rows(wide_of):
        for leg in range(D2):
            value = wide_of(leg)
            if leg < 8:
                s["rows"][pl.ds(leg, CHI, stride=8), :] = value
        return s["rows"][...].astype(BF).T, value.astype(BF).T

    s["zs"][...] = jnp.zeros_like(s["zs"])
    for form in (LOWER, UPPER):
        s["sites"][form] = site_form(ket, masks, form, s["ket_scr"])

    half = row_count // 2
    far = (lax.rem(row, half) + 1) // half

    def term(step, carry):
        which = lax.rem(step + far, 2)

        def operands(edge, corner, product_of):
            for leg in range(8):
                s["rows_x"][pl.ds(leg, CHI, stride=8), :] = edge[leg].astype(F32)
            s["last_x"][...] = edge[8]
            for leg in range(D2):
                value = product_of(corner, edge_left[leg])
                if leg < 8:
                    s["rows"][pl.ds(leg, CHI, stride=8), :] = value
            s["last"][...] = value

        @pl.when(which == LOWER)
        def _():
            operands(edge_bottom, corner_bl[...].T, dot_nt)

        @pl.when(which == UPPER)
        def _():
            operands(edge_top, corner_tl[...], dot)

        site_products(
            s["rows_x"][...].astype(BF),
            s["last_x"][...],
            flat_sketch(row_sketch[1 - which], s["s_scr"]),
            s["sites"][which][0:88],
            work,
        )
        v8t = s["rows"][...].astype(BF).T
        v1t = s["last"][...].astype(BF).T
        for number, piece in enumerate(PIECES):
            s["terms"][which, :, columns(piece)] = last_product(v8t, v1t, work, piece).astype(BF)
            if number == 0:

                @pl.when(step == 0)
                def _():
                    pl.semaphore_wait(barrier, 6)

            send_term(which, number).start()
        return carry

    lax.fori_loop(0, 2, term, 0)
    lower_copies = [send_term(LOWER, number) for number in range(2)]
    upper_copies = [send_term(UPPER, number) for number in range(2)]
    s["left8"][...] = leading(edge_left, s["rows"])
    s["sites"][AHEAD] = site_form(ket, masks, AHEAD, s["ket_scr"])

    for copy in lower_copies:
        copy.wait_recv()
    cut = joined(s["terms"].at[UPPER], s["terms_in"].at[LOWER])
    s["cut"][...] = cut
    site_products(s["left8"], edge_left[8], cut, site(AHEAD), work)
    for copy, piece in zip(upper_copies, PIECES):
        copy.wait_recv()
        for leg in range(*piece):
            at = slice(leg * CHI, (leg + 1) * CHI)
            value = joined(s["terms_in"].at[UPPER, :, at], s["terms"].at[LOWER, :, at])
            if leg < 8:
                s["rows"][pl.ds(leg, CHI, stride=8), :] = value.astype(F32)
    v8 = s["rows"][...].astype(BF)
    v8t, v1t = v8.T, value.T
    moved_copies = []
    for piece in PIECES:
        s["moved"][:, columns(piece)] = last_product(v8t, v1t, work, piece).astype(BF)
        moved_copies.append(send("moved", "moved_in", 0, 1, piece))
    corner_t = corner_tl[...].T
    for leg in range(D2):
        value = dot(corner_t, edge_top[leg])
        if leg < 8:
            s["rows"][pl.ds(leg, CHI, stride=8), :] = value
    s["near"][...] = (dot(v8t, s["rows"][...].astype(BF)) + dot(v1t, value.astype(BF))).astype(BF)
    moved_near_copy = send("near", "near_in", 0, 1)
    for leg in range(D2):
        s["below"][leg * CHI : (leg + 1) * CHI, :] = dot(corner_bl[...], edge_bottom[leg]).astype(BF)
    stacked = stack_legs(s["cut"][...])
    second = dot_tn(stacked, jnp.concatenate([stacked, s["below"][...]], 1))
    s["far"][...] = lanes(second, 1).astype(BF)

    s["sites"][RIGHT] = site_form(ket, masks, RIGHT, s["ket_scr"])
    corner_t = corner_tr[...].T
    right8t, right1t = transposed_rows(lambda leg: dot_nt(corner_t, edge_top[leg]))
    root = site_products(
        leading(edge_right, s["rows_x"]),
        edge_right[8],
        flat_sketch(col_sketch[1], s["s_scr"]),
        site(RIGHT),
        work,
        inverse_steps(lanes(second, 0)),
    )
    s["root"][...] = root.astype(BF)
    near_copy = send("root", "root_near", 0, 1)
    far_copy = send("root", "root_far", 1, 1)
    moved_far_copy = send("far", "far_in", 0, 1)
    s["right"][...] = last_product(right8t, right1t, work, (0, D2)).astype(BF)
    right_copy = send("right", "right_next", 0, -1)
    for leg in range(D2):
        s["beside"][leg * CHI : (leg + 1) * CHI, :] = dot(corner_tr[...], edge_right[leg]).astype(BF)
    s["top8"][...] = leading(edge_top, s["rows"])
    s["top8t"][...] = s["top8"][...].T
    s["top1t"][...] = edge_top[8].T
    s["left_y"][...] = flat_sketch(col_sketch[0], s["s_scr"])

    for copy in (moved_near_copy, near_copy, far_copy):
        copy.wait_recv()
    above_root = s["root_far"][...]
    own_root = s["root_near"][...]
    corner_raw = dot(above_root, s["near_in"][...])
    corner_scale = factor_of(jnp.sum(corner_raw * corner_raw), CHI * CHI)
    corner_mid = corner_raw.T.astype(BF)
    for copy, piece in zip(moved_copies, PIECES):
        copy.wait_recv()
        edge_raw = turned(s["moved_in"], piece, above_root, own_root)
        s["edge_raw"][:, columns(piece)] = edge_raw
        side = dot(corner_mid, edge_raw.astype(BF))
        for leg in range(*piece):
            value = lanes(side, leg - piece[0])
            if leg < 8:
                s["rows"][pl.ds(leg, CHI, stride=8), :] = value
    s["pair8"][...] = s["rows"][...].astype(BF)
    s["pair1"][...] = value.astype(BF)
    site_products(s["pair8"], s["pair1"][...], s["left_y"][...], site(AHEAD), work)
    edge_raw = s["edge_raw"][...]
    edge_scale = factor_of(jnp.sum(edge_raw * edge_raw), CHI * WIDE)
    side_scale = edge_scale * corner_scale
    cut_copies = []
    for piece in PIECES:
        left_term = last_product(s["top8t"][...], s["top1t"][...], work, piece) * side_scale
        if not cut_copies:
            right_copy.wait_recv()
        s["cut"][:, columns(piece)] = (left_term + s["right_next"][:, columns(piece)].astype(F32)).astype(BF)
        cut_copies.append(send("cut", "cut_west", 0, 1, piece))

    cut = s["cut"][...]
    stacked = stack_legs(cut)
    second = dot_tn(stacked, jnp.concatenate([stacked, s["beside"][...]], 1))
    root = site_products(
        s["top8"], edge_top[8], cut, site(UPPER), work, inverse_steps(lanes(second, 0))
    )
    s["root_col"][...] = root.astype(BF)
    near_copy = send("root_col", "root_col_near", 1, 0)
    far_copy = send("root_col", "root_col_far", 1, 1)
    s["far_up"][...] = lanes(second, 1).astype(BF)
    raised_far_copy = send("far_up", "far_up_in", 1, 0)
    left_out[:, :WIDE] = (s["edge_raw"][...] * edge_scale).astype(BF)
    moved_far_copy.wait_recv()
    left_out[:, WIDE + CHI :] = rescale(dot(s["root_near"][...], s["far_in"][...])).astype(BF)
    left_out[:, WIDE : WIDE + CHI] = corner_mid
    for copy, piece in zip(cut_copies, PIECES):
        copy.wait_recv()
        for leg in range(*piece):
            value = s["cut_west"][:, leg * CHI : (leg + 1) * CHI]
            if leg < 8:
                s["rows"][pl.ds(leg, CHI, stride=8), :] = value.astype(F32)
    v8 = s["rows"][...].astype(BF)
    v8t, v1t = v8.T, value.T
    raised_copies = []
    for piece in PIECES:
        s["raised"][:, columns(piece)] = last_product(v8t, v1t, work, piece).astype(BF)
        raised_copies.append(send("raised", "raised_in", 1, 0, piece))
    first = (dot(v8t, s["pair8"][...]) + dot(v1t, s["pair1"][...])) * side_scale
    s["near_up"][...] = first.astype(BF)
    raised_near_copy = send("near_up", "near_up_in", 1, 0)

    for copy in (near_copy, far_copy, raised_far_copy):
        copy.wait_recv()
    west_root = s["root_col_far"][...]
    own_root = s["root_col_near"][...]
    top_out[:, WIDE + CHI :] = rescale(dot(own_root, s["far_up_in"][...])).astype(BF)
    parts = []
    for copy, piece in zip(raised_copies, PIECES):
        copy.wait_recv()
        parts.append(turned(s["raised_in"], piece, west_root, own_root))
    top_scale = factor_of(sum(jnp.sum(part * part) for part in parts), CHI * WIDE)
    for part, piece in zip(parts, PIECES):
        top_out[:, columns(piece)] = (part * top_scale).astype(BF)
    raised_near_copy.wait_recv()
    top_out[:, WIDE : WIDE + CHI] = rescale(dot(west_root, s["near_up_in"][...])).astype(BF)
    for copy in lower_copies + upper_copies + sent:
        copy.wait_send()


def result_kernel(left, top, edge_left, corner_bl, edge_top, corner_tl, corner_tr, sems):
    blocks = [(left, leg, edge_left.at[leg]) for leg in range(D2)]
    blocks += [(top, leg, edge_top.at[leg]) for leg in range(D2)]
    blocks += [(left, 10, corner_bl), (top, 9, corner_tl), (top, 10, corner_tr)]
    copies = [
        pltpu.make_async_copy(pack.at[:, n * CHI : (n + 1) * CHI], target, sems.at[index])
        for index, (pack, n, target) in enumerate(blocks)
    ]
    for copy in copies:
        copy.start()
    for copy in copies:
        copy.wait()


def local(*arrays):
    ket, corner_tl, corner_tr, corner_bl, *edges, row_sketch, col_sketch = [a.reshape(a.shape[2:]) for a in arrays]
    edges = [edge.transpose(1, 0, 2) for edge in edges]
    vmem = pl.BlockSpec(memory_space=pltpu.VMEM)
    hbm = pl.BlockSpec(memory_space=pltpu.HBM)
    operands = (ket, jnp.asarray(site_masks(), BF), corner_tl, corner_tr, corner_bl, *edges, row_sketch, col_sketch)
    packs = pl.pallas_call(
        move_kernel,
        out_shape=[jax.ShapeDtypeStruct(PACK, BF)] * 2,
        in_specs=[vmem] * len(operands),
        out_specs=[vmem] * 2,
        scratch_shapes=list(SCRATCH.values()),
        compiler_params=pltpu.CompilerParams(
            vmem_limit_bytes=44 << 20, collective_id=0, has_side_effects=True
        ),
        name="moves",
    )(*operands)
    edge = jax.ShapeDtypeStruct((D2, CHI, CHI), BF)
    square = jax.ShapeDtypeStruct((CHI, CHI), BF)
    left, corner_bl, top, corner_tl, corner_tr = pl.pallas_call(
        result_kernel,
        out_shape=[edge, square, edge, square, square],
        in_specs=[vmem] * 2,
        out_specs=[hbm] * 5,
        scratch_shapes=[pltpu.SemaphoreType.DMA((2 * D2 + 3,))],
        compiler_params=pltpu.CompilerParams(vmem_limit_bytes=4 << 20),
        name="results",
    )(*packs)
    results = (left.transpose(1, 0, 2), corner_bl, top.transpose(1, 0, 2), corner_tl, corner_tr)
    return tuple(value[None, None] for value in results)


def solution(mesh):
    four = P("row", "col", None, None)
    five = P("row", "col", None, None, None)
    return jax.shard_map(
        local,
        mesh=mesh,
        in_specs=(four, four, four, four, five, five, five, five, five, five),
        out_specs=(five, four, five, four, four),
        check_vma=False,
    )
```

```python
import numpy as np
import jax
import jax.numpy as jnp
from jax import lax
from jax.experimental import pallas as pl
from jax.experimental.pallas import tpu as pltpu
from jax.sharding import PartitionSpec as P

D = 3
D2 = 9
CHI = 128
NS_STEPS = 8
EPS = 1e-6
WIDE = D2 * CHI
BF = jnp.bfloat16
F32 = jnp.float32

FORMS = ((0, 1, 3, 2), (2, 1, 3, 0), (1, 0, 2, 3), (3, 0, 2, 1))
LOWER, UPPER, RIGHT, AHEAD = range(4)


def padded_legs():
    legs = [(-1, -1)] * 96
    for major in range(D2):
        for minor in range(8):
            legs[major * 8 + minor] = (major, minor)
        legs[72 + major] = (major, 8)
    return legs


def site_masks():
    legs = padded_legs()
    entry = np.stack(np.unravel_index(np.arange(81), (D,) * 4))
    masks = np.zeros((4, 2, 2, 96, 128), np.float32)
    for form, (out, v_leg, y_leg, x_leg) in enumerate(FORMS):
        for side, (major_leg, minor_leg) in enumerate(((out, v_leg), (y_leg, x_leg))):
            for row, (major, minor) in enumerate(legs):
                if major < 0:
                    continue
                for layer in range(2):
                    part = (lambda n: n // D) if layer == 0 else (lambda n: n % D)
                    fits = (entry[major_leg] == part(major)) & (entry[minor_leg] == part(minor))
                    masks[form, layer, side, row, :81] = fits
    return masks


def dot(a, b):
    return jnp.dot(a, b, preferred_element_type=F32)


def dot_nt(a, b):
    return lax.dot_general(a, b, (((1,), (1,)), ((), ())), preferred_element_type=F32)


def dot_tn(a, b):
    return lax.dot_general(a, b, (((0,), (0,)), ((), ())), preferred_element_type=F32)


def lanes(value, index):
    return value[:, index * CHI : (index + 1) * CHI]


def site_form(ket_ref, masks_ref, form, ket_scr):
    ket_scr[...] = jnp.zeros_like(ket_scr)
    ket_scr[0:2, 0:81] = ket_ref[...]
    ket = ket_scr[...]
    high = ket.astype(BF)
    rest = ket - high.astype(F32)
    mid = rest.astype(BF)
    low = (rest - mid.astype(F32)).astype(BF)
    layers = []
    for layer in range(2):
        rows = masks_ref[form, layer, 0]
        cols = masks_ref[form, layer, 1]
        left = []
        for s in range(2):
            left.append(
                jnp.concatenate(
                    [(rows.astype(F32) * part[s : s + 1].astype(F32)).astype(BF) for part in (high, mid, low)],
                    axis=1,
                )
            )
        layers.append(dot_nt(jnp.concatenate(left, 0), jnp.concatenate([cols] * 3, 1)))
    first, second = layers
    return (first[:96] * second[:96] + first[96:] * second[96:]).astype(BF)


def flat_sketch(sketch, scr):
    scr[...] = sketch.astype(F32)
    return jnp.concatenate([scr[pl.ds(r, CHI, stride=D2), :] for r in range(D2)], 1).astype(BF)


def to_rows(wide, scr):
    for leg in range(8):
        scr[pl.ds(leg, CHI, stride=8), :] = lanes(wide, leg)
    return scr[...].astype(BF), lanes(wide, 8).astype(BF)


def split(value):
    high = value.astype(BF)
    return high, (value - high.astype(F32)).astype(BF)


def product(a, b):
    a_high, a_low = split(a)
    b_high, b_low = split(b)
    return dot(jnp.concatenate([a_high, a_low], 1), jnp.concatenate([b_high, b_high], 0)) + dot(a_high, b_low)


def start_inverse(gram):
    rows = lax.broadcasted_iota(jnp.int32, (CHI, CHI), 0)
    cols = lax.broadcasted_iota(jnp.int32, (CHI, CHI), 1)
    identity = jnp.where(rows == cols, 1.0, 0.0).astype(F32)
    scaling = jnp.sum(gram * identity) + EPS
    return identity, gram * (1.0 / scaling), scaling


def inverse_steps(gram):
    identity, current, scaling = start_inverse(gram)
    factor = 1.5 * identity - 0.5 * current
    inverse = factor
    current = product(factor, current)
    yield None
    for step in range(1, NS_STEPS):
        factor = 1.5 * identity - 0.5 * product(inverse, current)
        yield None
        if step + 1 < NS_STEPS:
            both = product(factor, jnp.concatenate([current, inverse], 1))
            current, inverse = lanes(both, 0), lanes(both, 1)
            yield None
        else:
            inverse = product(factor, inverse)
    yield inverse * lax.rsqrt(jnp.full((1, 1), scaling, F32))


def rescale(value):
    mean = jnp.sum(value * value) * (1.0 / value.size)
    return value * lax.rsqrt(jnp.full((1, 1), mean + EPS, F32))


PAIRS = CHI // 2
PIECES = ((0, 5), (5, 9))


def site_pairs(start, count, site, work):
    zs, ws, zb, wb = work

    def pair(step, carry):
        at = start + step
        z = zb[pl.ds(pl.multiple_of(at * 16, 16), 16), :]
        tail = zs[pl.ds(pl.multiple_of(at * 48, 48), 48), :]
        cols = []
        for h in range(2):
            cols.append(
                jnp.concatenate(
                    [lanes(z, q)[h * 8 : h * 8 + 8] for q in range(D2)] + [tail[h * 24 : h * 24 + 24]], 0
                )
            )
        w = dot(site, jnp.concatenate(cols, 1).astype(BF))
        halves = [lanes(w, h) for h in range(2)]
        wide = [jnp.concatenate([half[e * 8 : e * 8 + 8] for e in range(D2)], 1) for half in halves]
        wb[pl.ds(pl.multiple_of(at * 16, 16), 16), :] = jnp.concatenate(wide, 0).astype(BF)
        ws[pl.ds(pl.multiple_of(at * 32, 32), 32), :] = jnp.concatenate([half[72:88] for half in halves], 0)
        return carry

    lax.fori_loop(0, count, pair, 0, unroll=True)


def site_products(x8, x1, y, site, work, beside=None):
    zs, _, zb, _ = work
    z_last = dot(x1, y)
    for q in range(D2):
        zs[pl.ds(q, CHI, stride=24), :] = lanes(z_last, q)
    if beside is None:
        zb[...] = dot(x8[...], y)
        site_pairs(0, PAIRS, site, work)
        return None
    found = None
    for part in range(4):
        found = next(beside, found)
        zb[part * 256 : part * 256 + 256, :] = dot(x8[part * 256 : part * 256 + 256, :], y)
    for start in range(0, PAIRS, 6):
        found = next(beside, found)
        site_pairs(start, min(6, PAIRS - start), site, work)
    return found


def last_product(v8t, v1t, work, piece):
    ws, wb = work[1], work[3]
    low, high = piece
    w_last = jnp.concatenate([ws[pl.ds(e, CHI, stride=16), :] for e in range(low, high)], 1).astype(BF)
    return dot(v8t, wb[:, low * CHI : high * CHI]) + dot(v1t, w_last)


def columns(piece):
    return slice(piece[0] * CHI, piece[1] * CHI)


def leading(edge, scr):
    for leg in range(8):
        scr[pl.ds(leg, CHI, stride=8), :] = edge[leg].astype(F32)
    return scr[...].astype(BF)


def joined(one, other):
    return (one[...].astype(F32) + other[...].astype(F32)).astype(BF)


def stack_legs(wide):
    return jnp.concatenate([lanes(wide, leg) for leg in range(D2)], 0)


def turned(raw, piece, left, right):
    legs = piece[1] - piece[0]
    stacked = jnp.concatenate([raw[:, leg * CHI : (leg + 1) * CHI] for leg in range(*piece)], 0)
    after = dot(stacked, right).astype(BF)
    return dot(left, jnp.concatenate([after[n * CHI : (n + 1) * CHI] for n in range(legs)], 1))


def factor_of(squares, size):
    return lax.rsqrt(jnp.full((1, 1), squares * (1.0 / size) + EPS, F32))


SQ = (CHI, CHI)
FL = (CHI, WIDE)
PACK = (CHI, WIDE + 2 * CHI)
TALL = (CHI * 8, CHI)
V = pltpu.VMEM
SENDS = 20
SCRATCH = dict(
    ket_scr=V((8, 128), F32),
    sites=V((4, 96, 96), BF),
    s_scr=V((WIDE, CHI), F32),
    rows=V(TALL, F32),
    rows_x=V(TALL, F32),
    last=V(SQ, F32),
    last_x=V(SQ, BF),
    zs=V((CHI * 24, CHI), F32),
    ws=V((CHI * 16, CHI), F32),
    zb=V((CHI * 8, WIDE), F32),
    wb=V((CHI * 8, WIDE), BF),
    left8=V(TALL, BF),
    left_y=V(FL, BF),
    pair8=V(TALL, BF),
    pair1=V(SQ, BF),
    below=V((WIDE, CHI), BF),
    beside=V((WIDE, CHI), BF),
    top8=V(TALL, BF),
    top8t=V((CHI, CHI * 8), BF),
    top1t=V(SQ, BF),
    terms=V((2, CHI, WIDE), BF),
    terms_in=V((2, CHI, WIDE), BF),
    root=V(SQ, BF),
    root_near=V(SQ, BF),
    root_far=V(SQ, BF),
    moved=V(FL, BF),
    moved_in=V(FL, BF),
    near=V(SQ, BF),
    near_in=V(SQ, BF),
    far=V(SQ, BF),
    far_in=V(SQ, BF),
    edge_raw=V(FL, F32),
    right=V(FL, BF),
    right_next=V(FL, BF),
    cut=V(FL, BF),
    cut_west=V(FL, BF),
    root_col=V(SQ, BF),
    root_col_near=V(SQ, BF),
    root_col_far=V(SQ, BF),
    raised=V(FL, BF),
    raised_in=V(FL, BF),
    near_up=V(SQ, BF),
    near_up_in=V(SQ, BF),
    far_up=V(SQ, BF),
    far_up_in=V(SQ, BF),
    ket=V((2, 81), F32),
    masks=V((4, 2, 2, 96, 128), BF),
    edge_left=V((D2, CHI, CHI), BF),
    edge_bottom=V((D2, CHI, CHI), BF),
    corner_bl=V(SQ, BF),
    row_sketch=V((2, WIDE, CHI), BF),
    edge_top=V((D2, CHI, CHI), BF),
    corner_tl=V(SQ, BF),
    corner_tr=V(SQ, BF),
    edge_right=V((D2, CHI, CHI), BF),
    col_sketch=V((2, WIDE, CHI), BF),
    in_sems=pltpu.SemaphoreType.DMA((11,)),
    send_sems=pltpu.SemaphoreType.DMA((SENDS,)),
    recv_sems=pltpu.SemaphoreType.DMA((SENDS,)),
)


INPUTS = (
    "ket",
    "masks",
    "edge_left",
    "edge_bottom",
    "corner_bl",
    "row_sketch",
    "edge_top",
    "corner_tl",
    "corner_tr",
    "edge_right",
    "col_sketch",
)


def move_kernel(*refs):
    sources, (left_out, top_out) = refs[: len(INPUTS)], refs[len(INPUTS) : len(INPUTS) + 2]
    s = dict(zip(SCRATCH, refs[len(INPUTS) + 2 :]))
    loads = {}
    for index, (name, source) in enumerate(zip(INPUTS, sources)):
        loads[name] = pltpu.make_async_copy(source, s[name], s["in_sems"].at[index])
        loads[name].start()
    ket, masks, edge_left, edge_bottom, corner_bl, row_sketch, edge_top, corner_tl, corner_tr, edge_right, col_sketch = [
        s[name] for name in INPUTS
    ]
    work = (s["zs"], s["ws"], s["zb"], s["wb"])
    row, col = lax.axis_index("row"), lax.axis_index("col")
    row_count, col_count = lax.axis_size("row"), lax.axis_size("col")

    def device(down, across):
        return {
            "row": lax.rem(row + (row_count + down), row_count),
            "col": lax.rem(col + (col_count + across), col_count),
        }

    barrier = pltpu.get_barrier_semaphore()
    for offset in ((-1, 0), (1, 0), (0, -1), (0, 1), (1, 1), (-1, -1)):
        pl.semaphore_signal(barrier, inc=1, device_id=device(*offset), device_id_type=pl.DeviceIdType.MESH)

    def remote(number, source, target, down, across):
        return pltpu.make_async_remote_copy(
            src_ref=source,
            dst_ref=target,
            send_sem=s["send_sems"].at[number],
            recv_sem=s["recv_sems"].at[number],
            device_id=device(down, across),
            device_id_type=pl.DeviceIdType.MESH,
        )

    sent = []

    def send(source, target, down, across, piece=None):
        source, target = s[source], s[target]
        if piece is not None:
            source, target = source.at[:, columns(piece)], target.at[:, columns(piece)]
        copy = remote(len(sent) + 4, source, target, down, across)
        copy.start()
        sent.append(copy)
        return copy

    def send_term(which, number):
        places = (which, slice(None), columns(PIECES[number]))
        return remote(
            2 * which + number, s["terms"].at[places], s["terms_in"].at[places], 2 * which - 1, 0
        )

    def site(form):
        return s["sites"][form, 0:88, :]

    def transposed_rows(wide_of):
        for leg in range(D2):
            value = wide_of(leg)
            if leg < 8:
                s["rows"][pl.ds(leg, CHI, stride=8), :] = value
        return s["rows"][...].astype(BF).T, value.astype(BF).T

    s["zs"][...] = jnp.zeros_like(s["zs"])
    for name in INPUTS[:8]:
        loads[name].wait()
    for form in (LOWER, UPPER):
        s["sites"][form] = site_form(ket, masks, form, s["ket_scr"])

    half = row_count // 2
    far = (lax.rem(row, half) + 1) // half

    def term(step, carry):
        which = lax.rem(step + far, 2)

        def operands(edge, corner, product_of):
            for leg in range(8):
                s["rows_x"][pl.ds(leg, CHI, stride=8), :] = edge[leg].astype(F32)
            s["last_x"][...] = edge[8]
            for leg in range(D2):
                value = product_of(corner, edge_left[leg])
                if leg < 8:
                    s["rows"][pl.ds(leg, CHI, stride=8), :] = value
            s["last"][...] = value

        @pl.when(which == LOWER)
        def _():
            operands(edge_bottom, corner_bl[...].T, dot_nt)

        @pl.when(which == UPPER)
        def _():
            operands(edge_top, corner_tl[...], dot)

        site_products(
            s["rows_x"][...].astype(BF),
            s["last_x"][...],
            flat_sketch(row_sketch[1 - which], s["s_scr"]),
            s["sites"][which][0:88],
            work,
        )
        v8t = s["rows"][...].astype(BF).T
        v1t = s["last"][...].astype(BF).T
        for number, piece in enumerate(PIECES):
            s["terms"][which, :, columns(piece)] = last_product(v8t, v1t, work, piece).astype(BF)
            if number == 0:

                @pl.when(step == 0)
                def _():
                    pl.semaphore_wait(barrier, 6)

            send_term(which, number).start()
        return carry

    lax.fori_loop(0, 2, term, 0)
    lower_copies = [send_term(LOWER, number) for number in range(2)]
    upper_copies = [send_term(UPPER, number) for number in range(2)]
    for name in INPUTS[8:]:
        loads[name].wait()
    s["left8"][...] = leading(edge_left, s["rows"])
    s["sites"][AHEAD] = site_form(ket, masks, AHEAD, s["ket_scr"])

    for copy in lower_copies:
        copy.wait_recv()
    cut = joined(s["terms"].at[UPPER], s["terms_in"].at[LOWER])
    s["cut"][...] = cut
    site_products(s["left8"], edge_left[8], cut, site(AHEAD), work)
    for copy, piece in zip(upper_copies, PIECES):
        copy.wait_recv()
        for leg in range(*piece):
            at = slice(leg * CHI, (leg + 1) * CHI)
            value = joined(s["terms_in"].at[UPPER, :, at], s["terms"].at[LOWER, :, at])
            if leg < 8:
                s["rows"][pl.ds(leg, CHI, stride=8), :] = value.astype(F32)
    v8 = s["rows"][...].astype(BF)
    v8t, v1t = v8.T, value.T
    moved_copies = []
    for piece in PIECES:
        s["moved"][:, columns(piece)] = last_product(v8t, v1t, work, piece).astype(BF)
        moved_copies.append(send("moved", "moved_in", 0, 1, piece))
    corner_t = corner_tl[...].T
    for leg in range(D2):
        value = dot(corner_t, edge_top[leg])
        if leg < 8:
            s["rows"][pl.ds(leg, CHI, stride=8), :] = value
    s["near"][...] = (dot(v8t, s["rows"][...].astype(BF)) + dot(v1t, value.astype(BF))).astype(BF)
    moved_near_copy = send("near", "near_in", 0, 1)
    for leg in range(D2):
        s["below"][leg * CHI : (leg + 1) * CHI, :] = dot(corner_bl[...], edge_bottom[leg]).astype(BF)
    stacked = stack_legs(s["cut"][...])
    second = dot_tn(stacked, jnp.concatenate([stacked, s["below"][...]], 1))
    s["far"][...] = lanes(second, 1).astype(BF)

    s["sites"][RIGHT] = site_form(ket, masks, RIGHT, s["ket_scr"])
    corner_t = corner_tr[...].T
    right8t, right1t = transposed_rows(lambda leg: dot_nt(corner_t, edge_top[leg]))
    root = site_products(
        leading(edge_right, s["rows_x"]),
        edge_right[8],
        flat_sketch(col_sketch[1], s["s_scr"]),
        site(RIGHT),
        work,
        inverse_steps(lanes(second, 0)),
    )
    s["root"][...] = root.astype(BF)
    near_copy = send("root", "root_near", 0, 1)
    far_copy = send("root", "root_far", 1, 1)
    moved_far_copy = send("far", "far_in", 0, 1)
    s["right"][...] = last_product(right8t, right1t, work, (0, D2)).astype(BF)
    right_copy = send("right", "right_next", 0, -1)
    for leg in range(D2):
        s["beside"][leg * CHI : (leg + 1) * CHI, :] = dot(corner_tr[...], edge_right[leg]).astype(BF)
    s["top8"][...] = leading(edge_top, s["rows"])
    s["top8t"][...] = s["top8"][...].T
    s["top1t"][...] = edge_top[8].T
    s["left_y"][...] = flat_sketch(col_sketch[0], s["s_scr"])

    for copy in (moved_near_copy, near_copy, far_copy):
        copy.wait_recv()
    above_root = s["root_far"][...]
    own_root = s["root_near"][...]
    corner_raw = dot(above_root, s["near_in"][...])
    corner_scale = factor_of(jnp.sum(corner_raw * corner_raw), CHI * CHI)
    corner_mid = corner_raw.T.astype(BF)
    for copy, piece in zip(moved_copies, PIECES):
        copy.wait_recv()
        edge_raw = turned(s["moved_in"], piece, above_root, own_root)
        s["edge_raw"][:, columns(piece)] = edge_raw
        side = dot(corner_mid, edge_raw.astype(BF))
        for leg in range(*piece):
            value = lanes(side, leg - piece[0])
            if leg < 8:
                s["rows"][pl.ds(leg, CHI, stride=8), :] = value
    s["pair8"][...] = s["rows"][...].astype(BF)
    s["pair1"][...] = value.astype(BF)
    site_products(s["pair8"], s["pair1"][...], s["left_y"][...], site(AHEAD), work)
    edge_raw = s["edge_raw"][...]
    edge_scale = factor_of(jnp.sum(edge_raw * edge_raw), CHI * WIDE)
    side_scale = edge_scale * corner_scale
    cut_copies = []
    for piece in PIECES:
        left_term = last_product(s["top8t"][...], s["top1t"][...], work, piece) * side_scale
        if not cut_copies:
            right_copy.wait_recv()
        s["cut"][:, columns(piece)] = (left_term + s["right_next"][:, columns(piece)].astype(F32)).astype(BF)
        cut_copies.append(send("cut", "cut_west", 0, 1, piece))

    cut = s["cut"][...]
    stacked = stack_legs(cut)
    second = dot_tn(stacked, jnp.concatenate([stacked, s["beside"][...]], 1))
    root = site_products(
        s["top8"], edge_top[8], cut, site(UPPER), work, inverse_steps(lanes(second, 0))
    )
    s["root_col"][...] = root.astype(BF)
    near_copy = send("root_col", "root_col_near", 1, 0)
    far_copy = send("root_col", "root_col_far", 1, 1)
    s["far_up"][...] = lanes(second, 1).astype(BF)
    raised_far_copy = send("far_up", "far_up_in", 1, 0)
    left_out[:, :WIDE] = (s["edge_raw"][...] * edge_scale).astype(BF)
    moved_far_copy.wait_recv()
    left_out[:, WIDE + CHI :] = rescale(dot(s["root_near"][...], s["far_in"][...])).astype(BF)
    left_out[:, WIDE : WIDE + CHI] = corner_mid
    for copy, piece in zip(cut_copies, PIECES):
        copy.wait_recv()
        for leg in range(*piece):
            value = s["cut_west"][:, leg * CHI : (leg + 1) * CHI]
            if leg < 8:
                s["rows"][pl.ds(leg, CHI, stride=8), :] = value.astype(F32)
    v8 = s["rows"][...].astype(BF)
    v8t, v1t = v8.T, value.T
    raised_copies = []
    for piece in PIECES:
        s["raised"][:, columns(piece)] = last_product(v8t, v1t, work, piece).astype(BF)
        raised_copies.append(send("raised", "raised_in", 1, 0, piece))
    first = (dot(v8t, s["pair8"][...]) + dot(v1t, s["pair1"][...])) * side_scale
    s["near_up"][...] = first.astype(BF)
    raised_near_copy = send("near_up", "near_up_in", 1, 0)

    for copy in (near_copy, far_copy, raised_far_copy):
        copy.wait_recv()
    west_root = s["root_col_far"][...]
    own_root = s["root_col_near"][...]
    top_out[:, WIDE + CHI :] = rescale(dot(own_root, s["far_up_in"][...])).astype(BF)
    parts = []
    for copy, piece in zip(raised_copies, PIECES):
        copy.wait_recv()
        parts.append(turned(s["raised_in"], piece, west_root, own_root))
    top_scale = factor_of(sum(jnp.sum(part * part) for part in parts), CHI * WIDE)
    for part, piece in zip(parts, PIECES):
        top_out[:, columns(piece)] = (part * top_scale).astype(BF)
    raised_near_copy.wait_recv()
    top_out[:, WIDE : WIDE + CHI] = rescale(dot(west_root, s["near_up_in"][...])).astype(BF)
    for copy in lower_copies + upper_copies + sent:
        copy.wait_send()


def result_kernel(left, top, edge_left, corner_bl, edge_top, corner_tl, corner_tr, sems):
    blocks = [(left, leg, edge_left.at[leg]) for leg in range(D2)]
    blocks += [(top, leg, edge_top.at[leg]) for leg in range(D2)]
    blocks += [(left, 10, corner_bl), (top, 9, corner_tl), (top, 10, corner_tr)]
    copies = [
        pltpu.make_async_copy(pack.at[:, n * CHI : (n + 1) * CHI], target, sems.at[index])
        for index, (pack, n, target) in enumerate(blocks)
    ]
    for copy in copies:
        copy.start()
    for copy in copies:
        copy.wait()


def local(*arrays):
    ket, corner_tl, corner_tr, corner_bl, *edges, row_sketch, col_sketch = [a.reshape(a.shape[2:]) for a in arrays]
    edges = [edge.transpose(1, 0, 2) for edge in edges]
    vmem = pl.BlockSpec(memory_space=pltpu.VMEM)
    hbm = pl.BlockSpec(memory_space=pltpu.HBM)
    operands = tuple(pltpu.with_memory_space_constraint(x, pltpu.HBM) for x in (ket, jnp.asarray(site_masks(), BF), edges[0], edges[3], corner_bl, row_sketch, edges[1], corner_tl, corner_tr, edges[2], col_sketch))
    packs = pl.pallas_call(
        move_kernel,
        out_shape=[jax.ShapeDtypeStruct(PACK, BF)] * 2,
        in_specs=[hbm] * len(operands),
        out_specs=[vmem] * 2,
        scratch_shapes=list(SCRATCH.values()),
        compiler_params=pltpu.CompilerParams(
            vmem_limit_bytes=44 << 20, collective_id=0, has_side_effects=True
        ),
        name="moves",
    )(*operands)
    edge = jax.ShapeDtypeStruct((D2, CHI, CHI), BF)
    square = jax.ShapeDtypeStruct((CHI, CHI), BF)
    left, corner_bl, top, corner_tl, corner_tr = pl.pallas_call(
        result_kernel,
        out_shape=[edge, square, edge, square, square],
        in_specs=[vmem] * 2,
        out_specs=[hbm] * 5,
        scratch_shapes=[pltpu.SemaphoreType.DMA((2 * D2 + 3,))],
        compiler_params=pltpu.CompilerParams(vmem_limit_bytes=4 << 20),
        name="results",
    )(*packs)
    results = (left.transpose(1, 0, 2), corner_bl, top.transpose(1, 0, 2), corner_tl, corner_tr)
    return tuple(value[None, None] for value in results)


def solution(mesh):
    four = P("row", "col", None, None)
    five = P("row", "col", None, None, None)
    return jax.shard_map(
        local,
        mesh=mesh,
        in_specs=(four, four, four, four, five, five, five, five, five, five),
        out_specs=(five, four, five, four, four),
        check_vma=False,
    )
```

```python
import numpy as np
import jax
import jax.numpy as jnp
from jax import lax
from jax.experimental import pallas as pl
from jax.experimental.pallas import tpu as pltpu
from jax.sharding import PartitionSpec as P

D = 3
D2 = 9
CHI = 128
NS_STEPS = 8
EPS = 1e-6
WIDE = D2 * CHI
BF = jnp.bfloat16
F32 = jnp.float32

FORMS = ((0, 1, 3, 2), (2, 1, 3, 0), (1, 0, 2, 3), (3, 0, 2, 1))
LOWER, UPPER, RIGHT, AHEAD = range(4)


def padded_legs():
    legs = [(-1, -1)] * 96
    for major in range(D2):
        for minor in range(8):
            legs[major * 8 + minor] = (major, minor)
        legs[72 + major] = (major, 8)
    return legs


def site_masks():
    legs = padded_legs()
    entry = np.stack(np.unravel_index(np.arange(81), (D,) * 4))
    masks = np.zeros((4, 2, 2, 96, 128), np.float32)
    for form, (out, v_leg, y_leg, x_leg) in enumerate(FORMS):
        for side, (major_leg, minor_leg) in enumerate(((out, v_leg), (y_leg, x_leg))):
            for row, (major, minor) in enumerate(legs):
                if major < 0:
                    continue
                for layer in range(2):
                    part = (lambda n: n // D) if layer == 0 else (lambda n: n % D)
                    fits = (entry[major_leg] == part(major)) & (entry[minor_leg] == part(minor))
                    masks[form, layer, side, row, :81] = fits
    return masks


def dot(a, b):
    return jnp.dot(a, b, preferred_element_type=F32)


def dot_nt(a, b):
    return lax.dot_general(a, b, (((1,), (1,)), ((), ())), preferred_element_type=F32)


def dot_tn(a, b):
    return lax.dot_general(a, b, (((0,), (0,)), ((), ())), preferred_element_type=F32)


def lanes(value, index):
    return value[:, index * CHI : (index + 1) * CHI]


def site_form(ket_ref, masks_ref, form, ket_scr):
    ket_scr[...] = jnp.zeros_like(ket_scr)
    ket_scr[0:2, 0:81] = ket_ref[...]
    ket = ket_scr[...]
    high = ket.astype(BF)
    rest = ket - high.astype(F32)
    mid = rest.astype(BF)
    low = (rest - mid.astype(F32)).astype(BF)
    layers = []
    for layer in range(2):
        rows = masks_ref[form, layer, 0]
        cols = masks_ref[form, layer, 1]
        left = []
        for s in range(2):
            left.append(
                jnp.concatenate(
                    [(rows.astype(F32) * part[s : s + 1].astype(F32)).astype(BF) for part in (high, mid, low)],
                    axis=1,
                )
            )
        layers.append(dot_nt(jnp.concatenate(left, 0), jnp.concatenate([cols] * 3, 1)))
    first, second = layers
    return (first[:96] * second[:96] + first[96:] * second[96:]).astype(BF)


def flat_sketch(sketch, scr):
    scr[...] = sketch.astype(F32)
    return jnp.concatenate([scr[pl.ds(r, CHI, stride=D2), :] for r in range(D2)], 1).astype(BF)


def to_rows(wide, scr):
    for leg in range(8):
        scr[pl.ds(leg, CHI, stride=8), :] = lanes(wide, leg)
    return scr[...].astype(BF), lanes(wide, 8).astype(BF)


def split(value):
    high = value.astype(BF)
    return high, (value - high.astype(F32)).astype(BF)


def product(a, b):
    a_high, a_low = split(a)
    b_high, b_low = split(b)
    return dot(jnp.concatenate([a_high, a_low], 1), jnp.concatenate([b_high, b_high], 0)) + dot(a_high, b_low)


def start_inverse(gram):
    rows = lax.broadcasted_iota(jnp.int32, (CHI, CHI), 0)
    cols = lax.broadcasted_iota(jnp.int32, (CHI, CHI), 1)
    identity = jnp.where(rows == cols, 1.0, 0.0).astype(F32)
    scaling = jnp.sum(gram * identity) + EPS
    return identity, gram * (1.0 / scaling), scaling


def inverse_steps(gram):
    identity, current, scaling = start_inverse(gram)
    factor = 1.5 * identity - 0.5 * current
    inverse = factor
    current = product(factor, current)
    yield None
    for step in range(1, NS_STEPS):
        factor = 1.5 * identity - 0.5 * product(inverse, current)
        yield None
        if step + 1 < NS_STEPS:
            both = product(factor, jnp.concatenate([current, inverse], 1))
            current, inverse = lanes(both, 0), lanes(both, 1)
            yield None
        else:
            inverse = product(factor, inverse)
    yield inverse * lax.rsqrt(jnp.full((1, 1), scaling, F32))


def rescale(value):
    mean = jnp.sum(value * value) * (1.0 / value.size)
    return value * lax.rsqrt(jnp.full((1, 1), mean + EPS, F32))


PAIRS = CHI // 2
PIECES = ((0, 5), (5, 9))


def site_pairs(start, count, site, work):
    zs, ws, zb, wb = work

    def pair(step, carry):
        at = start + step
        z = zb[pl.ds(pl.multiple_of(at * 16, 16), 16), :]
        tail = zs[pl.ds(pl.multiple_of(at * 48, 48), 48), :]
        cols = []
        for h in range(2):
            cols.append(
                jnp.concatenate(
                    [lanes(z, q)[h * 8 : h * 8 + 8] for q in range(D2)] + [tail[h * 24 : h * 24 + 24]], 0
                )
            )
        w = dot(site, jnp.concatenate(cols, 1).astype(BF))
        halves = [lanes(w, h) for h in range(2)]
        wide = [jnp.concatenate([half[e * 8 : e * 8 + 8] for e in range(D2)], 1) for half in halves]
        wb[pl.ds(pl.multiple_of(at * 16, 16), 16), :] = jnp.concatenate(wide, 0).astype(BF)
        ws[pl.ds(pl.multiple_of(at * 32, 32), 32), :] = jnp.concatenate([half[72:88] for half in halves], 0)
        return carry

    lax.fori_loop(0, count, pair, 0, unroll=True)


def site_products(x8, x1, y, site, work, beside=None):
    zs, _, zb, _ = work
    z_last = dot(x1, y)
    for q in range(D2):
        zs[pl.ds(q, CHI, stride=24), :] = lanes(z_last, q)
    if beside is None:
        zb[...] = dot(x8[...], y)
        site_pairs(0, PAIRS, site, work)
        return None
    found = None
    for part in range(4):
        found = next(beside, found)
        zb[part * 256 : part * 256 + 256, :] = dot(x8[part * 256 : part * 256 + 256, :], y)
    for start in range(0, PAIRS, 6):
        found = next(beside, found)
        site_pairs(start, min(6, PAIRS - start), site, work)
    return found


def last_product(v8t, v1t, work, piece):
    ws, wb = work[1], work[3]
    low, high = piece
    w_last = jnp.concatenate([ws[pl.ds(e, CHI, stride=16), :] for e in range(low, high)], 1).astype(BF)
    return dot(v8t, wb[:, low * CHI : high * CHI]) + dot(v1t, w_last)


def columns(piece):
    return slice(piece[0] * CHI, piece[1] * CHI)


def leading(edge, scr):
    for leg in range(8):
        scr[pl.ds(leg, CHI, stride=8), :] = edge[leg].astype(F32)
    return scr[...].astype(BF)


def joined(one, other):
    return (one[...].astype(F32) + other[...].astype(F32)).astype(BF)


def stack_legs(wide):
    return jnp.concatenate([lanes(wide, leg) for leg in range(D2)], 0)


def turned(raw, piece, left, right):
    legs = piece[1] - piece[0]
    stacked = jnp.concatenate([raw[:, leg * CHI : (leg + 1) * CHI] for leg in range(*piece)], 0)
    after = dot(stacked, right).astype(BF)
    return dot(left, jnp.concatenate([after[n * CHI : (n + 1) * CHI] for n in range(legs)], 1))


def factor_of(squares, size):
    return lax.rsqrt(jnp.full((1, 1), squares * (1.0 / size) + EPS, F32))


SQ = (CHI, CHI)
FL = (CHI, WIDE)
PACK = (CHI, WIDE + 2 * CHI)
TALL = (CHI * 8, CHI)
V = pltpu.VMEM
SENDS = 20
SCRATCH = dict(
    ket_scr=V((8, 128), F32),
    sites=V((4, 96, 96), BF),
    s_scr=V((WIDE, CHI), F32),
    rows=V(TALL, F32),
    rows_x=V(TALL, F32),
    last=V(SQ, F32),
    last_x=V(SQ, BF),
    zs=V((CHI * 24, CHI), F32),
    ws=V((CHI * 16, CHI), F32),
    zb=V((CHI * 8, WIDE), F32),
    wb=V((CHI * 8, WIDE), BF),
    left8=V(TALL, BF),
    left_y=V(FL, BF),
    pair8=V(TALL, BF),
    pair1=V(SQ, BF),
    below=V((WIDE, CHI), BF),
    beside=V((WIDE, CHI), BF),
    top8=V(TALL, BF),
    top8t=V((CHI, CHI * 8), BF),
    top1t=V(SQ, BF),
    terms=V((2, CHI, WIDE), BF),
    terms_in=V((2, CHI, WIDE), BF),
    root=V(SQ, BF),
    root_near=V(SQ, BF),
    root_far=V(SQ, BF),
    moved=V(FL, BF),
    moved_in=V(FL, BF),
    near=V(SQ, BF),
    near_in=V(SQ, BF),
    far=V(SQ, BF),
    far_in=V(SQ, BF),
    edge_raw=V(FL, F32),
    right=V(FL, BF),
    right_next=V(FL, BF),
    cut=V(FL, BF),
    cut_west=V(FL, BF),
    root_col=V(SQ, BF),
    root_col_near=V(SQ, BF),
    root_col_far=V(SQ, BF),
    raised=V(FL, BF),
    raised_in=V(FL, BF),
    near_up=V(SQ, BF),
    near_up_in=V(SQ, BF),
    far_up=V(SQ, BF),
    far_up_in=V(SQ, BF),
    ket=V((2, 81), F32),
    masks=V((4, 2, 2, 96, 128), BF),
    edge_left=V((D2, CHI, CHI), BF),
    edge_bottom=V((D2, CHI, CHI), BF),
    corner_bl=V(SQ, BF),
    row_sketch=V((2, WIDE, CHI), BF),
    edge_top=V((D2, CHI, CHI), BF),
    corner_tl=V(SQ, BF),
    corner_tr=V(SQ, BF),
    edge_right=V((D2, CHI, CHI), BF),
    col_sketch=V((2, WIDE, CHI), BF),
    in_sems=pltpu.SemaphoreType.DMA((11,)),
    send_sems=pltpu.SemaphoreType.DMA((SENDS,)),
    recv_sems=pltpu.SemaphoreType.DMA((SENDS,)),
)


INPUTS = (
    "ket",
    "masks",
    "edge_left",
    "edge_bottom",
    "corner_bl",
    "row_sketch",
    "edge_top",
    "corner_tl",
    "corner_tr",
    "edge_right",
    "col_sketch",
)


def move_kernel(*refs):
    sources, (left_out, top_out) = refs[: len(INPUTS)], refs[len(INPUTS) : len(INPUTS) + 2]
    s = dict(zip(SCRATCH, refs[len(INPUTS) + 2 :]))
    loads = {}
    for index, (name, source) in enumerate(zip(INPUTS, sources)):
        loads[name] = pltpu.make_async_copy(source, s[name], s["in_sems"].at[index])
        loads[name].start()
    ket, masks, edge_left, edge_bottom, corner_bl, row_sketch, edge_top, corner_tl, corner_tr, edge_right, col_sketch = [
        s[name] for name in INPUTS
    ]
    work = (s["zs"], s["ws"], s["zb"], s["wb"])
    row, col = lax.axis_index("row"), lax.axis_index("col")
    row_count, col_count = lax.axis_size("row"), lax.axis_size("col")

    def device(down, across):
        return {
            "row": lax.rem(row + (row_count + down), row_count),
            "col": lax.rem(col + (col_count + across), col_count),
        }

    barrier = pltpu.get_barrier_semaphore()
    for offset in ((-1, 0), (1, 0), (0, -1), (0, 1), (1, 1), (-1, -1)):
        pl.semaphore_signal(barrier, inc=1, device_id=device(*offset), device_id_type=pl.DeviceIdType.MESH)

    def remote(number, source, target, down, across):
        return pltpu.make_async_remote_copy(
            src_ref=source,
            dst_ref=target,
            send_sem=s["send_sems"].at[number],
            recv_sem=s["recv_sems"].at[number],
            device_id=device(down, across),
            device_id_type=pl.DeviceIdType.MESH,
        )

    sent = []

    def send(source, target, down, across, piece=None):
        source, target = s[source], s[target]
        if piece is not None:
            source, target = source.at[:, columns(piece)], target.at[:, columns(piece)]
        copy = remote(len(sent) + 4, source, target, down, across)
        copy.start()
        sent.append(copy)
        return copy

    def send_term(which, number):
        places = (which, slice(None), columns(PIECES[number]))
        return remote(
            2 * which + number, s["terms"].at[places], s["terms_in"].at[places], 2 * which - 1, 0
        )

    def site(form):
        return s["sites"][form, 0:88, :]

    def transposed_rows(wide_of):
        for leg in range(D2):
            value = wide_of(leg)
            if leg < 8:
                s["rows"][pl.ds(leg, CHI, stride=8), :] = value
        return s["rows"][...].astype(BF).T, value.astype(BF).T

    s["zs"][...] = jnp.zeros_like(s["zs"])
    for name in INPUTS[:8]:
        loads[name].wait()
    for form in (LOWER, UPPER):
        s["sites"][form] = site_form(ket, masks, form, s["ket_scr"])

    half = row_count // 2
    far = (lax.rem(row, half) + 1) // half

    def term(step, carry):
        which = lax.rem(step + far, 2)

        def operands(edge, corner, product_of):
            for leg in range(8):
                s["rows_x"][pl.ds(leg, CHI, stride=8), :] = edge[leg].astype(F32)
            s["last_x"][...] = edge[8]
            for leg in range(D2):
                value = product_of(corner, edge_left[leg])
                if leg < 8:
                    s["rows"][pl.ds(leg, CHI, stride=8), :] = value
            s["last"][...] = value

        @pl.when(which == LOWER)
        def _():
            operands(edge_bottom, corner_bl[...].T, dot_nt)

        @pl.when(which == UPPER)
        def _():
            operands(edge_top, corner_tl[...], dot)

        site_products(
            s["rows_x"][...].astype(BF),
            s["last_x"][...],
            flat_sketch(row_sketch[1 - which], s["s_scr"]),
            s["sites"][which][0:88],
            work,
        )
        v8t = s["rows"][...].astype(BF).T
        v1t = s["last"][...].astype(BF).T
        for number, piece in enumerate(PIECES):
            s["terms"][which, :, columns(piece)] = last_product(v8t, v1t, work, piece).astype(BF)
            if number == 0:

                @pl.when(step == 0)
                def _():
                    pl.semaphore_wait(barrier, 6)

            send_term(which, number).start()
        return carry

    lax.fori_loop(0, 2, term, 0)
    lower_copies = [send_term(LOWER, number) for number in range(2)]
    upper_copies = [send_term(UPPER, number) for number in range(2)]
    for name in INPUTS[8:]:
        loads[name].wait()
    s["left8"][...] = leading(edge_left, s["rows"])
    for leg in range(D2):
        s["below"][leg * CHI : (leg + 1) * CHI, :] = dot(corner_bl[...], edge_bottom[leg]).astype(BF)
    corner_t = corner_tl[...].T
    for leg in range(D2):
        value = dot(corner_t, edge_top[leg])
        if leg < 8:
            s["rows_x"][pl.ds(leg, CHI, stride=8), :] = value
    s["pair8"][...] = s["rows_x"][...].astype(BF)
    s["pair1"][...] = value.astype(BF)
    s["sites"][AHEAD] = site_form(ket, masks, AHEAD, s["ket_scr"])

    for copy in lower_copies:
        copy.wait_recv()
    cut = joined(s["terms"].at[UPPER], s["terms_in"].at[LOWER])
    stacked = stack_legs(cut)
    second = dot_tn(stacked, jnp.concatenate([stacked, s["below"][...]], 1))
    root = site_products(
        s["left8"], edge_left[8], cut, site(AHEAD), work, inverse_steps(lanes(second, 0))
    )
    s["root"][...] = root.astype(BF)
    near_copy = send("root", "root_near", 0, 1)
    far_copy = send("root", "root_far", 1, 1)
    s["far"][...] = lanes(second, 1).astype(BF)
    for copy, piece in zip(upper_copies, PIECES):
        copy.wait_recv()
        for leg in range(*piece):
            at = slice(leg * CHI, (leg + 1) * CHI)
            value = joined(s["terms_in"].at[UPPER, :, at], s["terms"].at[LOWER, :, at])
            if leg < 8:
                s["rows"][pl.ds(leg, CHI, stride=8), :] = value.astype(F32)
    v8 = s["rows"][...].astype(BF)
    v8t, v1t = v8.T, value.T
    moved_copies = []
    for piece in PIECES:
        s["moved"][:, columns(piece)] = last_product(v8t, v1t, work, piece).astype(BF)
        moved_copies.append(send("moved", "moved_in", 0, 1, piece))
    s["near"][...] = (dot(v8t, s["pair8"][...]) + dot(v1t, s["pair1"][...])).astype(BF)
    moved_near_copy = send("near", "near_in", 0, 1)
    moved_far_copy = send("far", "far_in", 0, 1)

    s["sites"][RIGHT] = site_form(ket, masks, RIGHT, s["ket_scr"])
    corner_t = corner_tr[...].T
    right8t, right1t = transposed_rows(lambda leg: dot_nt(corner_t, edge_top[leg]))
    site_products(
        leading(edge_right, s["rows_x"]),
        edge_right[8],
        flat_sketch(col_sketch[1], s["s_scr"]),
        site(RIGHT),
        work,
    )
    s["right"][...] = last_product(right8t, right1t, work, (0, D2)).astype(BF)
    right_copy = send("right", "right_next", 0, -1)
    for leg in range(D2):
        s["beside"][leg * CHI : (leg + 1) * CHI, :] = dot(corner_tr[...], edge_right[leg]).astype(BF)
    s["top8"][...] = leading(edge_top, s["rows"])
    s["top8t"][...] = s["top8"][...].T
    s["top1t"][...] = edge_top[8].T
    s["left_y"][...] = flat_sketch(col_sketch[0], s["s_scr"])

    for copy in (moved_near_copy, near_copy, far_copy):
        copy.wait_recv()
    above_root = s["root_far"][...]
    own_root = s["root_near"][...]
    corner_raw = dot(above_root, s["near_in"][...])
    corner_scale = factor_of(jnp.sum(corner_raw * corner_raw), CHI * CHI)
    corner_mid = corner_raw.T.astype(BF)
    for copy, piece in zip(moved_copies, PIECES):
        copy.wait_recv()
        edge_raw = turned(s["moved_in"], piece, above_root, own_root)
        s["edge_raw"][:, columns(piece)] = edge_raw
        side = dot(corner_mid, edge_raw.astype(BF))
        for leg in range(*piece):
            value = lanes(side, leg - piece[0])
            if leg < 8:
                s["rows"][pl.ds(leg, CHI, stride=8), :] = value
    s["pair8"][...] = s["rows"][...].astype(BF)
    s["pair1"][...] = value.astype(BF)
    site_products(s["pair8"], s["pair1"][...], s["left_y"][...], site(AHEAD), work)
    edge_raw = s["edge_raw"][...]
    edge_scale = factor_of(jnp.sum(edge_raw * edge_raw), CHI * WIDE)
    side_scale = edge_scale * corner_scale
    cut_copies = []
    for piece in PIECES:
        left_term = last_product(s["top8t"][...], s["top1t"][...], work, piece) * side_scale
        if not cut_copies:
            right_copy.wait_recv()
        s["cut"][:, columns(piece)] = (left_term + s["right_next"][:, columns(piece)].astype(F32)).astype(BF)
        cut_copies.append(send("cut", "cut_west", 0, 1, piece))

    cut = s["cut"][...]
    stacked = stack_legs(cut)
    second = dot_tn(stacked, jnp.concatenate([stacked, s["beside"][...]], 1))
    root = site_products(
        s["top8"], edge_top[8], cut, site(UPPER), work, inverse_steps(lanes(second, 0))
    )
    s["root_col"][...] = root.astype(BF)
    near_copy = send("root_col", "root_col_near", 1, 0)
    far_copy = send("root_col", "root_col_far", 1, 1)
    s["far_up"][...] = lanes(second, 1).astype(BF)
    raised_far_copy = send("far_up", "far_up_in", 1, 0)
    left_out[:, :WIDE] = (s["edge_raw"][...] * edge_scale).astype(BF)
    moved_far_copy.wait_recv()
    left_out[:, WIDE + CHI :] = rescale(dot(s["root_near"][...], s["far_in"][...])).astype(BF)
    left_out[:, WIDE : WIDE + CHI] = corner_mid
    for copy, piece in zip(cut_copies, PIECES):
        copy.wait_recv()
        for leg in range(*piece):
            value = s["cut_west"][:, leg * CHI : (leg + 1) * CHI]
            if leg < 8:
                s["rows"][pl.ds(leg, CHI, stride=8), :] = value.astype(F32)
    v8 = s["rows"][...].astype(BF)
    v8t, v1t = v8.T, value.T
    raised_copies = []
    for piece in PIECES:
        s["raised"][:, columns(piece)] = last_product(v8t, v1t, work, piece).astype(BF)
        raised_copies.append(send("raised", "raised_in", 1, 0, piece))
    first = (dot(v8t, s["pair8"][...]) + dot(v1t, s["pair1"][...])) * side_scale
    s["near_up"][...] = first.astype(BF)
    raised_near_copy = send("near_up", "near_up_in", 1, 0)

    for copy in (near_copy, far_copy, raised_far_copy):
        copy.wait_recv()
    west_root = s["root_col_far"][...]
    own_root = s["root_col_near"][...]
    top_out[:, WIDE + CHI :] = rescale(dot(own_root, s["far_up_in"][...])).astype(BF)
    parts = []
    for copy, piece in zip(raised_copies, PIECES):
        copy.wait_recv()
        parts.append(turned(s["raised_in"], piece, west_root, own_root))
    top_scale = factor_of(sum(jnp.sum(part * part) for part in parts), CHI * WIDE)
    for part, piece in zip(parts, PIECES):
        top_out[:, columns(piece)] = (part * top_scale).astype(BF)
    raised_near_copy.wait_recv()
    top_out[:, WIDE : WIDE + CHI] = rescale(dot(west_root, s["near_up_in"][...])).astype(BF)
    for copy in lower_copies + upper_copies + sent:
        copy.wait_send()


def result_kernel(left, top, edge_left, corner_bl, edge_top, corner_tl, corner_tr, sems):
    blocks = [(left, leg, edge_left.at[leg]) for leg in range(D2)]
    blocks += [(top, leg, edge_top.at[leg]) for leg in range(D2)]
    blocks += [(left, 10, corner_bl), (top, 9, corner_tl), (top, 10, corner_tr)]
    copies = [
        pltpu.make_async_copy(pack.at[:, n * CHI : (n + 1) * CHI], target, sems.at[index])
        for index, (pack, n, target) in enumerate(blocks)
    ]
    for copy in copies:
        copy.start()
    for copy in copies:
        copy.wait()


def local(*arrays):
    ket, corner_tl, corner_tr, corner_bl, *edges, row_sketch, col_sketch = [a.reshape(a.shape[2:]) for a in arrays]
    edges = [edge.transpose(1, 0, 2) for edge in edges]
    vmem = pl.BlockSpec(memory_space=pltpu.VMEM)
    hbm = pl.BlockSpec(memory_space=pltpu.HBM)
    operands = tuple(pltpu.with_memory_space_constraint(x, pltpu.HBM) for x in (ket, jnp.asarray(site_masks(), BF), edges[0], edges[3], corner_bl, row_sketch, edges[1], corner_tl, corner_tr, edges[2], col_sketch))
    packs = pl.pallas_call(
        move_kernel,
        out_shape=[jax.ShapeDtypeStruct(PACK, BF)] * 2,
        in_specs=[hbm] * len(operands),
        out_specs=[vmem] * 2,
        scratch_shapes=list(SCRATCH.values()),
        compiler_params=pltpu.CompilerParams(
            vmem_limit_bytes=44 << 20, collective_id=0, has_side_effects=True
        ),
        name="moves",
    )(*operands)
    edge = jax.ShapeDtypeStruct((D2, CHI, CHI), BF)
    square = jax.ShapeDtypeStruct((CHI, CHI), BF)
    left, corner_bl, top, corner_tl, corner_tr = pl.pallas_call(
        result_kernel,
        out_shape=[edge, square, edge, square, square],
        in_specs=[vmem] * 2,
        out_specs=[hbm] * 5,
        scratch_shapes=[pltpu.SemaphoreType.DMA((2 * D2 + 3,))],
        compiler_params=pltpu.CompilerParams(vmem_limit_bytes=4 << 20),
        name="results",
    )(*packs)
    results = (left.transpose(1, 0, 2), corner_bl, top.transpose(1, 0, 2), corner_tl, corner_tr)
    return tuple(value[None, None] for value in results)


def solution(mesh):
    four = P("row", "col", None, None)
    five = P("row", "col", None, None, None)
    return jax.shard_map(
        local,
        mesh=mesh,
        in_specs=(four, four, four, four, five, five, five, five, five, five),
        out_specs=(five, four, five, four, four),
        check_vma=False,
    )
```

```python
import numpy as np
import jax
import jax.numpy as jnp
from jax import lax
from jax.experimental import pallas as pl
from jax.experimental.pallas import tpu as pltpu
from jax.sharding import PartitionSpec as P

D = 3
D2 = 9
CHI = 128
NS_STEPS = 8
EPS = 1e-6
WIDE = D2 * CHI
BF = jnp.bfloat16
F32 = jnp.float32

FORMS = ((0, 1, 3, 2), (2, 1, 3, 0), (1, 0, 2, 3), (3, 0, 2, 1))
LOWER, UPPER, RIGHT, AHEAD = range(4)


def padded_legs():
    legs = [(-1, -1)] * 96
    for major in range(D2):
        for minor in range(8):
            legs[major * 8 + minor] = (major, minor)
        legs[72 + major] = (major, 8)
    return legs


def site_masks():
    legs = padded_legs()
    entry = np.stack(np.unravel_index(np.arange(81), (D,) * 4))
    masks = np.zeros((4, 2, 2, 96, 128), np.float32)
    for form, (out, v_leg, y_leg, x_leg) in enumerate(FORMS):
        for side, (major_leg, minor_leg) in enumerate(((out, v_leg), (y_leg, x_leg))):
            for row, (major, minor) in enumerate(legs):
                if major < 0:
                    continue
                for layer in range(2):
                    part = (lambda n: n // D) if layer == 0 else (lambda n: n % D)
                    fits = (entry[major_leg] == part(major)) & (entry[minor_leg] == part(minor))
                    masks[form, layer, side, row, :81] = fits
    return masks


def dot(a, b):
    return jnp.dot(a, b, preferred_element_type=F32)


def dot_nt(a, b):
    return lax.dot_general(a, b, (((1,), (1,)), ((), ())), preferred_element_type=F32)


def dot_tn(a, b):
    return lax.dot_general(a, b, (((0,), (0,)), ((), ())), preferred_element_type=F32)


def lanes(value, index):
    return value[:, index * CHI : (index + 1) * CHI]


def site_form(ket_ref, masks_ref, form, ket_scr):
    ket_scr[...] = jnp.zeros_like(ket_scr)
    ket_scr[0:2, 0:81] = ket_ref[...]
    ket = ket_scr[...]
    high = ket.astype(BF)
    rest = ket - high.astype(F32)
    mid = rest.astype(BF)
    low = (rest - mid.astype(F32)).astype(BF)
    layers = []
    for layer in range(2):
        rows = masks_ref[form, layer, 0]
        cols = masks_ref[form, layer, 1]
        left = []
        for s in range(2):
            left.append(
                jnp.concatenate(
                    [(rows.astype(F32) * part[s : s + 1].astype(F32)).astype(BF) for part in (high, mid, low)],
                    axis=1,
                )
            )
        layers.append(dot_nt(jnp.concatenate(left, 0), jnp.concatenate([cols] * 3, 1)))
    first, second = layers
    return (first[:96] * second[:96] + first[96:] * second[96:]).astype(BF)


def flat_sketch(sketch, scr):
    scr[...] = sketch.astype(F32)
    return jnp.concatenate([scr[pl.ds(r, CHI, stride=D2), :] for r in range(D2)], 1).astype(BF)


def to_rows(wide, scr):
    for leg in range(8):
        scr[pl.ds(leg, CHI, stride=8), :] = lanes(wide, leg)
    return scr[...].astype(BF), lanes(wide, 8).astype(BF)


def split(value):
    high = value.astype(BF)
    return high, (value - high.astype(F32)).astype(BF)


def product(a, b):
    a_high, a_low = split(a)
    b_high, b_low = split(b)
    return dot(jnp.concatenate([a_high, a_low], 1), jnp.concatenate([b_high, b_high], 0)) + dot(a_high, b_low)


def start_inverse(gram):
    rows = lax.broadcasted_iota(jnp.int32, (CHI, CHI), 0)
    cols = lax.broadcasted_iota(jnp.int32, (CHI, CHI), 1)
    identity = jnp.where(rows == cols, 1.0, 0.0).astype(F32)
    scaling = jnp.sum(gram * identity) + EPS
    return identity, gram * (1.0 / scaling), scaling


def inverse_steps(gram):
    identity, current, scaling = start_inverse(gram)
    factor = 1.5 * identity - 0.5 * current
    inverse = factor
    current = product(factor, current)
    yield None
    for step in range(1, NS_STEPS):
        factor = 1.5 * identity - 0.5 * product(inverse, current)
        yield None
        if step + 1 < NS_STEPS:
            both = product(factor, jnp.concatenate([current, inverse], 1))
            current, inverse = lanes(both, 0), lanes(both, 1)
            yield None
        else:
            inverse = product(factor, inverse)
    yield inverse * lax.rsqrt(jnp.full((1, 1), scaling, F32))


def rescale(value):
    mean = jnp.sum(value * value) * (1.0 / value.size)
    return value * lax.rsqrt(jnp.full((1, 1), mean + EPS, F32))


PAIRS = CHI // 2
PIECES = ((0, 5), (5, 9))


def site_pairs(start, count, site, work):
    zs, ws, zb, wb = work

    def pair(step, carry):
        at = start + step
        z = zb[pl.ds(pl.multiple_of(at * 16, 16), 16), :]
        tail = zs[pl.ds(pl.multiple_of(at * 48, 48), 48), :]
        cols = []
        for h in range(2):
            cols.append(
                jnp.concatenate(
                    [lanes(z, q)[h * 8 : h * 8 + 8] for q in range(D2)] + [tail[h * 24 : h * 24 + 24]], 0
                )
            )
        w = dot(site, jnp.concatenate(cols, 1).astype(BF))
        halves = [lanes(w, h) for h in range(2)]
        wide = [jnp.concatenate([half[e * 8 : e * 8 + 8] for e in range(D2)], 1) for half in halves]
        wb[pl.ds(pl.multiple_of(at * 16, 16), 16), :] = jnp.concatenate(wide, 0).astype(BF)
        ws[pl.ds(pl.multiple_of(at * 32, 32), 32), :] = jnp.concatenate([half[72:88] for half in halves], 0)
        return carry

    lax.fori_loop(0, count, pair, 0, unroll=True)


def site_products(x8, x1, y, site, work, beside=None):
    zs, _, zb, _ = work
    z_last = dot(x1, y)
    for q in range(D2):
        zs[pl.ds(q, CHI, stride=24), :] = lanes(z_last, q)
    if beside is None:
        zb[...] = dot(x8[...], y)
        site_pairs(0, PAIRS, site, work)
        return None
    found = None
    for part in range(4):
        found = next(beside, found)
        zb[part * 256 : part * 256 + 256, :] = dot(x8[part * 256 : part * 256 + 256, :], y)
    for start in range(0, PAIRS, 6):
        found = next(beside, found)
        site_pairs(start, min(6, PAIRS - start), site, work)
    return found


def last_product(v8t, v1t, work, piece):
    ws, wb = work[1], work[3]
    low, high = piece
    w_last = jnp.concatenate([ws[pl.ds(e, CHI, stride=16), :] for e in range(low, high)], 1).astype(BF)
    return dot(v8t, wb[:, low * CHI : high * CHI]) + dot(v1t, w_last)


def columns(piece):
    return slice(piece[0] * CHI, piece[1] * CHI)


def leading(edge, scr):
    for leg in range(8):
        scr[pl.ds(leg, CHI, stride=8), :] = edge[leg].astype(F32)
    return scr[...].astype(BF)


def joined(one, other):
    return (one[...].astype(F32) + other[...].astype(F32)).astype(BF)


def stack_legs(wide):
    return jnp.concatenate([lanes(wide, leg) for leg in range(D2)], 0)


def turned(raw, piece, left, right):
    legs = piece[1] - piece[0]
    stacked = jnp.concatenate([raw[:, leg * CHI : (leg + 1) * CHI] for leg in range(*piece)], 0)
    after = dot(stacked, right).astype(BF)
    return dot(left, jnp.concatenate([after[n * CHI : (n + 1) * CHI] for n in range(legs)], 1))


def factor_of(squares, size):
    return lax.rsqrt(jnp.full((1, 1), squares * (1.0 / size) + EPS, F32))


SQ = (CHI, CHI)
FL = (CHI, WIDE)
PACK = (CHI, WIDE + 2 * CHI)
TALL = (CHI * 8, CHI)
V = pltpu.VMEM
SENDS = 20
SCRATCH = dict(
    ket_scr=V((8, 128), F32),
    sites=V((4, 96, 96), BF),
    s_scr=V((WIDE, CHI), F32),
    rows=V(TALL, F32),
    rows_x=V(TALL, F32),
    last=V(SQ, F32),
    last_x=V(SQ, BF),
    zs=V((CHI * 24, CHI), F32),
    ws=V((CHI * 16, CHI), F32),
    zb=V((CHI * 8, WIDE), F32),
    wb=V((CHI * 8, WIDE), BF),
    left8=V(TALL, BF),
    left_y=V(FL, BF),
    pair8=V(TALL, BF),
    pair1=V(SQ, BF),
    below=V((WIDE, CHI), BF),
    beside=V((WIDE, CHI), BF),
    top8=V(TALL, BF),
    top8t=V((CHI, CHI * 8), BF),
    top1t=V(SQ, BF),
    terms=V((2, CHI, WIDE), BF),
    terms_in=V((2, CHI, WIDE), BF),
    root=V(SQ, BF),
    root_near=V(SQ, BF),
    root_far=V(SQ, BF),
    moved=V(FL, BF),
    moved_in=V(FL, BF),
    near=V(SQ, BF),
    near_in=V(SQ, BF),
    far=V(SQ, BF),
    far_in=V(SQ, BF),
    edge_raw=V(FL, F32),
    right=V(FL, BF),
    right_next=V(FL, BF),
    cut=V(FL, BF),
    cut_west=V(FL, BF),
    root_col=V(SQ, BF),
    root_col_near=V(SQ, BF),
    root_col_far=V(SQ, BF),
    raised=V(FL, BF),
    raised_in=V(FL, BF),
    near_up=V(SQ, BF),
    near_up_in=V(SQ, BF),
    far_up=V(SQ, BF),
    far_up_in=V(SQ, BF),
    ket=V((2, 81), F32),
    masks=V((4, 2, 2, 96, 128), BF),
    edge_left=V((D2, CHI, CHI), BF),
    edge_bottom=V((D2, CHI, CHI), BF),
    corner_bl=V(SQ, BF),
    row_sketch=V((2, WIDE, CHI), BF),
    edge_top=V((D2, CHI, CHI), BF),
    corner_tl=V(SQ, BF),
    corner_tr=V(SQ, BF),
    edge_right=V((D2, CHI, CHI), BF),
    col_sketch=V((2, WIDE, CHI), BF),
    in_sems=pltpu.SemaphoreType.DMA((11,)),
    send_sems=pltpu.SemaphoreType.DMA((SENDS,)),
    recv_sems=pltpu.SemaphoreType.DMA((SENDS,)),
)


INPUTS = (
    "ket",
    "masks",
    "edge_left",
    "edge_bottom",
    "corner_bl",
    "row_sketch",
    "edge_top",
    "corner_tl",
    "corner_tr",
    "edge_right",
    "col_sketch",
)


def move_kernel(*refs):
    sources, (left_out, top_out) = refs[: len(INPUTS)], refs[len(INPUTS) : len(INPUTS) + 2]
    s = dict(zip(SCRATCH, refs[len(INPUTS) + 2 :]))
    loads = {}
    for index, (name, source) in enumerate(zip(INPUTS, sources)):
        loads[name] = pltpu.make_async_copy(source, s[name], s["in_sems"].at[index])
        if index < 9:
            loads[name].start()
    ket, masks, edge_left, edge_bottom, corner_bl, row_sketch, edge_top, corner_tl, corner_tr, edge_right, col_sketch = [
        s[name] for name in INPUTS
    ]
    work = (s["zs"], s["ws"], s["zb"], s["wb"])
    row, col = lax.axis_index("row"), lax.axis_index("col")
    row_count, col_count = lax.axis_size("row"), lax.axis_size("col")

    def device(down, across):
        return {
            "row": lax.rem(row + (row_count + down), row_count),
            "col": lax.rem(col + (col_count + across), col_count),
        }

    barrier = pltpu.get_barrier_semaphore()
    for offset in ((-1, 0), (1, 0), (0, -1), (0, 1), (1, 1), (-1, -1)):
        pl.semaphore_signal(barrier, inc=1, device_id=device(*offset), device_id_type=pl.DeviceIdType.MESH)

    def remote(number, source, target, down, across):
        return pltpu.make_async_remote_copy(
            src_ref=source,
            dst_ref=target,
            send_sem=s["send_sems"].at[number],
            recv_sem=s["recv_sems"].at[number],
            device_id=device(down, across),
            device_id_type=pl.DeviceIdType.MESH,
        )

    sent = []

    def send(source, target, down, across, piece=None):
        source, target = s[source], s[target]
        if piece is not None:
            source, target = source.at[:, columns(piece)], target.at[:, columns(piece)]
        copy = remote(len(sent) + 4, source, target, down, across)
        copy.start()
        sent.append(copy)
        return copy

    def send_term(which, number):
        places = (which, slice(None), columns(PIECES[number]))
        return remote(
            2 * which + number, s["terms"].at[places], s["terms_in"].at[places], 2 * which - 1, 0
        )

    def site(form):
        return s["sites"][form, 0:88, :]

    def transposed_rows(wide_of):
        for leg in range(D2):
            value = wide_of(leg)
            if leg < 8:
                s["rows"][pl.ds(leg, CHI, stride=8), :] = value
        return s["rows"][...].astype(BF).T, value.astype(BF).T

    s["zs"][...] = jnp.zeros_like(s["zs"])
    for name in INPUTS[:2]:
        loads[name].wait()
    for name in INPUTS[9:]:
        loads[name].start()
    for form in (LOWER, UPPER):
        s["sites"][form] = site_form(ket, masks, form, s["ket_scr"])
    for name in INPUTS[2:8]:
        loads[name].wait()

    half = row_count // 2
    far = (lax.rem(row, half) + 1) // half

    def term(step, carry):
        which = lax.rem(step + far, 2)

        def operands(edge, corner, product_of):
            for leg in range(8):
                s["rows_x"][pl.ds(leg, CHI, stride=8), :] = edge[leg].astype(F32)
            s["last_x"][...] = edge[8]
            for leg in range(D2):
                value = product_of(corner, edge_left[leg])
                if leg < 8:
                    s["rows"][pl.ds(leg, CHI, stride=8), :] = value
            s["last"][...] = value

        @pl.when(which == LOWER)
        def _():
            operands(edge_bottom, corner_bl[...].T, dot_nt)

        @pl.when(which == UPPER)
        def _():
            operands(edge_top, corner_tl[...], dot)

        site_products(
            s["rows_x"][...].astype(BF),
            s["last_x"][...],
            flat_sketch(row_sketch[1 - which], s["s_scr"]),
            s["sites"][which][0:88],
            work,
        )
        v8t = s["rows"][...].astype(BF).T
        v1t = s["last"][...].astype(BF).T
        for number, piece in enumerate(PIECES):
            s["terms"][which, :, columns(piece)] = last_product(v8t, v1t, work, piece).astype(BF)
            if number == 0:

                @pl.when(step == 0)
                def _():
                    pl.semaphore_wait(barrier, 6)

            send_term(which, number).start()
        return carry

    lax.fori_loop(0, 2, term, 0)
    lower_copies = [send_term(LOWER, number) for number in range(2)]
    upper_copies = [send_term(UPPER, number) for number in range(2)]
    for name in INPUTS[8:]:
        loads[name].wait()
    s["left8"][...] = leading(edge_left, s["rows"])
    for leg in range(D2):
        s["below"][leg * CHI : (leg + 1) * CHI, :] = dot(corner_bl[...], edge_bottom[leg]).astype(BF)
    corner_t = corner_tl[...].T
    for leg in range(D2):
        value = dot(corner_t, edge_top[leg])
        if leg < 8:
            s["rows_x"][pl.ds(leg, CHI, stride=8), :] = value
    s["pair8"][...] = s["rows_x"][...].astype(BF)
    s["pair1"][...] = value.astype(BF)
    s["sites"][AHEAD] = site_form(ket, masks, AHEAD, s["ket_scr"])

    for copy in lower_copies:
        copy.wait_recv()
    cut = joined(s["terms"].at[UPPER], s["terms_in"].at[LOWER])
    stacked = stack_legs(cut)
    second = dot_tn(stacked, jnp.concatenate([stacked, s["below"][...]], 1))
    root = site_products(
        s["left8"], edge_left[8], cut, site(AHEAD), work, inverse_steps(lanes(second, 0))
    )
    s["root"][...] = root.astype(BF)
    near_copy = send("root", "root_near", 0, 1)
    far_copy = send("root", "root_far", 1, 1)
    s["far"][...] = lanes(second, 1).astype(BF)
    for copy, piece in zip(upper_copies, PIECES):
        copy.wait_recv()
        for leg in range(*piece):
            at = slice(leg * CHI, (leg + 1) * CHI)
            value = joined(s["terms_in"].at[UPPER, :, at], s["terms"].at[LOWER, :, at])
            if leg < 8:
                s["rows"][pl.ds(leg, CHI, stride=8), :] = value.astype(F32)
    v8 = s["rows"][...].astype(BF)
    v8t, v1t = v8.T, value.T
    moved_copies = []
    for piece in PIECES:
        s["moved"][:, columns(piece)] = last_product(v8t, v1t, work, piece).astype(BF)
        moved_copies.append(send("moved", "moved_in", 0, 1, piece))
        if len(moved_copies) == 1:
            s["near"][...] = (dot(v8t, s["pair8"][...]) + dot(v1t, s["pair1"][...])).astype(BF)
            moved_near_copy = send("near", "near_in", 0, 1)

    s["sites"][RIGHT] = site_form(ket, masks, RIGHT, s["ket_scr"])
    corner_t = corner_tr[...].T
    right8t, right1t = transposed_rows(lambda leg: dot_nt(corner_t, edge_top[leg]))
    site_products(
        leading(edge_right, s["rows_x"]),
        edge_right[8],
        flat_sketch(col_sketch[1], s["s_scr"]),
        site(RIGHT),
        work,
    )
    s["right"][...] = last_product(right8t, right1t, work, (0, D2)).astype(BF)
    right_copy = send("right", "right_next", 0, -1)
    for leg in range(D2):
        s["beside"][leg * CHI : (leg + 1) * CHI, :] = dot(corner_tr[...], edge_right[leg]).astype(BF)
    s["top8"][...] = leading(edge_top, s["rows"])
    s["top8t"][...] = s["top8"][...].T
    s["top1t"][...] = edge_top[8].T
    s["left_y"][...] = flat_sketch(col_sketch[0], s["s_scr"])

    for copy in (moved_near_copy, near_copy, far_copy):
        copy.wait_recv()
    above_root = s["root_far"][...]
    own_root = s["root_near"][...]
    corner_raw = dot(above_root, s["near_in"][...])
    corner_scale = factor_of(jnp.sum(corner_raw * corner_raw), CHI * CHI)
    corner_mid = corner_raw.T.astype(BF)
    for copy, piece in zip(moved_copies, PIECES):
        copy.wait_recv()
        if piece == PIECES[-1]:
            moved_far_copy = send("far", "far_in", 0, 1)
        edge_raw = turned(s["moved_in"], piece, above_root, own_root)
        s["edge_raw"][:, columns(piece)] = edge_raw
        side = dot(corner_mid, edge_raw.astype(BF))
        for leg in range(*piece):
            value = lanes(side, leg - piece[0])
            if leg < 8:
                s["rows"][pl.ds(leg, CHI, stride=8), :] = value
    s["pair8"][...] = s["rows"][...].astype(BF)
    s["pair1"][...] = value.astype(BF)
    site_products(s["pair8"], s["pair1"][...], s["left_y"][...], site(AHEAD), work)
    edge_raw = s["edge_raw"][...]
    edge_scale = factor_of(jnp.sum(edge_raw * edge_raw), CHI * WIDE)
    side_scale = edge_scale * corner_scale
    cut_copies = []
    for piece in PIECES:
        left_term = last_product(s["top8t"][...], s["top1t"][...], work, piece) * side_scale
        if not cut_copies:
            right_copy.wait_recv()
        s["cut"][:, columns(piece)] = (left_term + s["right_next"][:, columns(piece)].astype(F32)).astype(BF)
        cut_copies.append(send("cut", "cut_west", 0, 1, piece))

    cut = s["cut"][...]
    stacked = stack_legs(cut)
    second = dot_tn(stacked, jnp.concatenate([stacked, s["beside"][...]], 1))
    root = site_products(
        s["top8"], edge_top[8], cut, site(UPPER), work, inverse_steps(lanes(second, 0))
    )
    s["root_col"][...] = root.astype(BF)
    near_copy = send("root_col", "root_col_near", 1, 0)
    far_copy = send("root_col", "root_col_far", 1, 1)
    s["far_up"][...] = lanes(second, 1).astype(BF)
    raised_far_copy = send("far_up", "far_up_in", 1, 0)
    left_out[:, :WIDE] = (s["edge_raw"][...] * edge_scale).astype(BF)
    moved_far_copy.wait_recv()
    left_out[:, WIDE + CHI :] = rescale(dot(s["root_near"][...], s["far_in"][...])).astype(BF)
    left_out[:, WIDE : WIDE + CHI] = corner_mid
    for copy, piece in zip(cut_copies, PIECES):
        copy.wait_recv()
        for leg in range(*piece):
            value = s["cut_west"][:, leg * CHI : (leg + 1) * CHI]
            if leg < 8:
                s["rows"][pl.ds(leg, CHI, stride=8), :] = value.astype(F32)
    v8 = s["rows"][...].astype(BF)
    v8t, v1t = v8.T, value.T
    raised_copies = []
    for piece in PIECES:
        s["raised"][:, columns(piece)] = last_product(v8t, v1t, work, piece).astype(BF)
        raised_copies.append(send("raised", "raised_in", 1, 0, piece))
        if len(raised_copies) == 1:
            first = (dot(v8t, s["pair8"][...]) + dot(v1t, s["pair1"][...])) * side_scale
            s["near_up"][...] = first.astype(BF)
            raised_near_copy = send("near_up", "near_up_in", 1, 0)

    for copy in (near_copy, far_copy, raised_far_copy):
        copy.wait_recv()
    west_root = s["root_col_far"][...]
    own_root = s["root_col_near"][...]
    top_out[:, WIDE + CHI :] = rescale(dot(own_root, s["far_up_in"][...])).astype(BF)
    raised_near_copy.wait_recv()
    top_out[:, WIDE : WIDE + CHI] = rescale(dot(west_root, s["near_up_in"][...])).astype(BF)
    parts = []
    for copy, piece in zip(raised_copies, PIECES):
        copy.wait_recv()
        parts.append(turned(s["raised_in"], piece, west_root, own_root))
    top_scale = factor_of(sum(jnp.sum(part * part) for part in parts), CHI * WIDE)
    for part, piece in zip(parts, PIECES):
        top_out[:, columns(piece)] = (part * top_scale).astype(BF)
    for copy in lower_copies + upper_copies + sent:
        copy.wait_send()


def result_kernel(left, top, edge_left, corner_bl, edge_top, corner_tl, corner_tr, sems):
    blocks = [(left, leg, edge_left.at[leg]) for leg in range(D2)]
    blocks += [(top, leg, edge_top.at[leg]) for leg in range(D2)]
    blocks += [(left, 10, corner_bl), (top, 9, corner_tl), (top, 10, corner_tr)]
    copies = [
        pltpu.make_async_copy(pack.at[:, n * CHI : (n + 1) * CHI], target, sems.at[index])
        for index, (pack, n, target) in enumerate(blocks)
    ]
    for copy in copies:
        copy.start()
    for copy in copies:
        copy.wait()


def local(*arrays):
    ket, corner_tl, corner_tr, corner_bl, *edges, row_sketch, col_sketch = [a.reshape(a.shape[2:]) for a in arrays]
    edges = [edge.transpose(1, 0, 2) for edge in edges]
    vmem = pl.BlockSpec(memory_space=pltpu.VMEM)
    hbm = pl.BlockSpec(memory_space=pltpu.HBM)
    operands = tuple(pltpu.with_memory_space_constraint(x, pltpu.HBM) for x in (ket, jnp.asarray(site_masks(), BF), edges[0], edges[3], corner_bl, row_sketch, edges[1], corner_tl, corner_tr, edges[2], col_sketch))
    packs = pl.pallas_call(
        move_kernel,
        out_shape=[jax.ShapeDtypeStruct(PACK, BF)] * 2,
        in_specs=[hbm] * len(operands),
        out_specs=[vmem] * 2,
        scratch_shapes=list(SCRATCH.values()),
        compiler_params=pltpu.CompilerParams(
            vmem_limit_bytes=44 << 20, collective_id=0, has_side_effects=True
        ),
        name="moves",
    )(*operands)
    edge = jax.ShapeDtypeStruct((D2, CHI, CHI), BF)
    square = jax.ShapeDtypeStruct((CHI, CHI), BF)
    left, corner_bl, top, corner_tl, corner_tr = pl.pallas_call(
        result_kernel,
        out_shape=[edge, square, edge, square, square],
        in_specs=[vmem] * 2,
        out_specs=[hbm] * 5,
        scratch_shapes=[pltpu.SemaphoreType.DMA((2 * D2 + 3,))],
        compiler_params=pltpu.CompilerParams(vmem_limit_bytes=4 << 20),
        name="results",
    )(*packs)
    results = (left.transpose(1, 0, 2), corner_bl, top.transpose(1, 0, 2), corner_tl, corner_tr)
    return tuple(value[None, None] for value in results)


def solution(mesh):
    four = P("row", "col", None, None)
    five = P("row", "col", None, None, None)
    return jax.shard_map(
        local,
        mesh=mesh,
        in_specs=(four, four, four, four, five, five, five, five, five, five),
        out_specs=(five, four, five, four, four),
        check_vma=False,
    )
```

```python
import numpy as np
import jax
import jax.numpy as jnp
from jax import lax
from jax.experimental import pallas as pl
from jax.experimental.pallas import tpu as pltpu
from jax.sharding import PartitionSpec as P

D = 3
D2 = 9
CHI = 128
NS_STEPS = 8
EPS = 1e-6
WIDE = D2 * CHI
BF = jnp.bfloat16
F32 = jnp.float32

FORMS = ((0, 1, 3, 2), (2, 1, 3, 0), (1, 0, 2, 3), (3, 0, 2, 1))
LOWER, UPPER, RIGHT, AHEAD = range(4)


def padded_legs():
    legs = [(-1, -1)] * 96
    for major in range(D2):
        for minor in range(8):
            legs[major * 8 + minor] = (major, minor)
        legs[72 + major] = (major, 8)
    return legs


def site_masks():
    legs = padded_legs()
    entry = np.stack(np.unravel_index(np.arange(81), (D,) * 4))
    masks = np.zeros((4, 2, 2, 96, 128), np.float32)
    for form, (out, v_leg, y_leg, x_leg) in enumerate(FORMS):
        for side, (major_leg, minor_leg) in enumerate(((out, v_leg), (y_leg, x_leg))):
            for row, (major, minor) in enumerate(legs):
                if major < 0:
                    continue
                for layer in range(2):
                    part = (lambda n: n // D) if layer == 0 else (lambda n: n % D)
                    fits = (entry[major_leg] == part(major)) & (entry[minor_leg] == part(minor))
                    masks[form, layer, side, row, :81] = fits
    return masks


def dot(a, b):
    return jnp.dot(a, b, preferred_element_type=F32)


def dot_nt(a, b):
    return lax.dot_general(a, b, (((1,), (1,)), ((), ())), preferred_element_type=F32)


def dot_tn(a, b):
    return lax.dot_general(a, b, (((0,), (0,)), ((), ())), preferred_element_type=F32)


def lanes(value, index):
    return value[:, index * CHI : (index + 1) * CHI]


def site_form(ket_ref, masks_ref, form, ket_scr):
    ket_scr[...] = jnp.zeros_like(ket_scr)
    ket_scr[0:2, 0:81] = ket_ref[...]
    ket = ket_scr[...]
    high = ket.astype(BF)
    rest = ket - high.astype(F32)
    mid = rest.astype(BF)
    low = (rest - mid.astype(F32)).astype(BF)
    layers = []
    for layer in range(2):
        rows = masks_ref[form, layer, 0]
        cols = masks_ref[form, layer, 1]
        left = []
        for s in range(2):
            left.append(
                jnp.concatenate(
                    [(rows.astype(F32) * part[s : s + 1].astype(F32)).astype(BF) for part in (high, mid, low)],
                    axis=1,
                )
            )
        layers.append(dot_nt(jnp.concatenate(left, 0), jnp.concatenate([cols] * 3, 1)))
    first, second = layers
    return (first[:96] * second[:96] + first[96:] * second[96:]).astype(BF)


def flat_sketch(sketch, scr):
    scr[...] = sketch.astype(F32)
    return jnp.concatenate([scr[pl.ds(r, CHI, stride=D2), :] for r in range(D2)], 1).astype(BF)


def to_rows(wide, scr):
    for leg in range(8):
        scr[pl.ds(leg, CHI, stride=8), :] = lanes(wide, leg)
    return scr[...].astype(BF), lanes(wide, 8).astype(BF)


def split(value):
    high = value.astype(BF)
    return high, (value - high.astype(F32)).astype(BF)


def product(a, b):
    a_high, a_low = split(a)
    b_high, b_low = split(b)
    return dot(jnp.concatenate([a_high, a_low], 1), jnp.concatenate([b_high, b_high], 0)) + dot(a_high, b_low)


def start_inverse(gram):
    rows = lax.broadcasted_iota(jnp.int32, (CHI, CHI), 0)
    cols = lax.broadcasted_iota(jnp.int32, (CHI, CHI), 1)
    identity = jnp.where(rows == cols, 1.0, 0.0).astype(F32)
    scaling = jnp.sum(gram * identity) + EPS
    return identity, gram * (1.0 / scaling), scaling


def inverse_steps(gram):
    identity, current, scaling = start_inverse(gram)
    factor = 1.5 * identity - 0.5 * current
    inverse = factor
    current = product(factor, current)
    yield None
    for step in range(1, NS_STEPS):
        factor = 1.5 * identity - 0.5 * product(inverse, current)
        yield None
        if step + 1 < NS_STEPS:
            both = product(factor, jnp.concatenate([current, inverse], 1))
            current, inverse = lanes(both, 0), lanes(both, 1)
            yield None
        else:
            inverse = product(factor, inverse)
    yield inverse * lax.rsqrt(jnp.full((1, 1), scaling, F32))


def rescale(value):
    mean = jnp.sum(value * value) * (1.0 / value.size)
    return value * lax.rsqrt(jnp.full((1, 1), mean + EPS, F32))


PAIRS = CHI // 2
PIECES = ((0, 2), (2, 6), (6, 9))


def site_pairs(start, count, site, work):
    zs, ws, zb, wb = work

    def pair(step, carry):
        at = start + step
        z = zb[pl.ds(pl.multiple_of(at * 16, 16), 16), :]
        tail = zs[pl.ds(pl.multiple_of(at * 48, 48), 48), :]
        cols = []
        for h in range(2):
            cols.append(
                jnp.concatenate(
                    [lanes(z, q)[h * 8 : h * 8 + 8] for q in range(D2)] + [tail[h * 24 : h * 24 + 24]], 0
                )
            )
        w = dot(site, jnp.concatenate(cols, 1).astype(BF))
        halves = [lanes(w, h) for h in range(2)]
        wide = [jnp.concatenate([half[e * 8 : e * 8 + 8] for e in range(D2)], 1) for half in halves]
        wb[pl.ds(pl.multiple_of(at * 16, 16), 16), :] = jnp.concatenate(wide, 0).astype(BF)
        ws[pl.ds(pl.multiple_of(at * 32, 32), 32), :] = jnp.concatenate([half[72:88] for half in halves], 0)
        return carry

    lax.fori_loop(0, count, pair, 0, unroll=True)


def site_products(x8, x1, y, site, work, beside=None):
    zs, _, zb, _ = work
    z_last = dot(x1, y)
    for q in range(D2):
        zs[pl.ds(q, CHI, stride=24), :] = lanes(z_last, q)
    if beside is None:
        zb[...] = dot(x8[...], y)
        site_pairs(0, PAIRS, site, work)
        return None
    found = None
    for part in range(4):
        found = next(beside, found)
        zb[part * 256 : part * 256 + 256, :] = dot(x8[part * 256 : part * 256 + 256, :], y)
    for start in range(0, PAIRS, 6):
        found = next(beside, found)
        site_pairs(start, min(6, PAIRS - start), site, work)
    return found


def last_product(v8t, v1t, work, piece):
    ws, wb = work[1], work[3]
    low, high = piece
    w_last = jnp.concatenate([ws[pl.ds(e, CHI, stride=16), :] for e in range(low, high)], 1).astype(BF)
    return dot(v8t, wb[:, low * CHI : high * CHI]) + dot(v1t, w_last)


def columns(piece):
    return slice(piece[0] * CHI, piece[1] * CHI)


def leading(edge, scr):
    for leg in range(8):
        scr[pl.ds(leg, CHI, stride=8), :] = edge[leg].astype(F32)
    return scr[...].astype(BF)


def joined(one, other):
    return (one[...].astype(F32) + other[...].astype(F32)).astype(BF)


def stack_legs(wide):
    return jnp.concatenate([lanes(wide, leg) for leg in range(D2)], 0)


def turned(raw, piece, left, right):
    legs = piece[1] - piece[0]
    stacked = jnp.concatenate([raw[:, leg * CHI : (leg + 1) * CHI] for leg in range(*piece)], 0)
    after = dot(stacked, right).astype(BF)
    return dot(left, jnp.concatenate([after[n * CHI : (n + 1) * CHI] for n in range(legs)], 1))


def factor_of(squares, size):
    return lax.rsqrt(jnp.full((1, 1), squares * (1.0 / size) + EPS, F32))


SQ = (CHI, CHI)
FL = (CHI, WIDE)
PACK = (CHI, WIDE + 2 * CHI)
TALL = (CHI * 8, CHI)
V = pltpu.VMEM
SENDS = 26
SCRATCH = dict(
    ket_scr=V((8, 128), F32),
    sites=V((4, 96, 96), BF),
    s_scr=V((WIDE, CHI), F32),
    rows=V(TALL, F32),
    rows_x=V(TALL, F32),
    corner_a=V((2, CHI, CHI), BF),
    edge_b=V((2, D2, CHI, CHI), BF),
    edges=V((2, D2, CHI, CHI), BF),
    zs=V((CHI * 24, CHI), F32),
    ws=V((CHI * 16, CHI), F32),
    zb=V((CHI * 8, WIDE), F32),
    wb=V((CHI * 8, WIDE), BF),
    left8=V(TALL, BF),
    left_y=V(FL, BF),
    pair8=V(TALL, BF),
    pair1=V(SQ, BF),
    below=V((WIDE, CHI), BF),
    beside=V((WIDE, CHI), BF),
    top8=V(TALL, BF),
    top8t=V((CHI, CHI * 8), BF),
    top1t=V(SQ, BF),
    terms=V((2, CHI, WIDE), BF),
    terms_in=V((2, CHI, WIDE), BF),
    root=V(SQ, BF),
    root_near=V(SQ, BF),
    root_far=V(SQ, BF),
    moved=V(FL, BF),
    moved_in=V(FL, BF),
    near=V(SQ, BF),
    near_in=V(SQ, BF),
    far=V(SQ, BF),
    far_in=V(SQ, BF),
    edge_raw=V(FL, F32),
    right=V(FL, BF),
    right_next=V(FL, BF),
    cut=V(FL, BF),
    cut_west=V(FL, BF),
    root_col=V(SQ, BF),
    root_col_near=V(SQ, BF),
    root_col_far=V(SQ, BF),
    raised=V(FL, BF),
    raised_in=V(FL, BF),
    near_up=V(SQ, BF),
    near_up_in=V(SQ, BF),
    far_up=V(SQ, BF),
    far_up_in=V(SQ, BF),
    ket=V((2, 81), F32),
    masks=V((4, 2, 2, 96, 128), BF),
    corner_bl=V(SQ, BF),
    row_sketch=V((2, WIDE, CHI), BF),
    corner_tl=V(SQ, BF),
    corner_tr=V(SQ, BF),
    edge_right=V((D2, CHI, CHI), BF),
    col_sketch=V((2, WIDE, CHI), BF),
    in_sems=pltpu.SemaphoreType.DMA((11,)),
    send_sems=pltpu.SemaphoreType.DMA((SENDS,)),
    recv_sems=pltpu.SemaphoreType.DMA((SENDS,)),
)


INPUTS = (
    "ket",
    "masks",
    "edge_left",
    "edge_bottom",
    "corner_bl",
    "row_sketch",
    "edge_top",
    "corner_tl",
    "corner_tr",
    "edge_right",
    "col_sketch",
)


def move_kernel(*refs):
    sources, (left_out, top_out) = refs[: len(INPUTS)], refs[len(INPUTS) : len(INPUTS) + 2]
    s = dict(zip(SCRATCH, refs[len(INPUTS) + 2 :]))
    held = {name: s[name] for name in INPUTS if name in s}
    held["edge_left"] = s["edge_b"].at[LOWER]
    held["edge_bottom"] = s["edges"].at[LOWER]
    held["edge_top"] = s["edges"].at[UPPER]
    loads = {}
    for index, (name, source) in enumerate(zip(INPUTS, sources)):
        loads[name] = pltpu.make_async_copy(source, held[name], s["in_sems"].at[index])
        if index < 9:
            loads[name].start()
    ket, masks, edge_left, edge_bottom, corner_bl, row_sketch, edge_top, corner_tl, corner_tr, edge_right, col_sketch = [
        held[name] for name in INPUTS
    ]
    work = (s["zs"], s["ws"], s["zb"], s["wb"])
    row, col = lax.axis_index("row"), lax.axis_index("col")
    row_count, col_count = lax.axis_size("row"), lax.axis_size("col")

    def device(down, across):
        return {
            "row": lax.rem(row + (row_count + down), row_count),
            "col": lax.rem(col + (col_count + across), col_count),
        }

    barrier = pltpu.get_barrier_semaphore()
    for offset in ((-1, 0), (1, 0), (0, -1), (0, 1), (1, 1), (-1, -1)):
        pl.semaphore_signal(barrier, inc=1, device_id=device(*offset), device_id_type=pl.DeviceIdType.MESH)

    def remote(number, source, target, down, across):
        return pltpu.make_async_remote_copy(
            src_ref=source,
            dst_ref=target,
            send_sem=s["send_sems"].at[number],
            recv_sem=s["recv_sems"].at[number],
            device_id=device(down, across),
            device_id_type=pl.DeviceIdType.MESH,
        )

    sent = []

    def send(source, target, down, across, piece=None):
        source, target = s[source], s[target]
        if piece is not None:
            source, target = source.at[:, columns(piece)], target.at[:, columns(piece)]
        copy = remote(len(sent) + 2 * len(PIECES), source, target, down, across)
        copy.start()
        sent.append(copy)
        return copy

    def send_term(which, number):
        places = (which, slice(None), columns(PIECES[number]))
        return remote(
            len(PIECES) * which + number, s["terms"].at[places], s["terms_in"].at[places], 2 * which - 1, 0
        )

    def site(form):
        return s["sites"][form, 0:88, :]

    def transposed_rows(wide_of):
        for leg in range(D2):
            value = wide_of(leg)
            if leg < 8:
                s["rows"][pl.ds(leg, CHI, stride=8), :] = value
        return s["rows"][...].astype(BF).T, value.astype(BF).T

    s["zs"][...] = jnp.zeros_like(s["zs"])
    for name in INPUTS[:2]:
        loads[name].wait()
    for name in INPUTS[9:]:
        loads[name].start()
    for form in (LOWER, UPPER):
        s["sites"][form] = site_form(ket, masks, form, s["ket_scr"])
    for name in INPUTS[2:8]:
        loads[name].wait()
    s["corner_a"][LOWER] = corner_bl[...].T
    s["corner_a"][UPPER] = corner_tl[...]
    for leg in range(D2):
        s["edge_b"][UPPER, leg] = edge_left[leg].T

    half = row_count // 2
    far = (lax.rem(row, half) + 1) // half

    def term(step, carry):
        which = lax.rem(step + far, 2)

        corner = s["corner_a"][which]
        for leg in range(D2):
            value = dot_nt(corner, s["edge_b"][which, leg])
            if leg < 8:
                s["rows_x"][pl.ds(leg, CHI, stride=8), :] = s["edges"][which, leg].astype(F32)
                s["rows"][pl.ds(leg, CHI, stride=8), :] = value
        v1t = value.astype(BF).T
        site_products(
            s["rows_x"][...].astype(BF),
            s["edges"][which, 8],
            flat_sketch(row_sketch[1 - which], s["s_scr"]),
            s["sites"][which][0:88],
            work,
        )
        v8t = s["rows"][...].astype(BF).T
        for number, piece in enumerate(PIECES):
            s["terms"][which, :, columns(piece)] = last_product(v8t, v1t, work, piece).astype(BF)
            if number == 0:

                @pl.when(step == 0)
                def _():
                    pl.semaphore_wait(barrier, 6)

            send_term(which, number).start()
        return carry

    lax.fori_loop(0, 2, term, 0)
    lower_copies = [send_term(LOWER, number) for number in range(len(PIECES))]
    upper_copies = [send_term(UPPER, number) for number in range(len(PIECES))]
    for name in INPUTS[8:]:
        loads[name].wait()
    s["left8"][...] = leading(edge_left, s["rows"])
    for leg in range(D2):
        s["below"][leg * CHI : (leg + 1) * CHI, :] = dot(corner_bl[...], edge_bottom[leg]).astype(BF)
    corner_t = corner_tl[...].T
    for leg in range(D2):
        value = dot(corner_t, edge_top[leg])
        if leg < 8:
            s["rows_x"][pl.ds(leg, CHI, stride=8), :] = value
    s["pair8"][...] = s["rows_x"][...].astype(BF)
    s["pair1"][...] = value.astype(BF)
    s["sites"][AHEAD] = site_form(ket, masks, AHEAD, s["ket_scr"])

    for copy in lower_copies:
        copy.wait_recv()
    cut = joined(s["terms"].at[UPPER], s["terms_in"].at[LOWER])
    stacked = stack_legs(cut)
    second = dot_tn(stacked, jnp.concatenate([stacked, s["below"][...]], 1))
    root = site_products(
        s["left8"], edge_left[8], cut, site(AHEAD), work, inverse_steps(lanes(second, 0))
    )
    s["root"][...] = root.astype(BF)
    near_copy = send("root", "root_near", 0, 1)
    far_copy = send("root", "root_far", 1, 1)
    s["far"][...] = lanes(second, 1).astype(BF)
    for copy, piece in zip(upper_copies, PIECES):
        copy.wait_recv()
        for leg in range(*piece):
            at = slice(leg * CHI, (leg + 1) * CHI)
            value = joined(s["terms_in"].at[UPPER, :, at], s["terms"].at[LOWER, :, at])
            if leg < 8:
                s["rows"][pl.ds(leg, CHI, stride=8), :] = value.astype(F32)
    v8 = s["rows"][...].astype(BF)
    v8t, v1t = v8.T, value.T
    moved_copies = []
    for piece in PIECES:
        s["moved"][:, columns(piece)] = last_product(v8t, v1t, work, piece).astype(BF)
        moved_copies.append(send("moved", "moved_in", 0, 1, piece))
        if len(moved_copies) == 1:
            s["near"][...] = (dot(v8t, s["pair8"][...]) + dot(v1t, s["pair1"][...])).astype(BF)
            moved_near_copy = send("near", "near_in", 0, 1)

    s["sites"][RIGHT] = site_form(ket, masks, RIGHT, s["ket_scr"])
    corner_t = corner_tr[...].T
    right8t, right1t = transposed_rows(lambda leg: dot_nt(corner_t, edge_top[leg]))
    site_products(
        leading(edge_right, s["rows_x"]),
        edge_right[8],
        flat_sketch(col_sketch[1], s["s_scr"]),
        site(RIGHT),
        work,
    )
    s["right"][...] = last_product(right8t, right1t, work, (0, D2)).astype(BF)
    right_copy = send("right", "right_next", 0, -1)
    for leg in range(D2):
        s["beside"][leg * CHI : (leg + 1) * CHI, :] = dot(corner_tr[...], edge_right[leg]).astype(BF)
    s["top8"][...] = leading(edge_top, s["rows"])
    s["top8t"][...] = s["top8"][...].T
    s["top1t"][...] = edge_top[8].T
    s["left_y"][...] = flat_sketch(col_sketch[0], s["s_scr"])

    for copy in (moved_near_copy, near_copy, far_copy):
        copy.wait_recv()
    above_root = s["root_far"][...]
    own_root = s["root_near"][...]
    corner_raw = dot(above_root, s["near_in"][...])
    corner_scale = factor_of(jnp.sum(corner_raw * corner_raw), CHI * CHI)
    corner_mid = corner_raw.T.astype(BF)
    for copy, piece in zip(moved_copies, PIECES):
        copy.wait_recv()
        if piece == PIECES[-1]:
            moved_far_copy = send("far", "far_in", 0, 1)
        edge_raw = turned(s["moved_in"], piece, above_root, own_root)
        s["edge_raw"][:, columns(piece)] = edge_raw
        side = dot(corner_mid, edge_raw.astype(BF))
        for leg in range(*piece):
            value = lanes(side, leg - piece[0])
            if leg < 8:
                s["rows"][pl.ds(leg, CHI, stride=8), :] = value
    s["pair8"][...] = s["rows"][...].astype(BF)
    s["pair1"][...] = value.astype(BF)
    site_products(s["pair8"], s["pair1"][...], s["left_y"][...], site(AHEAD), work)
    edge_raw = s["edge_raw"][...]
    edge_scale = factor_of(jnp.sum(edge_raw * edge_raw), CHI * WIDE)
    side_scale = edge_scale * corner_scale
    cut_copies = []
    for piece in PIECES:
        left_term = last_product(s["top8t"][...], s["top1t"][...], work, piece) * side_scale
        if not cut_copies:
            right_copy.wait_recv()
        s["cut"][:, columns(piece)] = (left_term + s["right_next"][:, columns(piece)].astype(F32)).astype(BF)
        cut_copies.append(send("cut", "cut_west", 0, 1, piece))

    cut = s["cut"][...]
    stacked = stack_legs(cut)
    second = dot_tn(stacked, jnp.concatenate([stacked, s["beside"][...]], 1))
    root = site_products(
        s["top8"], edge_top[8], cut, site(UPPER), work, inverse_steps(lanes(second, 0))
    )
    s["root_col"][...] = root.astype(BF)
    near_copy = send("root_col", "root_col_near", 1, 0)
    far_copy = send("root_col", "root_col_far", 1, 1)
    s["far_up"][...] = lanes(second, 1).astype(BF)
    raised_far_copy = send("far_up", "far_up_in", 1, 0)
    left_out[:, :WIDE] = (s["edge_raw"][...] * edge_scale).astype(BF)
    moved_far_copy.wait_recv()
    left_out[:, WIDE + CHI :] = rescale(dot(s["root_near"][...], s["far_in"][...])).astype(BF)
    left_out[:, WIDE : WIDE + CHI] = corner_mid
    for copy, piece in zip(cut_copies, PIECES):
        copy.wait_recv()
        for leg in range(*piece):
            value = s["cut_west"][:, leg * CHI : (leg + 1) * CHI]
            if leg < 8:
                s["rows"][pl.ds(leg, CHI, stride=8), :] = value.astype(F32)
    v8 = s["rows"][...].astype(BF)
    v8t, v1t = v8.T, value.T
    raised_copies = []
    for piece in PIECES:
        s["raised"][:, columns(piece)] = last_product(v8t, v1t, work, piece).astype(BF)
        raised_copies.append(send("raised", "raised_in", 1, 0, piece))
        if len(raised_copies) == 1:
            first = (dot(v8t, s["pair8"][...]) + dot(v1t, s["pair1"][...])) * side_scale
            s["near_up"][...] = first.astype(BF)
            raised_near_copy = send("near_up", "near_up_in", 1, 0)

    for copy in (near_copy, far_copy, raised_far_copy):
        copy.wait_recv()
    west_root = s["root_col_far"][...]
    own_root = s["root_col_near"][...]
    top_out[:, WIDE + CHI :] = rescale(dot(own_root, s["far_up_in"][...])).astype(BF)
    raised_near_copy.wait_recv()
    top_out[:, WIDE : WIDE + CHI] = rescale(dot(west_root, s["near_up_in"][...])).astype(BF)
    parts = []
    for copy, piece in zip(raised_copies, PIECES):
        copy.wait_recv()
        parts.append(turned(s["raised_in"], piece, west_root, own_root))
    top_scale = factor_of(sum(jnp.sum(part * part) for part in parts), CHI * WIDE)
    for part, piece in zip(parts, PIECES):
        top_out[:, columns(piece)] = (part * top_scale).astype(BF)
    for copy in lower_copies + upper_copies + sent:
        copy.wait_send()


def result_kernel(left, top, edge_left, corner_bl, edge_top, corner_tl, corner_tr, sems):
    blocks = [(left, leg, edge_left.at[leg]) for leg in range(D2)]
    blocks += [(top, leg, edge_top.at[leg]) for leg in range(D2)]
    blocks += [(left, 10, corner_bl), (top, 9, corner_tl), (top, 10, corner_tr)]
    copies = [
        pltpu.make_async_copy(pack.at[:, n * CHI : (n + 1) * CHI], target, sems.at[index])
        for index, (pack, n, target) in enumerate(blocks)
    ]
    for copy in copies:
        copy.start()
    for copy in copies:
        copy.wait()


def local(*arrays):
    ket, corner_tl, corner_tr, corner_bl, *edges, row_sketch, col_sketch = [a.reshape(a.shape[2:]) for a in arrays]
    edges = [edge.transpose(1, 0, 2) for edge in edges]
    vmem = pl.BlockSpec(memory_space=pltpu.VMEM)
    hbm = pl.BlockSpec(memory_space=pltpu.HBM)
    operands = tuple(pltpu.with_memory_space_constraint(x, pltpu.HBM) for x in (ket, jnp.asarray(site_masks(), BF), edges[0], edges[3], corner_bl, row_sketch, edges[1], corner_tl, corner_tr, edges[2], col_sketch))
    packs = pl.pallas_call(
        move_kernel,
        out_shape=[jax.ShapeDtypeStruct(PACK, BF)] * 2,
        in_specs=[hbm] * len(operands),
        out_specs=[vmem] * 2,
        scratch_shapes=list(SCRATCH.values()),
        compiler_params=pltpu.CompilerParams(
            vmem_limit_bytes=44 << 20, collective_id=0, has_side_effects=True
        ),
        name="moves",
    )(*operands)
    edge = jax.ShapeDtypeStruct((D2, CHI, CHI), BF)
    square = jax.ShapeDtypeStruct((CHI, CHI), BF)
    left, corner_bl, top, corner_tl, corner_tr = pl.pallas_call(
        result_kernel,
        out_shape=[edge, square, edge, square, square],
        in_specs=[vmem] * 2,
        out_specs=[hbm] * 5,
        scratch_shapes=[pltpu.SemaphoreType.DMA((2 * D2 + 3,))],
        compiler_params=pltpu.CompilerParams(vmem_limit_bytes=4 << 20),
        name="results",
    )(*packs)
    results = (left.transpose(1, 0, 2), corner_bl, top.transpose(1, 0, 2), corner_tl, corner_tr)
    return tuple(value[None, None] for value in results)


def solution(mesh):
    four = P("row", "col", None, None)
    five = P("row", "col", None, None, None)
    return jax.shard_map(
        local,
        mesh=mesh,
        in_specs=(four, four, four, four, five, five, five, five, five, five),
        out_specs=(five, four, five, four, four),
        check_vma=False,
    )
```

```python
import numpy as np
import jax
import jax.numpy as jnp
from jax import lax
from jax.experimental import pallas as pl
from jax.experimental.pallas import tpu as pltpu
from jax.sharding import PartitionSpec as P

D = 3
D2 = 9
CHI = 128
NS_STEPS = 8
EPS = 1e-6
WIDE = D2 * CHI
BF = jnp.bfloat16
F32 = jnp.float32

FORMS = ((0, 1, 3, 2), (2, 1, 3, 0), (1, 0, 2, 3), (3, 0, 2, 1))
LOWER, UPPER, RIGHT, AHEAD = range(4)


def padded_legs():
    legs = [(-1, -1)] * 96
    for major in range(D2):
        for minor in range(8):
            legs[major * 8 + minor] = (major, minor)
        legs[72 + major] = (major, 8)
    return legs


def site_masks():
    legs = padded_legs()
    entry = np.stack(np.unravel_index(np.arange(81), (D,) * 4))
    masks = np.zeros((4, 2, 2, 96, 128), np.float32)
    for form, (out, v_leg, y_leg, x_leg) in enumerate(FORMS):
        for side, (major_leg, minor_leg) in enumerate(((out, v_leg), (y_leg, x_leg))):
            for row, (major, minor) in enumerate(legs):
                if major < 0:
                    continue
                for layer in range(2):
                    part = (lambda n: n // D) if layer == 0 else (lambda n: n % D)
                    fits = (entry[major_leg] == part(major)) & (entry[minor_leg] == part(minor))
                    masks[form, layer, side, row, :81] = fits
    return masks


def dot(a, b):
    return jnp.dot(a, b, preferred_element_type=F32)


def dot_nt(a, b):
    return lax.dot_general(a, b, (((1,), (1,)), ((), ())), preferred_element_type=F32)


def dot_tn(a, b):
    return lax.dot_general(a, b, (((0,), (0,)), ((), ())), preferred_element_type=F32)


def lanes(value, index):
    return value[:, index * CHI : (index + 1) * CHI]


def site_form(ket_ref, masks_ref, form, ket_scr):
    ket_scr[...] = jnp.zeros_like(ket_scr)
    ket_scr[0:2, 0:81] = ket_ref[...]
    ket = ket_scr[...]
    high = ket.astype(BF)
    rest = ket - high.astype(F32)
    mid = rest.astype(BF)
    low = (rest - mid.astype(F32)).astype(BF)
    layers = []
    for layer in range(2):
        rows = masks_ref[form, layer, 0]
        cols = masks_ref[form, layer, 1]
        left = []
        for s in range(2):
            left.append(
                jnp.concatenate(
                    [(rows.astype(F32) * part[s : s + 1].astype(F32)).astype(BF) for part in (high, mid, low)],
                    axis=1,
                )
            )
        layers.append(dot_nt(jnp.concatenate(left, 0), jnp.concatenate([cols] * 3, 1)))
    first, second = layers
    return (first[:96] * second[:96] + first[96:] * second[96:]).astype(BF)


def flat_sketch(sketch, scr):
    scr[...] = sketch.astype(F32)
    return jnp.concatenate([scr[pl.ds(r, CHI, stride=D2), :] for r in range(D2)], 1).astype(BF)


def to_rows(wide, scr):
    for leg in range(8):
        scr[pl.ds(leg, CHI, stride=8), :] = lanes(wide, leg)
    return scr[...].astype(BF), lanes(wide, 8).astype(BF)


def split(value):
    high = value.astype(BF)
    return high, (value - high.astype(F32)).astype(BF)


def product(a, b):
    a_high, a_low = split(a)
    b_high, b_low = split(b)
    return dot(jnp.concatenate([a_high, a_low], 1), jnp.concatenate([b_high, b_high], 0)) + dot(a_high, b_low)


def start_inverse(gram):
    rows = lax.broadcasted_iota(jnp.int32, (CHI, CHI), 0)
    cols = lax.broadcasted_iota(jnp.int32, (CHI, CHI), 1)
    identity = jnp.where(rows == cols, 1.0, 0.0).astype(F32)
    scaling = jnp.sum(gram * identity) + EPS
    return identity, gram * (1.0 / scaling), scaling


def inverse_steps(gram):
    identity, current, scaling = start_inverse(gram)
    factor = 1.5 * identity - 0.5 * current
    inverse = factor
    current = product(factor, current)
    yield None
    for step in range(1, NS_STEPS):
        factor = 1.5 * identity - 0.5 * product(inverse, current)
        yield None
        if step + 1 < NS_STEPS:
            both = product(factor, jnp.concatenate([current, inverse], 1))
            current, inverse = lanes(both, 0), lanes(both, 1)
            yield None
        else:
            inverse = product(factor, inverse)
    yield inverse * lax.rsqrt(jnp.full((1, 1), scaling, F32))


def rescale(value):
    mean = jnp.sum(value * value) * (1.0 / value.size)
    return value * lax.rsqrt(jnp.full((1, 1), mean + EPS, F32))


PAIRS = CHI // 2
PIECES = ((0, 5), (5, 9))


def site_pairs(start, count, site, work):
    zs, ws, zb, wb = work

    def pair(step, carry):
        at = start + step
        z = zb[pl.ds(pl.multiple_of(at * 16, 16), 16), :]
        tail = zs[pl.ds(pl.multiple_of(at * 48, 48), 48), :]
        cols = []
        for h in range(2):
            cols.append(
                jnp.concatenate(
                    [lanes(z, q)[h * 8 : h * 8 + 8] for q in range(D2)] + [tail[h * 24 : h * 24 + 24]], 0
                )
            )
        w = dot(site, jnp.concatenate(cols, 1).astype(BF))
        halves = [lanes(w, h) for h in range(2)]
        wide = [jnp.concatenate([half[e * 8 : e * 8 + 8] for e in range(D2)], 1) for half in halves]
        wb[pl.ds(pl.multiple_of(at * 16, 16), 16), :] = jnp.concatenate(wide, 0).astype(BF)
        ws[pl.ds(pl.multiple_of(at * 32, 32), 32), :] = jnp.concatenate([half[72:88] for half in halves], 0)
        return carry

    lax.fori_loop(0, count, pair, 0, unroll=True)


def site_products(x8, x1, y, site, work, beside=None):
    zs, _, zb, _ = work
    z_last = dot(x1, y)
    for q in range(D2):
        zs[pl.ds(q, CHI, stride=24), :] = lanes(z_last, q)
    if beside is None:
        zb[...] = dot(x8[...], y)
        site_pairs(0, PAIRS, site, work)
        return None
    found = None
    for part in range(4):
        found = next(beside, found)
        zb[part * 256 : part * 256 + 256, :] = dot(x8[part * 256 : part * 256 + 256, :], y)
    for start in range(0, PAIRS, 6):
        found = next(beside, found)
        site_pairs(start, min(6, PAIRS - start), site, work)
    return found


def last_product(v8t, v1t, work, piece):
    ws, wb = work[1], work[3]
    low, high = piece
    w_last = jnp.concatenate([ws[pl.ds(e, CHI, stride=16), :] for e in range(low, high)], 1).astype(BF)
    return dot(v8t, wb[:, low * CHI : high * CHI]) + dot(v1t, w_last)


def columns(piece):
    return slice(piece[0] * CHI, piece[1] * CHI)


def leading(edge, scr):
    for leg in range(8):
        scr[pl.ds(leg, CHI, stride=8), :] = edge[leg].astype(F32)
    return scr[...].astype(BF)


def joined(one, other):
    return (one[...].astype(F32) + other[...].astype(F32)).astype(BF)


def stack_legs(wide):
    return jnp.concatenate([lanes(wide, leg) for leg in range(D2)], 0)


def turned(raw, piece, left, right):
    legs = piece[1] - piece[0]
    stacked = jnp.concatenate([raw[:, leg * CHI : (leg + 1) * CHI] for leg in range(*piece)], 0)
    after = dot(stacked, right).astype(BF)
    return dot(left, jnp.concatenate([after[n * CHI : (n + 1) * CHI] for n in range(legs)], 1))


def factor_of(squares, size):
    return lax.rsqrt(jnp.full((1, 1), squares * (1.0 / size) + EPS, F32))


SQ = (CHI, CHI)
FL = (CHI, WIDE)
PACK = (CHI, WIDE + 2 * CHI)
TALL = (CHI * 8, CHI)
V = pltpu.VMEM
FIRST_SEND = 2 * len(PIECES)
SENDS = 20
SCRATCH = dict(
    ket_scr=V((8, 128), F32),
    sites=V((4, 96, 96), BF),
    s_scr=V((WIDE, CHI), F32),
    rows=V(TALL, F32),
    rows_x=V(TALL, F32),
    last=V(SQ, F32),
    last_x=V(SQ, BF),
    zs=V((CHI * 24, CHI), F32),
    ws=V((CHI * 16, CHI), F32),
    zb=V((CHI * 8, WIDE), F32),
    wb=V((CHI * 8, WIDE), BF),
    left8=V(TALL, BF),
    left_y=V(FL, BF),
    pair8=V(TALL, BF),
    pair1=V(SQ, BF),
    below=V((WIDE, CHI), BF),
    beside=V((WIDE, CHI), BF),
    top8=V(TALL, BF),
    top8t=V((CHI, CHI * 8), BF),
    top1t=V(SQ, BF),
    terms=V((2, CHI, WIDE), BF),
    terms_in=V((2, CHI, WIDE), BF),
    root=V(SQ, BF),
    root_near=V(SQ, BF),
    root_far=V(SQ, BF),
    moved=V(FL, BF),
    moved_in=V(FL, BF),
    near=V(SQ, BF),
    near_in=V(SQ, BF),
    far=V(SQ, BF),
    far_in=V(SQ, BF),
    edge_raw=V(FL, F32),
    right=V(FL, BF),
    right_next=V(FL, BF),
    cut=V(FL, BF),
    cut_west=V(FL, BF),
    root_col=V(SQ, BF),
    root_col_near=V(SQ, BF),
    root_col_far=V(SQ, BF),
    raised=V(FL, BF),
    raised_in=V(FL, BF),
    near_up=V(SQ, BF),
    near_up_in=V(SQ, BF),
    far_up=V(SQ, BF),
    far_up_in=V(SQ, BF),
    ket=V((2, 81), F32),
    masks=V((4, 2, 2, 96, 128), BF),
    edge_left=V((D2, CHI, CHI), BF),
    edge_bottom=V((D2, CHI, CHI), BF),
    corner_bl=V(SQ, BF),
    row_sketch=V((2, WIDE, CHI), BF),
    edge_top=V((D2, CHI, CHI), BF),
    corner_tl=V(SQ, BF),
    corner_tr=V(SQ, BF),
    edge_right=V((D2, CHI, CHI), BF),
    col_sketch=V((2, WIDE, CHI), BF),
    in_sems=pltpu.SemaphoreType.DMA((11,)),
    send_sems=pltpu.SemaphoreType.DMA((SENDS,)),
    recv_sems=pltpu.SemaphoreType.DMA((SENDS,)),
)


INPUTS = (
    "ket",
    "masks",
    "edge_left",
    "edge_bottom",
    "corner_bl",
    "row_sketch",
    "edge_top",
    "corner_tl",
    "corner_tr",
    "edge_right",
    "col_sketch",
)


def move_kernel(*refs):
    sources, (left_out, top_out) = refs[: len(INPUTS)], refs[len(INPUTS) : len(INPUTS) + 2]
    s = dict(zip(SCRATCH, refs[len(INPUTS) + 2 :]))
    loads = {}
    for index, (name, source) in enumerate(zip(INPUTS, sources)):
        loads[name] = pltpu.make_async_copy(source, s[name], s["in_sems"].at[index])
        if index < 9:
            loads[name].start()
    ket, masks, edge_left, edge_bottom, corner_bl, row_sketch, edge_top, corner_tl, corner_tr, edge_right, col_sketch = [
        s[name] for name in INPUTS
    ]
    work = (s["zs"], s["ws"], s["zb"], s["wb"])
    row, col = lax.axis_index("row"), lax.axis_index("col")
    row_count, col_count = lax.axis_size("row"), lax.axis_size("col")

    def device(down, across):
        return {
            "row": lax.rem(row + (row_count + down), row_count),
            "col": lax.rem(col + (col_count + across), col_count),
        }

    barrier = pltpu.get_barrier_semaphore()
    for offset in ((-1, 0), (1, 0), (0, -1), (0, 1), (1, 1), (-1, -1)):
        pl.semaphore_signal(barrier, inc=1, device_id=device(*offset), device_id_type=pl.DeviceIdType.MESH)

    def remote(number, source, target, down, across):
        return pltpu.make_async_remote_copy(
            src_ref=source,
            dst_ref=target,
            send_sem=s["send_sems"].at[number],
            recv_sem=s["recv_sems"].at[number],
            device_id=device(down, across),
            device_id_type=pl.DeviceIdType.MESH,
        )

    sent = []

    def send(source, target, down, across, piece=None):
        source, target = s[source], s[target]
        if piece is not None:
            source, target = source.at[:, columns(piece)], target.at[:, columns(piece)]
        copy = remote(len(sent) + FIRST_SEND, source, target, down, across)
        copy.start()
        sent.append(copy)
        return copy

    def send_term(which, number):
        places = (which, slice(None), columns(PIECES[number]))
        return remote(
            2 * which + number, s["terms"].at[places], s["terms_in"].at[places], 2 * which - 1, 0
        )

    def site(form):
        return s["sites"][form, 0:88, :]

    def transposed_rows(wide_of):
        for leg in range(D2):
            value = wide_of(leg)
            if leg < 8:
                s["rows"][pl.ds(leg, CHI, stride=8), :] = value
        return s["rows"][...].astype(BF).T, value.astype(BF).T

    s["zs"][...] = jnp.zeros_like(s["zs"])
    for name in INPUTS[:2]:
        loads[name].wait()
    for name in INPUTS[9:]:
        loads[name].start()
    for form in (LOWER, UPPER):
        s["sites"][form] = site_form(ket, masks, form, s["ket_scr"])
    for name in INPUTS[2:8]:
        loads[name].wait()

    half = row_count // 2
    far = (lax.rem(row, half) + 1) // half
    patient = (lax.rem(row + 1, half) + 1) // half

    def term(step, carry):
        which = lax.rem(step + far, 2)

        def operands(edge, corner, product_of):
            for leg in range(8):
                s["rows_x"][pl.ds(leg, CHI, stride=8), :] = edge[leg].astype(F32)
            s["last_x"][...] = edge[8]
            for leg in range(D2):
                value = product_of(corner, edge_left[leg])
                if leg < 8:
                    s["rows"][pl.ds(leg, CHI, stride=8), :] = value
            s["last"][...] = value

        @pl.when(which == LOWER)
        def _():
            operands(edge_bottom, corner_bl[...].T, dot_nt)

        @pl.when(which == UPPER)
        def _():
            operands(edge_top, corner_tl[...], dot)

        site_products(
            s["rows_x"][...].astype(BF),
            s["last_x"][...],
            flat_sketch(row_sketch[1 - which], s["s_scr"]),
            s["sites"][which][0:88],
            work,
        )
        v8t = s["rows"][...].astype(BF).T
        v1t = s["last"][...].astype(BF).T
        for number, piece in enumerate(PIECES):
            s["terms"][which, :, columns(piece)] = last_product(v8t, v1t, work, piece).astype(BF)
            if number == 0:

                @pl.when(step == 0)
                def _():
                    pl.semaphore_wait(barrier, 6)

            send_term(which, number).start()
        return carry

    lax.fori_loop(0, 2, term, 0)
    lower_copies = [send_term(LOWER, number) for number in range(2)]
    upper_copies = [send_term(UPPER, number) for number in range(2)]
    for name in INPUTS[8:]:
        loads[name].wait()
    s["left8"][...] = leading(edge_left, s["rows"])
    for leg in range(D2):
        s["below"][leg * CHI : (leg + 1) * CHI, :] = dot(corner_bl[...], edge_bottom[leg]).astype(BF)
    corner_t = corner_tl[...].T
    for leg in range(D2):
        value = dot(corner_t, edge_top[leg])
        if leg < 8:
            s["rows_x"][pl.ds(leg, CHI, stride=8), :] = value
    s["pair8"][...] = s["rows_x"][...].astype(BF)
    s["pair1"][...] = value.astype(BF)
    s["sites"][AHEAD] = site_form(ket, masks, AHEAD, s["ket_scr"])

    for copy in lower_copies:
        copy.wait_recv()
    cut = joined(s["terms"].at[UPPER], s["terms_in"].at[LOWER])
    stacked = stack_legs(cut)
    second = dot_tn(stacked, jnp.concatenate([stacked, s["below"][...]], 1))
    root = site_products(
        s["left8"], edge_left[8], cut, site(AHEAD), work, inverse_steps(lanes(second, 0))
    )
    s["root"][...] = root.astype(BF)
    near_copy = send("root", "root_near", 0, 1)
    far_copy = send("root", "root_far", 1, 1)
    s["far"][...] = lanes(second, 1).astype(BF)
    for copy, piece in zip(upper_copies, PIECES):
        copy.wait_recv()
        for leg in range(*piece):
            at = slice(leg * CHI, (leg + 1) * CHI)
            value = joined(s["terms_in"].at[UPPER, :, at], s["terms"].at[LOWER, :, at])
            if leg < 8:
                s["rows"][pl.ds(leg, CHI, stride=8), :] = value.astype(F32)
    v8 = s["rows"][...].astype(BF)
    v8t, v1t = v8.T, value.T
    moved_copies = []
    for piece in PIECES:
        s["moved"][:, columns(piece)] = last_product(v8t, v1t, work, piece).astype(BF)
        moved_copies.append(send("moved", "moved_in", 0, 1, piece))
        if len(moved_copies) == 1:
            s["near"][...] = (dot(v8t, s["pair8"][...]) + dot(v1t, s["pair1"][...])).astype(BF)
            moved_near_copy = send("near", "near_in", 0, 1)

    s["sites"][RIGHT] = site_form(ket, masks, RIGHT, s["ket_scr"])
    corner_t = corner_tr[...].T
    right8t, right1t = transposed_rows(lambda leg: dot_nt(corner_t, edge_top[leg]))
    site_products(
        leading(edge_right, s["rows_x"]),
        edge_right[8],
        flat_sketch(col_sketch[1], s["s_scr"]),
        site(RIGHT),
        work,
    )
    s["right"][...] = last_product(right8t, right1t, work, (0, D2)).astype(BF)
    right_copy = send("right", "right_next", 0, -1)
    for leg in range(D2):
        s["beside"][leg * CHI : (leg + 1) * CHI, :] = dot(corner_tr[...], edge_right[leg]).astype(BF)
    s["top8"][...] = leading(edge_top, s["rows"])
    s["top8t"][...] = s["top8"][...].T
    s["top1t"][...] = edge_top[8].T
    s["left_y"][...] = flat_sketch(col_sketch[0], s["s_scr"])

    for copy in (moved_near_copy, near_copy, far_copy):
        copy.wait_recv()
    above_root = s["root_far"][...]
    own_root = s["root_near"][...]
    corner_raw = dot(above_root, s["near_in"][...])
    corner_scale = factor_of(jnp.sum(corner_raw * corner_raw), CHI * CHI)
    corner_mid = corner_raw.T.astype(BF)
    for copy, piece in zip(moved_copies, PIECES):
        copy.wait_recv()
        if piece == PIECES[-1]:
            moved_far_copy = send("far", "far_in", 0, 1)
        edge_raw = turned(s["moved_in"], piece, above_root, own_root)
        s["edge_raw"][:, columns(piece)] = edge_raw
        side = dot(corner_mid, edge_raw.astype(BF))
        for leg in range(*piece):
            value = lanes(side, leg - piece[0])
            if leg < 8:
                s["rows"][pl.ds(leg, CHI, stride=8), :] = value
    s["pair8"][...] = s["rows"][...].astype(BF)
    s["pair1"][...] = value.astype(BF)
    site_products(s["pair8"], s["pair1"][...], s["left_y"][...], site(AHEAD), work)
    edge_raw = s["edge_raw"][...]
    edge_scale = factor_of(jnp.sum(edge_raw * edge_raw), CHI * WIDE)
    side_scale = edge_scale * corner_scale
    cut_copies = []
    for piece in PIECES:
        left_term = last_product(s["top8t"][...], s["top1t"][...], work, piece) * side_scale
        if not cut_copies:
            right_copy.wait_recv()
        s["cut"][:, columns(piece)] = (left_term + s["right_next"][:, columns(piece)].astype(F32)).astype(BF)
        cut_copies.append(
            remote(
                len(sent) + FIRST_SEND,
                s["cut"].at[:, columns(piece)],
                s["cut_west"].at[:, columns(piece)],
                0,
                1,
            )
        )
        sent.append(cut_copies[-1])

        @pl.when(patient == 0)
        def _():
            cut_copies[-1].start()


    cut = s["cut"][...]
    stacked = stack_legs(cut)
    second = dot_tn(stacked, jnp.concatenate([stacked, s["beside"][...]], 1))
    root = site_products(
        s["top8"], edge_top[8], cut, site(UPPER), work, inverse_steps(lanes(second, 0))
    )
    @pl.when(patient == 1)
    def _():
        for copy in cut_copies:
            copy.start()

    s["root_col"][...] = root.astype(BF)
    near_copy = send("root_col", "root_col_near", 1, 0)
    far_copy = send("root_col", "root_col_far", 1, 1)
    s["far_up"][...] = lanes(second, 1).astype(BF)
    raised_far_copy = send("far_up", "far_up_in", 1, 0)
    left_out[:, :WIDE] = (s["edge_raw"][...] * edge_scale).astype(BF)
    moved_far_copy.wait_recv()
    left_out[:, WIDE + CHI :] = rescale(dot(s["root_near"][...], s["far_in"][...])).astype(BF)
    left_out[:, WIDE : WIDE + CHI] = corner_mid
    for copy, piece in zip(cut_copies, PIECES):
        copy.wait_recv()
        for leg in range(*piece):
            value = s["cut_west"][:, leg * CHI : (leg + 1) * CHI]
            if leg < 8:
                s["rows"][pl.ds(leg, CHI, stride=8), :] = value.astype(F32)
    v8 = s["rows"][...].astype(BF)
    v8t, v1t = v8.T, value.T
    raised_copies = []
    for piece in PIECES:
        s["raised"][:, columns(piece)] = last_product(v8t, v1t, work, piece).astype(BF)
        raised_copies.append(send("raised", "raised_in", 1, 0, piece))
        if len(raised_copies) == 1:
            first = (dot(v8t, s["pair8"][...]) + dot(v1t, s["pair1"][...])) * side_scale
            s["near_up"][...] = first.astype(BF)
            raised_near_copy = send("near_up", "near_up_in", 1, 0)

    for copy in (near_copy, far_copy, raised_far_copy):
        copy.wait_recv()
    west_root = s["root_col_far"][...]
    own_root = s["root_col_near"][...]
    top_out[:, WIDE + CHI :] = rescale(dot(own_root, s["far_up_in"][...])).astype(BF)
    raised_near_copy.wait_recv()
    top_out[:, WIDE : WIDE + CHI] = rescale(dot(west_root, s["near_up_in"][...])).astype(BF)
    parts = []
    for copy, piece in zip(raised_copies, PIECES):
        copy.wait_recv()
        parts.append(turned(s["raised_in"], piece, west_root, own_root))
    top_scale = factor_of(sum(jnp.sum(part * part) for part in parts), CHI * WIDE)
    for part, piece in zip(parts, PIECES):
        top_out[:, columns(piece)] = (part * top_scale).astype(BF)
    for copy in lower_copies + upper_copies + sent:
        copy.wait_send()


def result_kernel(left, top, edge_left, corner_bl, edge_top, corner_tl, corner_tr, sems):
    blocks = [(left, leg, edge_left.at[leg]) for leg in range(D2)]
    blocks += [(top, leg, edge_top.at[leg]) for leg in range(D2)]
    blocks += [(left, 10, corner_bl), (top, 9, corner_tl), (top, 10, corner_tr)]
    copies = [
        pltpu.make_async_copy(pack.at[:, n * CHI : (n + 1) * CHI], target, sems.at[index])
        for index, (pack, n, target) in enumerate(blocks)
    ]
    for copy in copies:
        copy.start()
    for copy in copies:
        copy.wait()


def local(*arrays):
    ket, corner_tl, corner_tr, corner_bl, *edges, row_sketch, col_sketch = [a.reshape(a.shape[2:]) for a in arrays]
    edges = [edge.transpose(1, 0, 2) for edge in edges]
    vmem = pl.BlockSpec(memory_space=pltpu.VMEM)
    hbm = pl.BlockSpec(memory_space=pltpu.HBM)
    operands = tuple(pltpu.with_memory_space_constraint(x, pltpu.HBM) for x in (ket, jnp.asarray(site_masks(), BF), edges[0], edges[3], corner_bl, row_sketch, edges[1], corner_tl, corner_tr, edges[2], col_sketch))
    packs = pl.pallas_call(
        move_kernel,
        out_shape=[jax.ShapeDtypeStruct(PACK, BF)] * 2,
        in_specs=[hbm] * len(operands),
        out_specs=[vmem] * 2,
        scratch_shapes=list(SCRATCH.values()),
        compiler_params=pltpu.CompilerParams(
            vmem_limit_bytes=44 << 20, collective_id=0, has_side_effects=True
        ),
        name="moves",
    )(*operands)
    edge = jax.ShapeDtypeStruct((D2, CHI, CHI), BF)
    square = jax.ShapeDtypeStruct((CHI, CHI), BF)
    left, corner_bl, top, corner_tl, corner_tr = pl.pallas_call(
        result_kernel,
        out_shape=[edge, square, edge, square, square],
        in_specs=[vmem] * 2,
        out_specs=[hbm] * 5,
        scratch_shapes=[pltpu.SemaphoreType.DMA((2 * D2 + 3,))],
        compiler_params=pltpu.CompilerParams(vmem_limit_bytes=4 << 20),
        name="results",
    )(*packs)
    results = (left.transpose(1, 0, 2), corner_bl, top.transpose(1, 0, 2), corner_tl, corner_tr)
    return tuple(value[None, None] for value in results)


def solution(mesh):
    four = P("row", "col", None, None)
    five = P("row", "col", None, None, None)
    return jax.shard_map(
        local,
        mesh=mesh,
        in_specs=(four, four, four, four, five, five, five, five, five, five),
        out_specs=(five, four, five, four, four),
        check_vma=False,
    )
```

```python
import numpy as np
import jax
import jax.numpy as jnp
from jax import lax
from jax.experimental import pallas as pl
from jax.experimental.pallas import tpu as pltpu
from jax.sharding import PartitionSpec as P

D = 3
D2 = 9
CHI = 128
NS_STEPS = 8
EPS = 1e-6
WIDE = D2 * CHI
BF = jnp.bfloat16
F32 = jnp.float32

FORMS = ((0, 1, 3, 2), (2, 1, 3, 0), (1, 0, 2, 3), (3, 0, 2, 1))
LOWER, UPPER, RIGHT, AHEAD = range(4)


def padded_legs():
    legs = [(-1, -1)] * 96
    for major in range(D2):
        for minor in range(8):
            legs[major * 8 + minor] = (major, minor)
        legs[72 + major] = (major, 8)
    return legs


def site_masks():
    legs = padded_legs()
    entry = np.stack(np.unravel_index(np.arange(81), (D,) * 4))
    masks = np.zeros((4, 2, 2, 96, 128), np.float32)
    for form, (out, v_leg, y_leg, x_leg) in enumerate(FORMS):
        for side, (major_leg, minor_leg) in enumerate(((out, v_leg), (y_leg, x_leg))):
            for row, (major, minor) in enumerate(legs):
                if major < 0:
                    continue
                for layer in range(2):
                    part = (lambda n: n // D) if layer == 0 else (lambda n: n % D)
                    fits = (entry[major_leg] == part(major)) & (entry[minor_leg] == part(minor))
                    masks[form, layer, side, row, :81] = fits
    return masks


def dot(a, b):
    return jnp.dot(a, b, preferred_element_type=F32)


def dot_nt(a, b):
    return lax.dot_general(a, b, (((1,), (1,)), ((), ())), preferred_element_type=F32)


def dot_tn(a, b):
    return lax.dot_general(a, b, (((0,), (0,)), ((), ())), preferred_element_type=F32)


def lanes(value, index):
    return value[:, index * CHI : (index + 1) * CHI]


def site_form(ket_ref, masks_ref, form, ket_scr):
    ket_scr[...] = jnp.zeros_like(ket_scr)
    ket_scr[0:2, 0:81] = ket_ref[...]
    ket = ket_scr[...]
    high = ket.astype(BF)
    rest = ket - high.astype(F32)
    mid = rest.astype(BF)
    low = (rest - mid.astype(F32)).astype(BF)
    layers = []
    for layer in range(2):
        rows = masks_ref[form, layer, 0]
        cols = masks_ref[form, layer, 1]
        left = []
        for s in range(2):
            left.append(
                jnp.concatenate(
                    [(rows.astype(F32) * part[s : s + 1].astype(F32)).astype(BF) for part in (high, mid, low)],
                    axis=1,
                )
            )
        layers.append(dot_nt(jnp.concatenate(left, 0), jnp.concatenate([cols] * 3, 1)))
    first, second = layers
    return (first[:96] * second[:96] + first[96:] * second[96:]).astype(BF)


def flat_sketch(sketch, scr):
    scr[...] = sketch.astype(F32)
    return jnp.concatenate([scr[pl.ds(r, CHI, stride=D2), :] for r in range(D2)], 1).astype(BF)


def to_rows(wide, scr):
    for leg in range(8):
        scr[pl.ds(leg, CHI, stride=8), :] = lanes(wide, leg)
    return scr[...].astype(BF), lanes(wide, 8).astype(BF)


def split(value):
    high = value.astype(BF)
    return high, (value - high.astype(F32)).astype(BF)


def product(a, b):
    a_high, a_low = split(a)
    b_high, b_low = split(b)
    return dot(jnp.concatenate([a_high, a_low], 1), jnp.concatenate([b_high, b_high], 0)) + dot(a_high, b_low)


def start_inverse(gram):
    rows = lax.broadcasted_iota(jnp.int32, (CHI, CHI), 0)
    cols = lax.broadcasted_iota(jnp.int32, (CHI, CHI), 1)
    identity = jnp.where(rows == cols, 1.0, 0.0).astype(F32)
    scaling = jnp.sum(gram * identity) + EPS
    return identity, gram * (1.0 / scaling), scaling


def inverse_steps(gram):
    identity, current, scaling = start_inverse(gram)
    factor = 1.5 * identity - 0.5 * current
    inverse = factor
    current = product(factor, current)
    yield None
    for step in range(1, NS_STEPS):
        factor = 1.5 * identity - 0.5 * product(inverse, current)
        yield None
        if step + 1 < NS_STEPS:
            both = product(factor, jnp.concatenate([current, inverse], 1))
            current, inverse = lanes(both, 0), lanes(both, 1)
            yield None
        else:
            inverse = product(factor, inverse)
    yield inverse * lax.rsqrt(jnp.full((1, 1), scaling, F32))


def rescale(value):
    mean = jnp.sum(value * value) * (1.0 / value.size)
    return value * lax.rsqrt(jnp.full((1, 1), mean + EPS, F32))


PAIRS = CHI // 2
PIECES = ((0, 5), (5, 9))


def site_pairs(start, count, site, work):
    zs, ws, zb, wb = work

    def pair(step, carry):
        at = start + step
        z = zb[pl.ds(pl.multiple_of(at * 16, 16), 16), :]
        tail = zs[pl.ds(pl.multiple_of(at * 48, 48), 48), :]
        cols = []
        for h in range(2):
            cols.append(
                jnp.concatenate(
                    [lanes(z, q)[h * 8 : h * 8 + 8] for q in range(D2)] + [tail[h * 24 : h * 24 + 24]], 0
                )
            )
        w = dot(site, jnp.concatenate(cols, 1).astype(BF))
        halves = [lanes(w, h) for h in range(2)]
        wide = [jnp.concatenate([half[e * 8 : e * 8 + 8] for e in range(D2)], 1) for half in halves]
        wb[pl.ds(pl.multiple_of(at * 16, 16), 16), :] = jnp.concatenate(wide, 0).astype(BF)
        ws[pl.ds(pl.multiple_of(at * 32, 32), 32), :] = jnp.concatenate([half[72:88] for half in halves], 0)
        return carry

    lax.fori_loop(0, count, pair, 0, unroll=True)


def site_products(x8, x1, y, site, work, beside=None):
    zs, _, zb, _ = work
    z_last = dot(x1, y)
    for q in range(D2):
        zs[pl.ds(q, CHI, stride=24), :] = lanes(z_last, q)
    if beside is None:
        zb[...] = dot(x8[...], y)
        site_pairs(0, PAIRS, site, work)
        return None
    found = None
    for part in range(4):
        found = next(beside, found)
        zb[part * 256 : part * 256 + 256, :] = dot(x8[part * 256 : part * 256 + 256, :], y)
    for start in range(0, PAIRS, 6):
        found = next(beside, found)
        site_pairs(start, min(6, PAIRS - start), site, work)
    return found


def last_product(v8t, v1t, work, piece):
    ws, wb = work[1], work[3]
    low, high = piece
    w_last = jnp.concatenate([ws[pl.ds(e, CHI, stride=16), :] for e in range(low, high)], 1).astype(BF)
    return dot(v8t, wb[:, low * CHI : high * CHI]) + dot(v1t, w_last)


def columns(piece):
    return slice(piece[0] * CHI, piece[1] * CHI)


def leading(edge, scr):
    for leg in range(8):
        scr[pl.ds(leg, CHI, stride=8), :] = edge[leg].astype(F32)
    return scr[...].astype(BF)


def joined(one, other):
    return (one[...].astype(F32) + other[...].astype(F32)).astype(BF)


def stack_legs(wide):
    return jnp.concatenate([lanes(wide, leg) for leg in range(D2)], 0)


def turned(raw, piece, left, right):
    legs = piece[1] - piece[0]
    stacked = jnp.concatenate([raw[:, leg * CHI : (leg + 1) * CHI] for leg in range(*piece)], 0)
    after = dot(stacked, right).astype(BF)
    return dot(left, jnp.concatenate([after[n * CHI : (n + 1) * CHI] for n in range(legs)], 1))


def factor_of(squares, size):
    return lax.rsqrt(jnp.full((1, 1), squares * (1.0 / size) + EPS, F32))


SQ = (CHI, CHI)
FL = (CHI, WIDE)
PACK = (CHI, WIDE + 2 * CHI)
TALL = (CHI * 8, CHI)
V = pltpu.VMEM
FIRST_SEND = 2 * len(PIECES)
SENDS = 20
SCRATCH = dict(
    ket_scr=V((8, 128), F32),
    sites=V((4, 96, 96), BF),
    s_scr=V((WIDE, CHI), F32),
    rows=V(TALL, F32),
    rows_x=V(TALL, F32),
    last=V(SQ, F32),
    last_x=V(SQ, BF),
    zs=V((CHI * 24, CHI), F32),
    ws=V((CHI * 16, CHI), F32),
    zb=V((CHI * 8, WIDE), F32),
    wb=V((CHI * 8, WIDE), BF),
    left8=V(TALL, BF),
    left_y=V(FL, BF),
    pair8=V(TALL, BF),
    pair1=V(SQ, BF),
    below=V((WIDE, CHI), BF),
    beside=V((WIDE, CHI), BF),
    top8=V(TALL, BF),
    top8t=V((CHI, CHI * 8), BF),
    top1t=V(SQ, BF),
    terms=V((2, CHI, WIDE), BF),
    terms_in=V((2, CHI, WIDE), BF),
    root=V(SQ, BF),
    root_near=V(SQ, BF),
    root_far=V(SQ, BF),
    moved=V(FL, BF),
    moved_in=V(FL, BF),
    near=V(SQ, BF),
    near_in=V(SQ, BF),
    far=V(SQ, BF),
    far_in=V(SQ, BF),
    edge_raw=V(FL, F32),
    right=V(FL, BF),
    right_next=V(FL, BF),
    cut=V(FL, BF),
    cut_west=V(FL, BF),
    root_col=V(SQ, BF),
    root_col_near=V(SQ, BF),
    root_col_far=V(SQ, BF),
    raised=V(FL, BF),
    raised_in=V(FL, BF),
    near_up=V(SQ, BF),
    near_up_in=V(SQ, BF),
    far_up=V(SQ, BF),
    far_up_in=V(SQ, BF),
    ket=V((2, 81), F32),
    masks=V((4, 2, 2, 96, 128), BF),
    edge_left=V((D2, CHI, CHI), BF),
    edge_bottom=V((D2, CHI, CHI), BF),
    corner_bl=V(SQ, BF),
    row_sketch=V((2, WIDE, CHI), BF),
    edge_top=V((D2, CHI, CHI), BF),
    corner_tl=V(SQ, BF),
    corner_tr=V(SQ, BF),
    edge_right=V((D2, CHI, CHI), BF),
    col_sketch=V((2, WIDE, CHI), BF),
    in_sems=pltpu.SemaphoreType.DMA((11,)),
    send_sems=pltpu.SemaphoreType.DMA((SENDS,)),
    recv_sems=pltpu.SemaphoreType.DMA((SENDS,)),
)


INPUTS = (
    "ket",
    "masks",
    "edge_left",
    "edge_bottom",
    "corner_bl",
    "row_sketch",
    "edge_top",
    "corner_tl",
    "corner_tr",
    "edge_right",
    "col_sketch",
)


def move_kernel(*refs):
    sources, (left_out, top_out) = refs[: len(INPUTS)], refs[len(INPUTS) : len(INPUTS) + 2]
    s = dict(zip(SCRATCH, refs[len(INPUTS) + 2 :]))
    loads = {}
    for index, (name, source) in enumerate(zip(INPUTS, sources)):
        loads[name] = pltpu.make_async_copy(source, s[name], s["in_sems"].at[index])
        if index < 9:
            loads[name].start()
    ket, masks, edge_left, edge_bottom, corner_bl, row_sketch, edge_top, corner_tl, corner_tr, edge_right, col_sketch = [
        s[name] for name in INPUTS
    ]
    work = (s["zs"], s["ws"], s["zb"], s["wb"])
    row, col = lax.axis_index("row"), lax.axis_index("col")
    row_count, col_count = lax.axis_size("row"), lax.axis_size("col")

    def device(down, across):
        return {
            "row": lax.rem(row + (row_count + down), row_count),
            "col": lax.rem(col + (col_count + across), col_count),
        }

    barrier = pltpu.get_barrier_semaphore()
    for offset in ((-1, 0), (1, 0), (0, -1), (0, 1), (1, 1), (-1, -1)):
        pl.semaphore_signal(barrier, inc=1, device_id=device(*offset), device_id_type=pl.DeviceIdType.MESH)

    def remote(number, source, target, down, across):
        return pltpu.make_async_remote_copy(
            src_ref=source,
            dst_ref=target,
            send_sem=s["send_sems"].at[number],
            recv_sem=s["recv_sems"].at[number],
            device_id=device(down, across),
            device_id_type=pl.DeviceIdType.MESH,
        )

    sent = []

    def send(source, target, down, across, piece=None):
        source, target = s[source], s[target]
        if piece is not None:
            source, target = source.at[:, columns(piece)], target.at[:, columns(piece)]
        copy = remote(len(sent) + FIRST_SEND, source, target, down, across)
        copy.start()
        sent.append(copy)
        return copy

    def send_term(which, number):
        places = (which, slice(None), columns(PIECES[number]))
        return remote(
            2 * which + number, s["terms"].at[places], s["terms_in"].at[places], 2 * which - 1, 0
        )

    def site(form):
        return s["sites"][form, 0:88, :]

    def transposed_rows(wide_of):
        for leg in range(D2):
            value = wide_of(leg)
            if leg < 8:
                s["rows"][pl.ds(leg, CHI, stride=8), :] = value
        return s["rows"][...].astype(BF).T, value.astype(BF).T

    s["zs"][...] = jnp.zeros_like(s["zs"])
    for name in INPUTS[:2]:
        loads[name].wait()
    for name in INPUTS[9:]:
        loads[name].start()
    for form in (LOWER, UPPER):
        s["sites"][form] = site_form(ket, masks, form, s["ket_scr"])
    for name in INPUTS[2:8]:
        loads[name].wait()

    half = row_count // 2
    far = (lax.rem(row, half) + 1) // half
    patient = (lax.rem(row + 1, half) + 1) // half

    def term(step, carry):
        which = lax.rem(step + far, 2)

        def operands(edge, corner, product_of):
            for leg in range(8):
                s["rows_x"][pl.ds(leg, CHI, stride=8), :] = edge[leg].astype(F32)
            s["last_x"][...] = edge[8]
            for leg in range(D2):
                value = product_of(corner, edge_left[leg])
                if leg < 8:
                    s["rows"][pl.ds(leg, CHI, stride=8), :] = value
            s["last"][...] = value

        @pl.when(which == LOWER)
        def _():
            operands(edge_bottom, corner_bl[...].T, dot_nt)

        @pl.when(which == UPPER)
        def _():
            operands(edge_top, corner_tl[...], dot)

        site_products(
            s["rows_x"][...].astype(BF),
            s["last_x"][...],
            flat_sketch(row_sketch[1 - which], s["s_scr"]),
            s["sites"][which][0:88],
            work,
        )
        v8t = s["rows"][...].astype(BF).T
        v1t = s["last"][...].astype(BF).T
        for number, piece in enumerate(PIECES):
            s["terms"][which, :, columns(piece)] = last_product(v8t, v1t, work, piece).astype(BF)
            if number == 0:

                @pl.when(step == 0)
                def _():
                    pl.semaphore_wait(barrier, 6)

            send_term(which, number).start()
        return carry

    lax.fori_loop(0, 2, term, 0)
    lower_copies = [send_term(LOWER, number) for number in range(2)]
    upper_copies = [send_term(UPPER, number) for number in range(2)]
    for name in INPUTS[8:]:
        loads[name].wait()
    s["left8"][...] = leading(edge_left, s["rows"])
    for leg in range(D2):
        s["below"][leg * CHI : (leg + 1) * CHI, :] = dot(corner_bl[...], edge_bottom[leg]).astype(BF)
    corner_t = corner_tl[...].T
    for leg in range(D2):
        value = dot(corner_t, edge_top[leg])
        if leg < 8:
            s["rows_x"][pl.ds(leg, CHI, stride=8), :] = value
    s["pair8"][...] = s["rows_x"][...].astype(BF)
    s["pair1"][...] = value.astype(BF)
    s["sites"][AHEAD] = site_form(ket, masks, AHEAD, s["ket_scr"])

    for copy in lower_copies:
        copy.wait_recv()
    cut = joined(s["terms"].at[UPPER], s["terms_in"].at[LOWER])
    stacked = stack_legs(cut)
    second = dot_tn(stacked, jnp.concatenate([stacked, s["below"][...]], 1))
    root = site_products(
        s["left8"], edge_left[8], cut, site(AHEAD), work, inverse_steps(lanes(second, 0))
    )
    s["root"][...] = root.astype(BF)
    near_copy = send("root", "root_near", 0, 1)
    far_copy = send("root", "root_far", 1, 1)
    s["far"][...] = lanes(second, 1).astype(BF)
    for copy, piece in zip(upper_copies, PIECES):
        copy.wait_recv()
        for leg in range(*piece):
            at = slice(leg * CHI, (leg + 1) * CHI)
            value = joined(s["terms_in"].at[UPPER, :, at], s["terms"].at[LOWER, :, at])
            if leg < 8:
                s["rows"][pl.ds(leg, CHI, stride=8), :] = value.astype(F32)
    v8 = s["rows"][...].astype(BF)
    v8t, v1t = v8.T, value.T
    moved_copies = []
    for piece in PIECES:
        s["moved"][:, columns(piece)] = last_product(v8t, v1t, work, piece).astype(BF)
        moved_copies.append(
            remote(
                len(sent) + FIRST_SEND,
                s["moved"].at[:, columns(piece)],
                s["moved_in"].at[:, columns(piece)],
                0,
                1,
            )
        )
        sent.append(moved_copies[-1])
        if len(moved_copies) == 1:
            moved_copies[0].start()
        else:

            @pl.when(patient == 0)
            def _():
                moved_copies[-1].start()

        if len(moved_copies) == 1:
            s["near"][...] = (dot(v8t, s["pair8"][...]) + dot(v1t, s["pair1"][...])).astype(BF)
            moved_near_copy = send("near", "near_in", 0, 1)

    s["sites"][RIGHT] = site_form(ket, masks, RIGHT, s["ket_scr"])
    corner_t = corner_tr[...].T
    right8t, right1t = transposed_rows(lambda leg: dot_nt(corner_t, edge_top[leg]))
    site_products(
        leading(edge_right, s["rows_x"]),
        edge_right[8],
        flat_sketch(col_sketch[1], s["s_scr"]),
        site(RIGHT),
        work,
    )
    @pl.when(patient == 1)
    def _():
        moved_copies[-1].start()

    s["right"][...] = last_product(right8t, right1t, work, (0, D2)).astype(BF)
    right_copy = send("right", "right_next", 0, -1)
    for leg in range(D2):
        s["beside"][leg * CHI : (leg + 1) * CHI, :] = dot(corner_tr[...], edge_right[leg]).astype(BF)
    s["top8"][...] = leading(edge_top, s["rows"])
    s["top8t"][...] = s["top8"][...].T
    s["top1t"][...] = edge_top[8].T
    s["left_y"][...] = flat_sketch(col_sketch[0], s["s_scr"])

    for copy in (moved_near_copy, near_copy, far_copy):
        copy.wait_recv()
    above_root = s["root_far"][...]
    own_root = s["root_near"][...]
    corner_raw = dot(above_root, s["near_in"][...])
    corner_scale = factor_of(jnp.sum(corner_raw * corner_raw), CHI * CHI)
    corner_mid = corner_raw.T.astype(BF)
    for copy, piece in zip(moved_copies, PIECES):
        copy.wait_recv()
        if piece == PIECES[-1]:
            moved_far_copy = send("far", "far_in", 0, 1)
        edge_raw = turned(s["moved_in"], piece, above_root, own_root)
        s["edge_raw"][:, columns(piece)] = edge_raw
        side = dot(corner_mid, edge_raw.astype(BF))
        for leg in range(*piece):
            value = lanes(side, leg - piece[0])
            if leg < 8:
                s["rows"][pl.ds(leg, CHI, stride=8), :] = value
    s["pair8"][...] = s["rows"][...].astype(BF)
    s["pair1"][...] = value.astype(BF)
    site_products(s["pair8"], s["pair1"][...], s["left_y"][...], site(AHEAD), work)
    edge_raw = s["edge_raw"][...]
    edge_scale = factor_of(jnp.sum(edge_raw * edge_raw), CHI * WIDE)
    side_scale = edge_scale * corner_scale
    cut_copies = []
    for piece in PIECES:
        left_term = last_product(s["top8t"][...], s["top1t"][...], work, piece) * side_scale
        if not cut_copies:
            right_copy.wait_recv()
        s["cut"][:, columns(piece)] = (left_term + s["right_next"][:, columns(piece)].astype(F32)).astype(BF)
        cut_copies.append(
            remote(
                len(sent) + FIRST_SEND,
                s["cut"].at[:, columns(piece)],
                s["cut_west"].at[:, columns(piece)],
                0,
                1,
            )
        )
        sent.append(cut_copies[-1])

        @pl.when(patient == 0)
        def _():
            cut_copies[-1].start()


    cut = s["cut"][...]
    stacked = stack_legs(cut)
    second = dot_tn(stacked, jnp.concatenate([stacked, s["beside"][...]], 1))
    root = site_products(
        s["top8"], edge_top[8], cut, site(UPPER), work, inverse_steps(lanes(second, 0))
    )
    @pl.when(patient == 1)
    def _():
        for copy in cut_copies:
            copy.start()

    s["root_col"][...] = root.astype(BF)
    near_copy = send("root_col", "root_col_near", 1, 0)
    far_copy = send("root_col", "root_col_far", 1, 1)
    s["far_up"][...] = lanes(second, 1).astype(BF)
    raised_far_copy = send("far_up", "far_up_in", 1, 0)
    left_out[:, :WIDE] = (s["edge_raw"][...] * edge_scale).astype(BF)
    moved_far_copy.wait_recv()
    left_out[:, WIDE + CHI :] = rescale(dot(s["root_near"][...], s["far_in"][...])).astype(BF)
    left_out[:, WIDE : WIDE + CHI] = corner_mid
    for copy, piece in zip(cut_copies, PIECES):
        copy.wait_recv()
        for leg in range(*piece):
            value = s["cut_west"][:, leg * CHI : (leg + 1) * CHI]
            if leg < 8:
                s["rows"][pl.ds(leg, CHI, stride=8), :] = value.astype(F32)
    v8 = s["rows"][...].astype(BF)
    v8t, v1t = v8.T, value.T
    raised_copies = []
    for piece in PIECES:
        s["raised"][:, columns(piece)] = last_product(v8t, v1t, work, piece).astype(BF)
        raised_copies.append(send("raised", "raised_in", 1, 0, piece))
        if len(raised_copies) == 1:
            first = (dot(v8t, s["pair8"][...]) + dot(v1t, s["pair1"][...])) * side_scale
            s["near_up"][...] = first.astype(BF)
            raised_near_copy = send("near_up", "near_up_in", 1, 0)

    for copy in (near_copy, far_copy, raised_far_copy):
        copy.wait_recv()
    west_root = s["root_col_far"][...]
    own_root = s["root_col_near"][...]
    top_out[:, WIDE + CHI :] = rescale(dot(own_root, s["far_up_in"][...])).astype(BF)
    raised_near_copy.wait_recv()
    top_out[:, WIDE : WIDE + CHI] = rescale(dot(west_root, s["near_up_in"][...])).astype(BF)
    parts = []
    for copy, piece in zip(raised_copies, PIECES):
        copy.wait_recv()
        parts.append(turned(s["raised_in"], piece, west_root, own_root))
    top_scale = factor_of(sum(jnp.sum(part * part) for part in parts), CHI * WIDE)
    for part, piece in zip(parts, PIECES):
        top_out[:, columns(piece)] = (part * top_scale).astype(BF)
    for copy in lower_copies + upper_copies + sent:
        copy.wait_send()


def result_kernel(left, top, edge_left, corner_bl, edge_top, corner_tl, corner_tr, sems):
    blocks = [(left, leg, edge_left.at[leg]) for leg in range(D2)]
    blocks += [(top, leg, edge_top.at[leg]) for leg in range(D2)]
    blocks += [(left, 10, corner_bl), (top, 9, corner_tl), (top, 10, corner_tr)]
    copies = [
        pltpu.make_async_copy(pack.at[:, n * CHI : (n + 1) * CHI], target, sems.at[index])
        for index, (pack, n, target) in enumerate(blocks)
    ]
    for copy in copies:
        copy.start()
    for copy in copies:
        copy.wait()


def local(*arrays):
    ket, corner_tl, corner_tr, corner_bl, *edges, row_sketch, col_sketch = [a.reshape(a.shape[2:]) for a in arrays]
    edges = [edge.transpose(1, 0, 2) for edge in edges]
    vmem = pl.BlockSpec(memory_space=pltpu.VMEM)
    hbm = pl.BlockSpec(memory_space=pltpu.HBM)
    operands = tuple(pltpu.with_memory_space_constraint(x, pltpu.HBM) for x in (ket, jnp.asarray(site_masks(), BF), edges[0], edges[3], corner_bl, row_sketch, edges[1], corner_tl, corner_tr, edges[2], col_sketch))
    packs = pl.pallas_call(
        move_kernel,
        out_shape=[jax.ShapeDtypeStruct(PACK, BF)] * 2,
        in_specs=[hbm] * len(operands),
        out_specs=[vmem] * 2,
        scratch_shapes=list(SCRATCH.values()),
        compiler_params=pltpu.CompilerParams(
            vmem_limit_bytes=44 << 20, collective_id=0, has_side_effects=True
        ),
        name="moves",
    )(*operands)
    edge = jax.ShapeDtypeStruct((D2, CHI, CHI), BF)
    square = jax.ShapeDtypeStruct((CHI, CHI), BF)
    left, corner_bl, top, corner_tl, corner_tr = pl.pallas_call(
        result_kernel,
        out_shape=[edge, square, edge, square, square],
        in_specs=[vmem] * 2,
        out_specs=[hbm] * 5,
        scratch_shapes=[pltpu.SemaphoreType.DMA((2 * D2 + 3,))],
        compiler_params=pltpu.CompilerParams(vmem_limit_bytes=4 << 20),
        name="results",
    )(*packs)
    results = (left.transpose(1, 0, 2), corner_bl, top.transpose(1, 0, 2), corner_tl, corner_tr)
    return tuple(value[None, None] for value in results)


def solution(mesh):
    four = P("row", "col", None, None)
    five = P("row", "col", None, None, None)
    return jax.shard_map(
        local,
        mesh=mesh,
        in_specs=(four, four, four, four, five, five, five, five, five, five),
        out_specs=(five, four, five, four, four),
        check_vma=False,
    )
```
